32 devices in a mesh: dp: 8 (over z, x), tensor: 4 (over y, core).
Axes of the slice: x: 2, y: 2, z: 4, core: 2. Of those that a mesh axis runs over, the one named last changes fastest.
Arguments:
- tokens: bfloat16 [16384, 768], P('dp'), may hold values from -6 to 6
- seq_lens: int32 [16], P('dp'), may hold values from 512 to 1024, as said below
- block_sizes: int32 [16], P('dp'), may hold values from 128 to 512
- w_query: bfloat16 [768, 768], P('dp', 'tensor'), may hold values from -0.3125 to 0.3125
- b_query: bfloat16 [768], P('tensor'), may hold values from -3 to 3
- w_key: bfloat16 [768, 768], P('dp', 'tensor'), may hold values from -0.21875 to 0.21875
- w_value: bfloat16 [768, 768], P('dp', 'tensor'), may hold values from -0.21875 to 0.21875
- b_value: bfloat16 [768], P('tensor'), may hold values from -3 to 3
- w_out: bfloat16 [768, 768], P('tensor', 'dp'), may hold values from -1.25 to 1.25
- b_out: bfloat16 [768], P('dp'), may hold values from -2 to 2
- gain_one: bfloat16 [768], P('dp'), may hold values from 0.25 to 1.75
- shift_one: bfloat16 [768], P('dp'), may hold values from -2 to 2
- w_up: bfloat16 [768, 3072], P('dp', 'tensor'), may hold values from -0.21875 to 0.21875
- b_up: bfloat16 [3072], P('tensor'), may hold values from -3 to 3
- w_down: bfloat16 [3072, 768], P('tensor', 'dp'), may hold values from -0.109375 to 0.109375
- b_down: bfloat16 [768], P('dp'), may hold values from -2 to 2
- gain_two: bfloat16 [768], P('dp'), may hold values from 0.25 to 1.75
- shift_two: bfloat16 [768], P('dp'), may hold values from -2 to 2
- cotangent: bfloat16 [16384, 768], P('dp'), may hold values from -6 to 6
Outputs:
- output: bfloat16 [16384, 768], P('dp')
- input_grad: float32 [16384, 768], P('dp', 'tensor')
- grad_w_query: float32 [768, 768], P('dp', 'tensor')
- grad_b_query: float32 [768], P('tensor')
- grad_w_key: float32 [768, 768], P('dp', 'tensor')
- grad_w_value: float32 [768, 768], P('dp', 'tensor')
- grad_b_value: float32 [768], P('tensor')
- grad_w_out: float32 [768, 768], P('tensor', 'dp')
- grad_b_out: float32 [768], P('dp')
- grad_gain_one: float32 [768], P('dp')
- grad_shift_one: float32 [768], P('dp')
- grad_w_up: float32 [768, 3072], P('dp', 'tensor')
- grad_b_up: float32 [3072], P('tensor')
- grad_w_down: float32 [3072, 768], P('tensor', 'dp')
- grad_b_down: float32 [768], P('dp')
- grad_gain_two: float32 [768], P('dp')
- grad_shift_two: float32 [768], P('dp')
The draws below stay inside these ranges and needn't reach their ends.
Inputs may be any that keep to these rules, and one draw needn't show every extreme that they name: seq_lens[s] counts the key positions of sequence s that any query may see; at least one sequence is whole.
All inputs are finite; a program needn't handle non-finite values.
Results may differ from the reference program's by a relative error of at most 0.015.
The reference program's roundings to bfloat16 on the way count: a program that leaves them out, or rounds other values in their place, can miss the bound.
Values may be sent and summed in bfloat16 or wider, within the bound.
A program may use at most 192 MiB of HBM per device.

```python
import jax
import jax.numpy as jnp
from jax import lax

D = 768
HEADS = 12
HEAD = 64
FF = 3072
SEQ = 1024
SEQS = 16
TOKENS = 16384


def draw_seq_lens(key, part):
    drawn = jax.random.randint(key, (SEQS,), SEQ // 2, SEQ + 1, dtype=jnp.int32)
    return drawn.at[0].set(SEQ)


def plant(array, key, low, top_value):
    longest = array.shape.index(max(array.shape))
    spots = []
    for shift in (0, 1):
        where = [jax.random.randint(jax.random.fold_in(key, axis), (), 0, length) for axis, length in enumerate(array.shape)]
        where[longest] = (where[longest] + shift) % array.shape[longest]
        spots.append(tuple(where))
    return array.at[spots[0]].set(low).at[spots[1]].set(top_value)


def strengthened(array, key, source, target, blocks, factor):
    owner, partner = [(jnp.arange(array.shape[position]) // (array.shape[position] // blocks)).reshape([-1 if axis == position else 1 for axis in range(array.ndim)]) for position in (source, target)]
    chosen = jax.random.permutation(key, blocks)[partner]
    strong = (owner == chosen) | (owner == (partner + blocks // 2) % blocks)
    return jnp.where(strong, factor * array, array)


def shard_levels(own_key, dims, split, low, top_value):
    gain = 1.0
    for dim, parts in split:
        steps = jax.random.uniform(jax.random.fold_in(jax.random.fold_in(own_key, 6), dim), (parts,), jnp.float32, low / len(split), top_value / len(split))
        gain = gain * jnp.repeat(jnp.exp(steps), dims[dim] // parts).reshape((-1,) + (1,) * (len(dims) - 1 - dim))
    return gain


def bell_draw(own_key, shape, scale, bound, cuts=(), held_as=jnp.bfloat16):
    result = scale * jax.random.normal(own_key, shape, jnp.float32)
    if cuts:
        result = result * shard_levels(own_key, shape, cuts, -0.22, 0.18)
    return jnp.clip(result, -bound, bound).astype(held_as)


def noise_with(key, dims, deviation, most, split, heavy, held_as=jnp.bfloat16):
    array = deviation * jax.random.normal(key, dims, jnp.float32)
    if split:
        array = array * shard_levels(key, dims, split, -0.22, 0.18)
    return jnp.clip(strengthened(array, jax.random.fold_in(key, 3), *heavy), -most, most).astype(held_as)


def setup_inputs(seed: int = 0) -> dict:
    seeds = jax.random.split(jax.random.key(seed), 20)
    tokens = bell_draw(seeds[0], (TOKENS, D), 1.0, 6.0, ((0, 8),))
    seq_lens = draw_seq_lens(jax.random.fold_in(seeds[19], 71), 0)
    block_sizes = plant(jax.random.randint(seeds[2], (SEQS,), SEQ // 8, SEQ // 2 + 1), jax.random.fold_in(seeds[2], 1), SEQ // 8, (SEQ // 2 + 1) - 1).astype(jnp.int32)
    w_query = bell_draw(seeds[3], (D, D), (D // 2) ** -0.5, 0.3125, ((0, 8), (1, 4)))
    b_query = bell_draw(seeds[4], (D,), 0.5, 3.0, ((0, 4),))
    w_key = bell_draw(seeds[5], (D, D), D ** -0.5, 0.21875, ((0, 8), (1, 4)))
    w_value = bell_draw(seeds[6], (D, D), D ** -0.5, 0.21875, ((0, 8), (1, 4)))
    b_value = bell_draw(seeds[7], (D,), 0.5, 3.0, ((0, 4),))
    w_out = bell_draw(seeds[8], (D, D), (D // 32) ** -0.5, 1.25, ((0, 4), (1, 8)))
    b_out = bell_draw(seeds[9], (D,), 0.3, 2.0, ((0, 8),))
    gain_one = jnp.clip(1.0 + 0.15 * jax.random.normal(seeds[10], (D,), jnp.float32), 0.25, 1.75).astype(jnp.bfloat16)
    shift_one = bell_draw(seeds[11], (D,), 0.3, 2.0, ((0, 8),))
    w_up = bell_draw(seeds[12], (D, FF), D ** -0.5, 0.21875, ((0, 8), (1, 4)))
    b_up = bell_draw(seeds[13], (FF,), 0.5, 3.0, ((0, 4),))
    w_down = bell_draw(seeds[14], (FF, D), FF ** -0.5, 0.109375, ((0, 4), (1, 8)))
    b_down = bell_draw(seeds[15], (D,), 0.3, 2.0, ((0, 8),))
    gain_two = jnp.clip(1.0 + 0.15 * jax.random.normal(seeds[16], (D,), jnp.float32), 0.25, 1.75).astype(jnp.bfloat16)
    shift_two = bell_draw(seeds[17], (D,), 0.3, 2.0, ((0, 8),))
    cotangent = noise_with(seeds[18], (TOKENS, D), 1.0, 6.0, ((0, 8),), (0, 1, 8, 2.0))
    return dict(tokens=tokens, seq_lens=seq_lens, block_sizes=block_sizes, w_query=w_query, b_query=b_query, w_key=w_key, w_value=w_value, b_value=b_value, w_out=w_out, b_out=b_out, gain_one=gain_one, shift_one=shift_one, w_up=w_up, b_up=b_up, w_down=w_down, b_down=b_down, gain_two=gain_two, shift_two=shift_two, cotangent=cotangent)


@jax.custom_vjp
def low(v):
    return lax.optimization_barrier(v.astype(jnp.bfloat16)).astype(jnp.float32)

@jax.custom_vjp
def low_back(v):
    return v

def low_keep(v):
    return (low(v), None)

def low_pass(kept, grad):
    return (grad,)

def back_keep(v):
    return (v, None)

def back_low(kept, grad):
    return (low(grad),)
low.defvjp(low_keep, low_pass)
low_back.defvjp(back_keep, back_low)
norm_epsilon = 1e-12
highest = lax.Precision.HIGHEST

def rounded_both(tensor_value):
    return low(low_back(tensor_value))

def product(first_operand, second_operand):
    return jnp.dot(first_operand, second_operand, precision=highest)

def layer_norm(row_values, gain_row, offset_row):
    row_mean = lax.optimization_barrier(jnp.mean(row_values, axis=-1, keepdims=True))
    centred = row_values - row_mean
    variance = lax.optimization_barrier(jnp.mean(centred * centred, axis=-1, keepdims=True))
    return centred * lax.rsqrt(variance + norm_epsilon) * gain_row + offset_row

def gelu_exact(expanded):
    return 0.5 * expanded * (1.0 + jax.scipy.special.erf(expanded * 0.7071067811865476))

def layer(params, inputs, seq_length, block_size):
    w_query, b_query, w_key, w_value, b_value, w_out, b_out, gain_one, shift_one, w_up, b_up, w_down, b_down, gain_two, shift_two = params
    row_count = inputs.shape[0]
    query_rows = low((low_back(product(inputs, w_query)) + b_query) * 0.125)
    key_rows = low(low_back(product(inputs, w_key)))
    value_rows = low(low_back(product(inputs, w_value)) + b_value)
    query_rows = query_rows.reshape(row_count, HEADS, HEAD)
    key_rows = key_rows.reshape(row_count, HEADS, HEAD)
    value_rows = value_rows.reshape(row_count, HEADS, HEAD)
    scores = low_back(jnp.einsum('qhd,khd->hqk', query_rows, key_rows, precision=highest))
    positions = jnp.arange(row_count, dtype=jnp.int32)
    allowed = (positions[None, :] // block_size <= positions[:, None] // block_size) & (positions[None, :] < seq_length)
    scores = jnp.where(allowed[None], scores, -1000000000.0)
    top_score = lax.optimization_barrier(jnp.max(scores, axis=-1, keepdims=True))
    exp_scores = jnp.exp(scores - top_score)
    probabilities = low(exp_scores / lax.optimization_barrier(jnp.sum(exp_scores, axis=-1, keepdims=True)))
    context = jnp.einsum('hqk,khd->qhd', probabilities, value_rows, precision=highest).reshape(row_count, D)
    context = rounded_both(context)
    attended = low_back(product(context, w_out)) + b_out
    normed = low(layer_norm(inputs + attended, gain_one, shift_one))
    expanded = low_back(product(normed, w_up)) + b_up
    hidden = low(gelu_exact(expanded))
    lowered = low_back(product(hidden, w_down)) + b_down
    return layer_norm(normed + lowered, gain_two, shift_two)

def reference(tokens, seq_lens, block_sizes, w_query, b_query, w_key, w_value, b_value, w_out, b_out, gain_one, shift_one, w_up, b_up, w_down, b_down, gain_two, shift_two, cotangent):
    params = tuple((weight_array.astype(jnp.float32) for weight_array in (w_query, b_query, w_key, w_value, b_value, w_out, b_out, gain_one, shift_one, w_up, b_up, w_down, b_down, gain_two, shift_two)))
    inputs = tokens.astype(jnp.float32).reshape(SEQS, SEQ, D)
    upstream = cotangent.astype(jnp.float32).reshape(SEQS, SEQ, D)

    def one_sequence(totals, seq_item):
        seq_input, seq_upstream, seq_length, block_size = seq_item

        def forward(param_list, layer_input):
            return layer(param_list, layer_input, seq_length, block_size)
        layer_output, pullback = jax.vjp(forward, params, seq_input)
        grads, seq_grad = pullback(seq_upstream)
        totals = jax.tree.map(lambda running, addend: running + addend, totals, grads)
        return (totals, (layer_output, seq_grad))
    zeros = jax.tree.map(jnp.zeros_like, params)
    totals, (outputs, input_grads) = lax.scan(one_sequence, zeros, (inputs, upstream, seq_lens, block_sizes))
    return (outputs.reshape(TOKENS, D).astype(jnp.bfloat16), input_grads.reshape(TOKENS, D), totals[0], totals[1], totals[2], totals[3], totals[4], totals[5], totals[6], totals[7], totals[8], totals[9], totals[10], totals[11], totals[12], totals[13], totals[14])
```

```python
import functools

import jax
import jax.numpy as jnp
from jax import lax
from jax.experimental import pallas as pl
from jax.experimental.pallas import tpu as pltpu
from jax.sharding import PartitionSpec as P

HEAD = 64
MESH = pl.DeviceIdType.MESH

norm_epsilon = 1e-12
inv_root_two = 0.7071067811865476
inv_root_tau = 0.3989422804014327
masked_score = -1000000000.0


def matmul(first_operand, second_operand):
    return jnp.dot(first_operand, second_operand, preferred_element_type=jnp.float32)


def contract_rows(first_operand, second_operand):
    return lax.dot_general(
        first_operand, second_operand, (((0,), (0,)), ((), ())), preferred_element_type=jnp.float32
    )


def contract_cols(first_operand, second_operand):
    return lax.dot_general(
        first_operand, second_operand, (((1,), (1,)), ((), ())), preferred_element_type=jnp.float32
    )


def norm_forward(row_values, gain_row, offset_row):
    row_mean = jnp.mean(row_values, axis=-1, keepdims=True)
    centred = row_values - row_mean
    variance = jnp.mean(centred * centred, axis=-1, keepdims=True)
    inv_scale = lax.rsqrt(variance + norm_epsilon)
    normal_rows = centred * inv_scale
    return (normal_rows * gain_row + offset_row, normal_rows, inv_scale)


def norm_backward(upstream, normal_rows, inv_scale, gain_row):
    scaled = upstream * gain_row
    row_grad = inv_scale * (
        scaled
        - jnp.mean(scaled, axis=-1, keepdims=True)
        - normal_rows * jnp.mean(scaled * normal_rows, axis=-1, keepdims=True)
    )
    return (row_grad, jnp.sum(upstream * normal_rows, axis=0), jnp.sum(upstream, axis=0))


def allowed_mask(first_row, row_total, key_total, seq_length, block_size):
    row_pos = first_row + lax.broadcasted_iota(jnp.int32, (row_total, key_total), 0)
    key_pos = lax.broadcasted_iota(jnp.int32, (row_total, key_total), 1)
    return (key_pos // block_size <= row_pos // block_size) & (key_pos < seq_length)


def attend(query_rows, key_rows, value_rows, seq_length, block_size):
    row_total, local_heads, head_size = query_rows.shape
    block_rows = min(512, row_total)
    block_count = row_total // block_rows
    query_blocks = query_rows.reshape(block_count, block_rows, local_heads, head_size)

    def one_block(block_pair):
        block_index, query_block = block_pair
        scores = jnp.einsum(
            "qhd,khd->hqk", query_block, key_rows, preferred_element_type=jnp.float32
        )
        allowed = allowed_mask(
            block_index * block_rows, block_rows, row_total, seq_length, block_size
        )
        scores = jnp.where(allowed[None], scores, masked_score)
        top_score = jnp.max(scores, axis=-1, keepdims=True)
        exp_scores = jnp.exp(scores - top_score)
        exp_total = jnp.sum(exp_scores, axis=-1, keepdims=True)
        probabilities = (exp_scores / exp_total).astype(jnp.bfloat16)
        context = jnp.einsum(
            "hqk,khd->qhd", probabilities, value_rows, preferred_element_type=jnp.float32
        )
        return (context.astype(jnp.bfloat16), top_score[..., 0] + jnp.log(exp_total[..., 0]))

    contexts, log_sums = lax.map(
        one_block, (jnp.arange(block_count, dtype=jnp.int32), query_blocks)
    )
    return (contexts.reshape(row_total, local_heads * head_size), log_sums)


def attend_back(query_rows, key_rows, value_rows, context_grad, log_sums, seq_length, block_size):
    row_total, local_heads, head_size = query_rows.shape
    block_rows = min(512, row_total)
    block_count = row_total // block_rows
    query_blocks = query_rows.reshape(block_count, block_rows, local_heads, head_size)
    grad_blocks = context_grad.reshape(block_count, block_rows, local_heads, head_size)

    def one_block(running, block_pack):
        key_grad, value_grad = running
        block_index, query_block, grad_block, log_block = block_pack
        scores = jnp.einsum(
            "qhd,khd->hqk", query_block, key_rows, preferred_element_type=jnp.float32
        )
        allowed = allowed_mask(
            block_index * block_rows, block_rows, row_total, seq_length, block_size
        )
        probabilities = jnp.where(allowed[None], jnp.exp(scores - log_block[..., None]), 0.0)
        prob_grad = jnp.einsum(
            "qhd,khd->hqk", grad_block, value_rows, preferred_element_type=jnp.float32
        )
        row_dot = jnp.sum(prob_grad * probabilities, axis=-1, keepdims=True)
        score_grad = (probabilities * (prob_grad - row_dot)).astype(jnp.bfloat16)
        query_grad = jnp.einsum(
            "hqk,khd->qhd", score_grad, key_rows, preferred_element_type=jnp.float32
        )
        key_grad = key_grad + jnp.einsum(
            "hqk,qhd->khd", score_grad, query_block, preferred_element_type=jnp.float32
        )
        value_grad = value_grad + jnp.einsum(
            "hqk,qhd->khd",
            probabilities.astype(jnp.bfloat16),
            grad_block,
            preferred_element_type=jnp.float32,
        )
        return ((key_grad, value_grad), query_grad)

    empty = jnp.zeros((row_total, local_heads, head_size), jnp.float32)
    (key_grad, value_grad), query_grads = lax.scan(
        one_block,
        (empty, empty),
        (jnp.arange(block_count, dtype=jnp.int32), query_blocks, grad_blocks, log_sums),
    )
    width = local_heads * head_size
    return (
        query_grads.reshape(row_total, width),
        key_grad.reshape(row_total, width),
        value_grad.reshape(row_total, width),
    )


def on_device_plain(
    tokens,
    seq_lens,
    block_sizes,
    w_query,
    b_query,
    w_key,
    w_value,
    b_value,
    w_out,
    b_out,
    gain_one,
    shift_one,
    w_up,
    b_up,
    w_down,
    b_down,
    gain_two,
    shift_two,
    cotangent,
):
    micro_total = seq_lens.shape[0]
    seq_rows = tokens.shape[0] // micro_total
    head_cols = w_query.shape[1]
    local_heads = head_cols // HEAD
    model_width = tokens.shape[1]
    own_cols = model_width // lax.axis_size("tensor")
    column_start = lax.axis_index("tensor") * own_cols
    query_bias = b_query.astype(jnp.float32)
    value_bias = b_value.astype(jnp.float32)
    up_bias = b_up.astype(jnp.float32)
    owned = (
        w_query,
        w_key,
        w_value,
        w_out,
        w_up,
        w_down,
        b_out,
        gain_one,
        shift_one,
        b_down,
        gain_two,
        shift_two,
    )

    def shaped(flat_rows):
        return flat_rows.reshape(seq_rows, local_heads, HEAD)

    layer_outputs = []
    input_grads = []
    totals = None
    for micro_index in range(micro_total):
        rows_in = tokens[micro_index * seq_rows : (micro_index + 1) * seq_rows]
        upstream = cotangent[micro_index * seq_rows : (micro_index + 1) * seq_rows].astype(
            jnp.float32
        )
        seq_length = seq_lens[micro_index]
        block_size = block_sizes[micro_index]
        forward_set = (
            lax.all_gather(owned[0], "dp", axis=0, tiled=True),
            lax.all_gather(owned[1], "dp", axis=0, tiled=True),
            lax.all_gather(owned[2], "dp", axis=0, tiled=True),
            lax.all_gather(owned[3], "dp", axis=1, tiled=True),
            lax.all_gather(owned[4], "dp", axis=0, tiled=True),
            lax.all_gather(owned[5], "dp", axis=1, tiled=True),
            lax.all_gather(owned[6], "dp", axis=0, tiled=True),
            lax.all_gather(owned[7], "dp", axis=0, tiled=True),
            lax.all_gather(owned[8], "dp", axis=0, tiled=True),
            lax.all_gather(owned[9], "dp", axis=0, tiled=True),
            lax.all_gather(owned[10], "dp", axis=0, tiled=True),
            lax.all_gather(owned[11], "dp", axis=0, tiled=True),
        )
        (
            full_query,
            full_key,
            full_value,
            full_out,
            full_up,
            full_down,
            full_out_bias,
            full_gain_one,
            full_shift_one,
            full_down_bias,
            full_gain_two,
            full_shift_two,
        ) = forward_set
        out_bias = full_out_bias.astype(jnp.float32)
        down_bias = full_down_bias.astype(jnp.float32)
        first_gain = full_gain_one.astype(jnp.float32)
        first_shift = full_shift_one.astype(jnp.float32)
        second_gain = full_gain_two.astype(jnp.float32)
        second_shift = full_shift_two.astype(jnp.float32)
        query_rows = ((matmul(rows_in, full_query) + query_bias) * 0.125).astype(jnp.bfloat16)
        key_rows = matmul(rows_in, full_key).astype(jnp.bfloat16)
        value_rows = (matmul(rows_in, full_value) + value_bias).astype(jnp.bfloat16)
        context, log_sums = attend(
            shaped(query_rows), shaped(key_rows), shaped(value_rows), seq_length, block_size
        )
        attended = lax.psum(matmul(context, full_out), "tensor") + out_bias
        first_norm, first_hat, first_scale = norm_forward(
            rows_in.astype(jnp.float32) + attended, first_gain, first_shift
        )
        normed = first_norm.astype(jnp.bfloat16)
        expanded = matmul(normed, full_up) + up_bias
        normal_cdf = 0.5 * (1.0 + lax.erf(expanded * inv_root_two))
        hidden = (expanded * normal_cdf).astype(jnp.bfloat16)
        lowered = lax.psum(matmul(hidden, full_down), "tensor") + down_bias
        second_norm, second_hat, second_scale = norm_forward(
            normed.astype(jnp.float32) + lowered, second_gain, second_shift
        )
        layer_outputs.append(second_norm.astype(jnp.bfloat16))
        second_grad, grad_gain_two, grad_shift_two = norm_backward(
            upstream, second_hat, second_scale, second_gain
        )
        down_bias_grad = jnp.sum(second_grad, axis=0)
        second_low = second_grad.astype(jnp.bfloat16)
        down_grad = contract_rows(hidden, second_low)
        hidden_grad = contract_cols(second_low, full_down)
        expanded_grad = hidden_grad * (
            normal_cdf + expanded * jnp.exp(-0.5 * expanded * expanded) * inv_root_tau
        )
        up_bias_grad = jnp.sum(expanded_grad, axis=0)
        expanded_low = expanded_grad.astype(jnp.bfloat16)
        up_grad = contract_rows(normed, expanded_low)
        normed_grad = lax.psum(contract_cols(expanded_low, full_up), "tensor") + second_grad
        first_grad, grad_gain_one, grad_shift_one = norm_backward(
            normed_grad, first_hat, first_scale, first_gain
        )
        out_bias_grad = jnp.sum(first_grad, axis=0)
        first_low = first_grad.astype(jnp.bfloat16)
        out_grad = contract_rows(context, first_low)
        context_grad = contract_cols(first_low, full_out).astype(jnp.bfloat16)
        query_grad, key_grad, value_grad = attend_back(
            shaped(query_rows),
            shaped(key_rows),
            shaped(value_rows),
            shaped(context_grad),
            log_sums,
            seq_length,
            block_size,
        )
        query_grad = query_grad * 0.125
        query_bias_grad = jnp.sum(query_grad, axis=0)
        value_bias_grad = jnp.sum(value_grad, axis=0)
        query_low = query_grad.astype(jnp.bfloat16)
        key_low = key_grad.astype(jnp.bfloat16)
        value_low = value_grad.astype(jnp.bfloat16)
        query_w_grad = contract_rows(rows_in, query_low)
        key_w_grad = contract_rows(rows_in, key_low)
        value_w_grad = contract_rows(rows_in, value_low)
        input_term = (
            contract_cols(query_low, full_query)
            + contract_cols(key_low, full_key)
            + contract_cols(value_low, full_value)
        )
        own_grad = lax.psum_scatter(
            input_term.astype(jnp.bfloat16), "tensor", scatter_dimension=1, tiled=True
        ).astype(jnp.float32)
        input_grads.append(
            own_grad + lax.dynamic_slice_in_dim(first_grad, column_start, own_cols, 1)
        )
        terms = (
            query_w_grad,
            query_bias_grad,
            key_w_grad,
            value_w_grad,
            value_bias_grad,
            out_grad,
            out_bias_grad,
            grad_gain_one,
            grad_shift_one,
            up_grad,
            up_bias_grad,
            down_grad,
            down_bias_grad,
            grad_gain_two,
            grad_shift_two,
        )
        if totals is None:
            totals = terms
        else:
            totals = tuple((running + addend for running, addend in zip(totals, terms)))
    summed = (
        lax.psum_scatter(totals[0], "dp", scatter_dimension=0, tiled=True),
        lax.psum_scatter(totals[2], "dp", scatter_dimension=0, tiled=True),
        lax.psum_scatter(totals[3], "dp", scatter_dimension=0, tiled=True),
        lax.psum_scatter(totals[5], "dp", scatter_dimension=1, tiled=True),
        lax.psum_scatter(totals[9], "dp", scatter_dimension=0, tiled=True),
        lax.psum_scatter(totals[11], "dp", scatter_dimension=1, tiled=True),
        lax.psum_scatter(totals[6], "dp", scatter_dimension=0, tiled=True),
        lax.psum_scatter(totals[7], "dp", scatter_dimension=0, tiled=True),
        lax.psum_scatter(totals[8], "dp", scatter_dimension=0, tiled=True),
        lax.psum_scatter(totals[12], "dp", scatter_dimension=0, tiled=True),
        lax.psum_scatter(totals[13], "dp", scatter_dimension=0, tiled=True),
        lax.psum_scatter(totals[14], "dp", scatter_dimension=0, tiled=True),
    )
    bias_sums = lax.psum((totals[1], totals[4], totals[10]), "dp")
    return (
        jnp.concatenate(layer_outputs, 0),
        jnp.concatenate(input_grads, 0),
        summed[0],
        bias_sums[0],
        summed[1],
        summed[2],
        bias_sums[1],
        summed[3],
        summed[6],
        summed[7],
        summed[8],
        summed[4],
        bias_sums[2],
        summed[5],
        summed[9],
        summed[10],
        summed[11],
    )


def place():
    dp = lax.axis_index("dp")
    tensor = lax.axis_index("tensor")
    return dp // 2, dp % 2, tensor // 2, tensor % 2

def device(z, x, y, core):
    return (z * 2 + x, y * 2 + core)

def greet(lines, all_along=False):
    z, x, y, core = place()
    barrier = pltpu.get_barrier_semaphore()

    def signal(target):
        pl.semaphore_signal(barrier, inc=1, device_id=target, device_id_type=MESH)

    signal(device(z, 1 - x, y, core))
    signal(device(z, x, 1 - y, core))
    signal(device(z, x, y, 1 - core))
    for k in range(1, lines if all_along else 2):
        pl.when(z >= k)(lambda: signal(device(z - k, x, y, core)))
        pl.when(z + k < lines)(lambda: signal(device(z + k, x, y, core)))
    if all_along:
        ends = lines - 1
    else:
        ends = jnp.where(z > 0, 1, 0) + jnp.where(z < lines - 1, 1, 0)
    pl.semaphore_wait(barrier, 3 + ends)


class Gather:
    def __init__(self, lines, whole, recv_sem, send_sem, rows):
        self.lines, self.whole, self.recv_sem, self.send_sem, self.rows = lines, whole, recv_sem, send_sem, rows
        self.here = place()
        self.sent = []

    def view(self, z, x, y):
        start = (z * 2 + x) * self.rows
        if not isinstance(start, int):
            start = pl.multiple_of(start, self.rows)
        return self.whole.at[y, pl.ds(start, self.rows)]

    def copy(self, z, x, y, way):
        mz, mx, my, core = self.here
        target = {"up": (mz + 1, mx, my), "down": (mz - 1, mx, my), "x": (mz, 1 - mx, my), "y": (mz, mx, 1 - my)}[way]
        index = y * self.lines * 2 + z * 2 + x
        return pltpu.make_async_remote_copy(
            src_ref=self.view(z, x, y), dst_ref=self.view(z, x, y),
            send_sem=self.send_sem.at[("up", "down", "x", "y").index(way), index],
            recv_sem=self.recv_sem.at[index],
            device_id=device(*target, core), device_id_type=MESH)

    def send(self, z, x, y, way, ok=None):
        if ok is None:
            self.copy(z, x, y, way).start()
        else:
            @pl.when(ok)
            def _():
                self.copy(z, x, y, way).start()
        self.sent.append((z, x, y, way, ok))

    def take(self, z, x, y):
        self.copy(z, x, y, "x").wait_recv()

    def begin(self):
        z, x, y, core = self.here
        self.send(z, x, y, "x")
        self.send(z, x, y, "y")
        self.send(z, x, y, "up", z < self.lines - 1)
        self.send(z, x, y, "down", z > 0)

    def planes(self, k):
        z, x, y, core = self.here
        for zz, ok in (((z, None),) if k == 0 else ((z - k, z - k >= 0), (z + k, z + k < self.lines))):
            def arrive(zz=zz):
                self.take(zz, 1 - x, y)
                self.take(zz, x, 1 - y)
            if ok is None:
                arrive()
            else:
                pl.when(ok)(arrive)
            even = zz % 2 == 0
            odd = zz % 2 == 1
            if ok is not None:
                even, odd = even & ok, odd & ok
            self.send(zz, 1 - x, y, "y", odd)
            self.send(zz, x, 1 - y, "x", even)

    def round(self, k):
        z, x, y, core = self.here
        if k < self.lines:
            for zz, ok, on, way in ((z - k, z - k >= 0, z < self.lines - 1, "up"), (z + k, z + k < self.lines, z > 0, "down")):
                pl.when(ok)(functools.partial(self.take, zz, x, y))
                self.send(zz, x, y, way, ok & on)
                self.send(zz, x, y, "x", ok)
                self.send(zz, x, y, "y", ok)
        self.planes(k - 1)

    def last(self):
        z, x, y, core = self.here
        for zz in range(self.lines):
            self.take(zz, 1 - x, 1 - y)

    def drain(self):
        for z, x, y, way, ok in self.sent:
            if ok is None:
                self.copy(z, x, y, way).wait_send()
            else:
                pl.when(ok)(lambda: self.copy(z, x, y, way).wait_send())


lanes = 128
block = 256


def dot(first, second, dims):
    return lax.dot_general(first, second, ((dims[:1], dims[1:]), ((), ())), preferred_element_type=jnp.float32)


plain, right_turned, left_turned = (1, 0), (1, 1), (0, 0)


def rows_at(start, size):
    return pl.ds(pl.multiple_of(start, size), size)


def low_half(rows):
    return lax.broadcasted_iota(jnp.int32, (rows, lanes), 1) < HEAD


def tile(index):
    return slice(index * lanes, (index + 1) * lanes)


def swapped(values):
    return pltpu.roll(values, HEAD, 1)


def attend_kernel(lines, shard, extra, tokens, limit, whole, extras, query, key, value, context, log_sum, recv, send, extra_recv, extra_send):
    z, x, y, core = place()
    own = z * 2 + x
    unit = shard.shape[1]
    total = tokens.shape[0]
    for part in range(3):
        whole[part, y, rows_at(own * unit, unit)] = shard[part]
    extras[y, rows_at(own * 16, 16)] = extra[...]
    greet(lines)
    parts = [Gather(lines, whole.at[part], recv.at[part], send.at[part], unit) for part in range(3)]
    small = Gather(lines, extras, extra_recv, extra_send, 16)
    small.begin()
    parts[0].begin()
    for step in range(1, lines + 1):
        small.round(step)
        parts[0].round(step)
        if step == lines - 1:
            parts[1].begin()
    small.last()
    parts[0].last()
    parts[1].round(1)

    low = low_half(block)
    bias = [extras[near, rows_at(own * 16, 16)].astype(jnp.float32)[0:1] for near in range(2)]

    def project(index, carry):
        rows = rows_at(index * block, block)
        inputs = tokens[rows]
        first = dot(inputs, whole[0, 0], plain) + bias[0]
        second = dot(inputs, whole[0, 1], plain) + bias[1]
        for which, target in enumerate((query, key, value)):
            scale = 0.125 if which == 0 else 1.0
            near, far = first[:, tile(which)], second[:, tile(which)]
            mixed = jnp.where(low, first[:, tile(3 + which)], second[:, tile(3 + which)])
            for pair, values in enumerate((near, far, mixed)):
                target[rows, tile(pair)] = (values * scale).astype(jnp.bfloat16)
        return carry

    lax.fori_loop(0, total // block, project, 0)
    steps = [
        lambda: parts[1].round(2),
        lambda: parts[1].round(3),
        lambda: (parts[1].round(4), parts[2].begin()),
        lambda: (parts[1].last(), parts[2].round(1)),
        lambda: parts[2].round(2),
        lambda: parts[2].round(3),
    ]
    keep = low_half(total)
    for head in range(6):
        steps[head]()
        attend_head(head, query, key, value, limit, context, log_sum, keep)
    parts[2].round(4)
    parts[2].last()
    for part in parts:
        part.drain()
    small.drain()


def attend_head(head, query, key, value, limit, context, log_sum, keep):
    pair, upper = head // 2, head % 2
    total = query.shape[0]
    chosen = ~keep if upper else keep
    keys = jnp.where(chosen, key[:, tile(pair)], jnp.zeros((), jnp.bfloat16))
    values = value[:, tile(pair)]
    low = low_half(block)
    here = lax.broadcasted_iota(jnp.int32, (block, lanes), 1) == head
    places = lax.broadcasted_iota(jnp.int32, (block, total), 1)

    def one(index, carry):
        rows = rows_at(index * block, block)
        scores = dot(query[rows, tile(pair)], keys, right_turned)
        scores = jnp.where(places < limit[rows], scores, masked_score)
        top = jnp.max(scores, axis=-1, keepdims=True)
        grown = jnp.exp(scores - top)
        sums = jnp.sum(grown, axis=-1, keepdims=True)
        probs = (grown * (1.0 / sums)).astype(jnp.bfloat16)
        result = dot(probs, values, plain).astype(jnp.bfloat16)
        logs = top + jnp.log(sums)
        if upper:
            context[rows, tile(pair)] = jnp.where(low, context[rows, tile(pair)], result)
        else:
            context[rows, tile(pair)] = result
        if head == 0:
            log_sum[rows] = jnp.where(here, logs, 0.0)
        else:
            log_sum[rows] = jnp.where(here, logs, log_sum[rows])
        return carry

    lax.fori_loop(0, total // block, one, 0)


def norm_rows(values):
    centred = values - jnp.mean(values, axis=-1, keepdims=True)
    variance = jnp.mean(centred * centred, axis=-1, keepdims=True)
    scale = lax.rsqrt(variance + norm_epsilon)
    return centred * scale, scale


def norm_rows_back(upstream, hat, scale, gain):
    scaled = upstream * gain
    return scale * (scaled - jnp.mean(scaled, axis=-1, keepdims=True) - hat * jnp.mean(scaled * hat, axis=-1, keepdims=True))


def total_rows(values):
    return jnp.sum(values, axis=0, keepdims=True)


def swap_copy(src, dst, sems, index, near):
    z, x, y, core = place()
    target = device(z, x, y, 1 - core) if near else device(z, x, 1 - y, core)
    return pltpu.make_async_remote_copy(
        src_ref=src, dst_ref=dst, send_sem=sems.at[0, index], recv_sem=sems.at[1, index],
        device_id=target, device_id_type=MESH)


def turn_out(whole, target):
    low = low_half(whole.shape[2])
    first = [whole[0, 0, :, tile(3 + i)].astype(jnp.float32) for i in range(3)]
    second = [whole[0, 1, :, tile(3 + i)].astype(jnp.float32) for i in range(3)]
    for pair, values in enumerate((
        jnp.where(low, swapped(first[0]), first[1]),
        jnp.where(low, second[0], swapped(second[1])),
        jnp.where(low, swapped(first[2]), swapped(second[2])),
    )):
        target[:, tile(pair)] = values.astype(jnp.bfloat16)


def spread_vectors(lines, extras, vectors):
    unit = vectors.shape[1] // (lines * 2)
    column = lax.broadcasted_iota(jnp.int32, (lanes, vectors.shape[1]), 1)
    row = lax.broadcasted_iota(jnp.int32, (lanes, vectors.shape[1]), 0)
    result = jnp.zeros((16, vectors.shape[1]), jnp.float32)
    for own in range(lines * 2):
        spot = ((column == row + own * unit) & (row < unit)).astype(jnp.bfloat16)
        result = result + dot(extras[0, own * 16 : own * 16 + 16, 0:lanes], spot, plain)
    vectors[...] = result


def feed_kernel(lines, whole, extras, tokens, context, cotangent,
                output, first_grad, context_grad, down_grad, up_grad, out_grad, sums,
                turned, vectors, sent, got, hat_one, scale_one, normed, slope, hidden, second_grad, second_low, expanded_low, first_low, sems):
    z, x, y, core = place()
    own = z * 2 + x
    half = tokens.shape[0] // 2
    mine, theirs = core * half, (1 - core) * half
    barrier = pltpu.get_barrier_semaphore()
    for target in (device(z, x, y, 1 - core), device(z, x, 1 - y, core)):
        pl.semaphore_signal(barrier, inc=1, device_id=target, device_id_type=MESH)
    spread_vectors(lines, extras, vectors)
    turn_out(whole, turned)
    pl.semaphore_wait(barrier, 2)
    sums[...] = jnp.zeros_like(sums)
    vector = lambda index: vectors[2 + index : 3 + index]
    up_bias = [extras[near, rows_at(own * 16, 16)].astype(jnp.float32)[1:2] for near in range(2)]
    count = half // block

    def loop(body):
        lax.fori_loop(0, count, lambda index, carry: (body(index), carry)[1], 0)

    def add_sum(index, values):
        sums[index : index + 1] += total_rows(values)

    def attended(rows):
        return dot(context[rows], turned[...], right_turned)

    def away(term, index):
        def body(step):
            sent[index, rows_at(step * block, block)] = term(rows_at(theirs + step * block, block))
        loop(body)
        copy = swap_copy(sent.at[index], got.at[index], sems, index, True)
        copy.start()
        return copy

    copy_a = away(attended, 0)
    def stay_a(step):
        hat_one[rows_at(step * block, block)] = attended(rows_at(mine + step * block, block))
    loop(stay_a)
    copy_a.wait_recv()

    def first_norm(step):
        rows = rows_at(step * block, block)
        full = rows_at(mine + step * block, block)
        values = tokens[full].astype(jnp.float32) + ((hat_one[rows] + got[0, rows]) + vector(0))
        hat, scale = norm_rows(values)
        hat_one[rows] = hat
        scale_one[rows] = jnp.broadcast_to(scale, (block, lanes))
        normed[full] = (hat * vector(1) + vector(2)).astype(jnp.bfloat16)
    loop(first_norm)
    copy_n = swap_copy(normed.at[rows_at(mine, half)], normed.at[rows_at(mine, half)], sems, 3, True)
    copy_n.start()

    def expand(base):
        def body(step):
            rows = rows_at(base + step * block, block)
            inputs = normed[rows]
            for near in range(2):
                columns = slice(near * whole.shape[3], (near + 1) * whole.shape[3])
                expanded = dot(inputs, whole[1, near], plain) + up_bias[near]
                cdf = 0.5 * (1.0 + lax.erf(expanded * inv_root_two))
                hidden[rows, columns] = (expanded * cdf).astype(jnp.bfloat16)
                slope[rows, columns] = cdf + expanded * jnp.exp(-0.5 * expanded * expanded) * inv_root_tau
        loop(body)
    expand(mine)
    copy_n.wait_recv()
    expand(theirs)

    def lowered(rows):
        width = whole.shape[3]
        return dot(hidden[rows, 0:width], whole[2, 0], right_turned) + dot(hidden[rows, width : 2 * width], whole[2, 1], right_turned)
    copy_b = away(lowered, 1)
    def stay_b(step):
        second_grad[rows_at(step * block, block)] = lowered(rows_at(mine + step * block, block))
    loop(stay_b)
    copy_b.wait_recv()
    home = y * tokens.shape[0] + mine

    def second_norm(step):
        rows = rows_at(step * block, block)
        full = rows_at(mine + step * block, block)
        values = normed[full].astype(jnp.float32) + ((second_grad[rows] + got[1, rows]) + vector(3))
        hat, scale = norm_rows(values)
        output[rows_at(home + step * block, block)] = (hat * vector(4) + vector(5)).astype(jnp.bfloat16)
        upstream = cotangent[full].astype(jnp.float32)
        grad = norm_rows_back(upstream, hat, scale, vector(4))
        second_grad[rows] = grad
        second_low[full] = grad.astype(jnp.bfloat16)
        add_sum(3, grad)
        add_sum(4, upstream * hat)
        add_sum(5, upstream)
    loop(second_norm)
    copy_s = swap_copy(second_low.at[rows_at(mine, half)], second_low.at[rows_at(mine, half)], sems, 4, True)
    copy_s.start()
    out_rows = output.at[rows_at(home, half)]
    copy_o = swap_copy(out_rows, out_rows, sems, 5, True)
    copy_o.start()
    copy_p = swap_copy(out_rows, out_rows, sems, 6, False)
    copy_p.start()

    def contract(base):
        def body(step):
            rows = rows_at(base + step * block, block)
            inputs = second_low[rows]
            for near in range(2):
                width = whole.shape[3]
                columns = slice(near * width, (near + 1) * width)
                grad = dot(inputs, whole[2, near], plain) * slope[rows, columns]
                add_sum(8 + near, grad)
                expanded_low[rows, columns] = grad.astype(jnp.bfloat16)
        loop(body)
    contract(mine)
    copy_s.wait_recv()
    contract(theirs)

    def normed_term(rows):
        width = whole.shape[3]
        return dot(expanded_low[rows, 0:width], whole[1, 0], right_turned) + dot(expanded_low[rows, width : 2 * width], whole[1, 1], right_turned)
    copy_c = away(normed_term, 2)
    def stay_c(step):
        rows = rows_at(step * block, block)
        second_grad[rows] = second_grad[rows] + normed_term(rows_at(mine + step * block, block))
    loop(stay_c)
    width = whole.shape[3]
    for near in range(2):
        columns = slice(near * width, (near + 1) * width)
        down_grad[near] = dot(second_low[...], hidden[:, columns], left_turned).astype(jnp.bfloat16)
    copy_c.wait_recv()

    def first_norm_back(step):
        rows = rows_at(step * block, block)
        full = rows_at(mine + step * block, block)
        upstream = second_grad[rows] + got[2, rows]
        hat = hat_one[rows]
        grad = norm_rows_back(upstream, hat, scale_one[rows][:, 0:1], vector(1))
        first_grad[rows] = grad
        first_low[full] = grad.astype(jnp.bfloat16)
        add_sum(0, grad)
        add_sum(1, upstream * hat)
        add_sum(2, upstream)
    loop(first_norm_back)
    copy_f = swap_copy(first_low.at[rows_at(mine, half)], first_low.at[rows_at(mine, half)], sems, 7, True)
    copy_f.start()
    for near in range(2):
        columns = slice(near * width, (near + 1) * width)
        up_grad[near] = dot(normed[...], expanded_low[:, columns], left_turned).astype(jnp.bfloat16)
    copy_f.wait_recv()

    def back_out(step):
        rows = rows_at(step * block, block)
        context_grad[rows] = dot(first_low[rows], turned[...], plain).astype(jnp.bfloat16)
    lax.fori_loop(0, 2 * count, lambda index, carry: (back_out(index), carry)[1], 0)
    out_grad[...] = dot(first_low[...], context[...], left_turned)

    copy_p.wait_recv()
    far_rows = output.at[rows_at((1 - y) * tokens.shape[0] + mine, half)]
    copy_q = swap_copy(far_rows, far_rows, sems, 8, True)
    copy_q.start()
    copy_o.wait_recv()
    copy_q.wait_recv()
    for copy in (copy_a, copy_b, copy_c, copy_n, copy_s, copy_f, copy_o, copy_p, copy_q):
        copy.wait_send()


class Scatter:
    def __init__(self, lines, terms, slots, recv_sem, send_sem, rows):
        self.lines, self.terms, self.slots = lines, terms, slots
        self.recv_sem, self.send_sem, self.rows = recv_sem, send_sem, rows
        self.here = place()
        self.sent = []
        self.order = [z for pair in zip(range(lines // 2), reversed(range(lines // 2, lines))) for z in reversed(pair)]

    def view(self, z, x, y):
        return self.terms.at[y, rows_at((z * 2 + x) * self.rows, self.rows)]

    def copy(self, z, x, y, way, kind):
        mz, mx, my, core = self.here
        target = {"up": (mz + 1, mx, my), "down": (mz - 1, mx, my), "x": (mz, 1 - mx, my), "y": (mz, mx, 1 - my)}[way]
        return pltpu.make_async_remote_copy(
            src_ref=self.view(z, x, y), dst_ref=self.slots.at[kind, z],
            send_sem=self.send_sem.at[kind, z], recv_sem=self.recv_sem.at[kind, z],
            device_id=device(*target, core), device_id_type=MESH)

    def send(self, z, x, y, way, kind, ok=None):
        if ok is None:
            self.copy(z, x, y, way, kind).start()
        else:
            pl.when(ok)(lambda: self.copy(z, x, y, way, kind).start())
        self.sent.append((z, x, y, way, kind, ok))

    def taken(self, z, x, y, kind):
        self.copy(z, x, y, "x", kind).wait_recv()
        return self.slots[kind, z].astype(jnp.float32)

    def add(self, z, x, y, kind):
        arrived = self.taken(z, x, y, kind)
        start = rows_at((z * 2 + x) * self.rows, self.rows)
        self.terms[y, start] = (self.terms[y, start].astype(jnp.float32) + arrived).astype(jnp.bfloat16)

    def begin(self):
        z, x, y, core = self.here
        for zz in self.order:
            self.send(zz, 1 - x, 1 - y, "x" if zz % 2 == 0 else "y", 0)
        for zz in self.order:
            if zz % 2:
                self.send(zz, x, 1 - y, "y", 2)
            else:
                self.send(zz, 1 - x, y, "x", 1)

    def corners(self):
        z, x, y, core = self.here
        for zz in self.order:
            if zz % 2 == 0:
                self.add(zz, x, 1 - y, 0)
                self.send(zz, x, 1 - y, "y", 2)
            else:
                self.add(zz, 1 - x, y, 0)
                self.send(zz, 1 - x, y, "x", 1)

    def line(self, k):
        z, x, y, core = self.here
        for zz, ok, on, way, kind in ((z + k, z + k < self.lines, z > 0, "up", 3), (z - k, z - k >= 0, z < self.lines - 1, "down", 4)):
            def step(zz=zz, on=on, kind=kind):
                self.add(zz, x, y, 1)
                self.add(zz, x, y, 2)
                pl.when(on)(lambda: self.add(zz, x, y, kind))
            pl.when(ok)(step)
            self.send(zz, x, y, way, kind, ok)

    def own(self, target):
        z, x, y, core = self.here
        start = rows_at((z * 2 + x) * self.rows, self.rows)
        target[...] = self.terms[y, start].astype(jnp.float32) + self.taken(z, x, y, 1) + self.taken(z, x, y, 2)
        def more(kind):
            target[...] += self.taken(z, x, y, kind)
        pl.when(z > 0)(lambda: more(3))
        pl.when(z < self.lines - 1)(lambda: more(4))

    def drain(self):
        for z, x, y, way, kind, ok in self.sent:
            if ok is None:
                self.copy(z, x, y, way, kind).wait_send()
            else:
                pl.when(ok)(lambda: self.copy(z, x, y, way, kind).wait_send())


def back_head(head, query, key, value, context_grad, limit, log_rows, dot_rows, keep, query_acc, key_acc, value_acc):
    pair, upper = head // 2, head % 2
    total = query.shape[0]
    chosen = ~keep if upper else keep
    nothing = jnp.zeros((), jnp.bfloat16)
    keys = jnp.where(chosen, key[:, tile(pair)], nothing)
    values = jnp.where(chosen, value[:, tile(pair)], nothing)
    low = low_half(block)
    low = ~low if upper else low
    places = lax.broadcasted_iota(jnp.int32, (total, block), 0)

    def one(index, carry):
        rows = rows_at(index * block, block)
        asked = query[rows, tile(pair)]
        wanted = context_grad[rows, tile(pair)]
        scores = dot(keys, asked, right_turned)
        grown = jnp.exp(scores - log_rows[index, head : head + 1])
        probs = jnp.where(places < limit[index, 0:1], grown, 0.0)
        prob_grad = dot(values, wanted, right_turned)
        score_grad = (probs * (prob_grad - dot_rows[index, head : head + 1])).astype(jnp.bfloat16)
        value_term = dot(probs.astype(jnp.bfloat16), jnp.where(low, wanted, nothing), plain)
        key_term = dot(score_grad, jnp.where(low, asked, nothing), plain)
        query_term = dot(score_grad, keys, left_turned)
        if upper:
            query_acc[rows] += query_term
            value_acc[...] += value_term
            key_acc[...] += key_term
        else:
            query_acc[rows] = query_term
            @pl.when(index == 0)
            def _():
                value_acc[...] = value_term
                key_acc[...] = key_term
            @pl.when(index > 0)
            def _():
                value_acc[...] += value_term
                key_acc[...] += key_term
        return carry

    lax.fori_loop(0, total // block, one, 0)


def back_kernel(lines, whole, tokens, query, key, value, context, context_grad, log_sum, limit, first_grad, down_grad, up_grad, out_grad, sums,
                own_sums, shards, input_grad,
                log_rows, dot_rows, query_acc, key_acc, value_acc, packed, terms, slots, row_got, turn_sent, turn_got, far_sent, far_got, vec_got,
                recv, send, sems):
    z, x, y, core = place()
    own = z * 2 + x
    total = tokens.shape[0]
    half = total // 2
    mine, theirs = core * half, (1 - core) * half
    unit = shards.shape[1]
    greet(lines, True)
    for near in range(2):
        terms[2, near] = down_grad[near]
        terms[1, near] = up_grad[near]
    parts = [Scatter(lines, terms.at[part], slots.at[part], recv.at[part], send.at[part], unit) for part in range(3)]
    parts[2].begin()
    low = low_half(block)
    lane = lax.broadcasted_iota(jnp.int32, (block, lanes), 1)
    for index in range(total // block):
        rows = slice(index * block, (index + 1) * block)
        stats = jnp.zeros((block, lanes), jnp.float32)
        for pair in range(3):
            product = context_grad[rows, tile(pair)].astype(jnp.float32) * context[rows, tile(pair)].astype(jnp.float32)
            lower = jnp.sum(jnp.where(low, product, 0.0), axis=-1, keepdims=True)
            upper = jnp.sum(jnp.where(low, 0.0, product), axis=-1, keepdims=True)
            stats = jnp.where(lane == 2 * pair, lower, jnp.where(lane == 2 * pair + 1, upper, stats))
        dot_rows[index] = stats.T[0:8]
        log_rows[index] = log_sum[rows].T[0:8]
    keep = low_half(total)
    packed[:, :, 3 * lanes :] = jnp.zeros((2, total, 3 * lanes), jnp.bfloat16)
    steps = [
        lambda: parts[2].corners(),
        lambda: (parts[2].line(3), parts[1].begin()),
        lambda: (parts[2].line(2), parts[1].corners()),
        lambda: (parts[2].line(1), parts[1].line(3)),
        lambda: (parts[2].own(shards.at[2]), parts[1].line(2)),
        lambda: parts[1].line(1),
    ]
    value_sums, query_sums = [], []
    for head in range(6):
        back_head(head, query, key, value, context_grad, limit, log_rows, dot_rows, keep, query_acc, key_acc, value_acc)
        steps[head]()
        pair = head // 2
        if head % 2:
            def place_pair(index, carry):
                rows = rows_at(index * block, block)
                asked = query_acc[rows] * 0.125
                keyed = key_acc[rows]
                valued = value_acc[rows]
                carry = (carry[0] + total_rows(asked), carry[1] + total_rows(valued))
                for which, values in enumerate((asked, keyed, valued)):
                    if pair < 2:
                        packed[pair, rows, tile(which)] = values.astype(jnp.bfloat16)
                    else:
                        packed[0, rows, tile(3 + which)] = jnp.where(low, values, 0.0).astype(jnp.bfloat16)
                        packed[1, rows, tile(3 + which)] = jnp.where(low, 0.0, values).astype(jnp.bfloat16)
                return carry
            empty = jnp.zeros((1, lanes), jnp.float32)
            asked_sum, valued_sum = lax.fori_loop(0, total // block, place_pair, (empty, empty))
            query_sums.append(asked_sum)
            value_sums.append(valued_sum)
    low = low_half(whole.shape[2])
    outs = [out_grad[:, tile(pair)] for pair in range(3)]
    homes = (
        (swapped(outs[0]), outs[0], swapped(outs[2])),
        (outs[1], swapped(outs[1]), swapped(outs[2])),
    )
    for near in range(2):
        grads = dot(tokens[...], packed[near], left_turned)
        terms[0, near, :, 0 : 3 * lanes] = grads[:, 0 : 3 * lanes].astype(jnp.bfloat16)
        for which in range(3):
            values = grads[:, tile(3 + which)]
            home = homes[near][which]
            values = jnp.where(low, values, home) if near == 0 else jnp.where(low, home, values)
            terms[0, near, :, tile(3 + which)] = values.astype(jnp.bfloat16)
    parts[0].begin()
    narrow = whole.shape[2] // 4
    def columns(near, which, rows):
        spot = rows_at((2 * near + which) * narrow, narrow)
        return dot(packed[0, rows], whole[0, spot], right_turned) + dot(packed[1, rows], whole[1, spot], right_turned)
    def pick(values, near, which):
        left = values[:, 2 * near * narrow : (2 * near + 1) * narrow]
        right = values[:, (2 * near + 1) * narrow : (2 * near + 2) * narrow]
        return jnp.where(which == 0, left, right)
    def across(index, carry):
        for near in range(2):
            mine_rows = rows_at(mine + index * block, block)
            turn_sent[near, mine_rows] = (columns(near, 1 - core, mine_rows) + pick(first_grad[rows_at(index * block, block)], near, 1 - core)).astype(jnp.bfloat16)
            their_rows = rows_at(theirs + index * block, block)
            turn_sent[near, their_rows] = columns(near, 1 - core, their_rows).astype(jnp.bfloat16)
        return carry
    lax.fori_loop(0, half // block, across, 0)
    copy_t = swap_copy(turn_sent, turn_got, sems, 0, True)
    copy_t.start()
    parts[1].own(shards.at[1])
    parts[0].corners()
    parts[0].line(3)
    parts[0].line(2)
    copy_t.wait_recv()
    def pick_y(values, near, which):
        return jnp.where(near == 0, pick(values, 0, which), pick(values, 1, which))
    def finish_any(near, rows, local):
        values = columns(near, core, rows) + turn_got[near, rows].astype(jnp.float32)
        if local is not None:
            values = values + pick_y(first_grad[local], near, core)
        return values
    def far(index, carry):
        for base, local in ((mine, rows_at(index * block, block)), (theirs, None)):
            rows = rows_at(base + index * block, block)
            far_sent[rows] = finish_any(1 - y, rows, local).astype(jnp.bfloat16)
        return carry
    lax.fori_loop(0, half // block, far, 0)
    copy_u = swap_copy(far_sent, far_got, sems, 1, False)
    copy_u.start()
    def close(index, carry):
        for base, local in ((mine, rows_at(index * block, block)), (theirs, None)):
            rows = rows_at(base + index * block, block)
            input_grad[rows_at(y * total + base + index * block, block)] = finish_any(y, rows, local)
        return carry
    lax.fori_loop(0, half // block, close, 0)
    row_got[0] = sums[...]
    copies = []
    empty = jnp.zeros((1, 3 * lanes), jnp.float32)
    lower = lax.broadcasted_iota(jnp.int32, (1, lanes), 1) < HEAD
    for near in range(2):
        row_got[0, 6 + near : 7 + near] = jnp.concatenate(
            [query_sums[near], jnp.zeros((1, lanes), jnp.float32), value_sums[near],
             query_sums[2], jnp.zeros((1, lanes), jnp.float32), value_sums[2]], axis=1)
    def vector_step(step, target, count):
        copy = pltpu.make_async_remote_copy(
            src_ref=row_got.at[step, pl.ds(0, count)], dst_ref=vec_got.at[step, pl.ds(0, count)], send_sem=sems.at[0, 3 + step], recv_sem=sems.at[1, 3 + step],
            device_id=target, device_id_type=MESH)
        copy.start()
        return copy
    copy_v = vector_step(0, device(z, x, y, 1 - core), 16)
    copy_v.wait_recv()
    rows16 = lax.broadcasted_iota(jnp.int32, row_got.shape[1:], 0)
    row_got[1] = row_got[0] + jnp.where(rows16 < 6, vec_got[0], 0.0)
    copies.append(copy_v)
    copy_v = vector_step(1, device(z, 1 - x, y, core), 16)
    parts[0].line(1)
    copy_v.wait_recv()
    copies.append(copy_v)
    row_got[2] = row_got[1] + vec_got[1]
    copy_v = vector_step(2, device(z, x, 1 - y, core), 16)
    copy_v.wait_recv()
    copies.append(copy_v)
    row_got[3] = row_got[2] + vec_got[2]
    line_copies = []
    for k in range(1, lines):
        for there, ok in ((z + k, z + k < lines), (z - k, z - k >= 0)):
            def start(there=there):
                pltpu.make_async_remote_copy(
                    src_ref=row_got.at[3], dst_ref=row_got.at[4 + z], send_sem=sems.at[0, 8 + there], recv_sem=sems.at[1, 8 + z],
                    device_id=device(there, x, y, core), device_id_type=MESH).start()
            pl.when(ok)(start)
            line_copies.append((there, ok))
    row_got[4 + z] = row_got[3]
    parts[0].own(shards.at[0])
    for k in range(1, lines):
        for there, ok in ((z + k, z + k < lines), (z - k, z - k >= 0)):
            def wait(there=there):
                pltpu.make_async_remote_copy(
                    src_ref=row_got.at[3], dst_ref=row_got.at[4 + there], send_sem=sems.at[0, 8 + there], recv_sem=sems.at[1, 8 + there],
                    device_id=device(there, x, y, core), device_id_type=MESH).wait()
            pl.when(ok)(wait)
    result = row_got[4]
    for line in range(1, lines):
        result = result + row_got[4 + line]
    own_sums[...] = result
    copy_u.wait_recv()
    input_grad[rows_at((1 - y) * total, total)] = far_got[...].astype(jnp.float32)
    for copy in (copy_t, copy_u, *copies):
        copy.wait_send()
    for part in parts:
        part.drain()


def fits(mesh, tokens, seq_lens, block_sizes, w_query, *others):
    unit, columns = w_query.shape
    w_up = others[8]
    return (
        mesh.shape["tensor"] == 4
        and mesh.shape["dp"] % 4 == 0
        and seq_lens.shape[0] == 2
        and tokens.shape[0] % (4 * block) == 0
        and columns == 3 * HEAD
        and unit % 16 == 0
        and unit <= lanes
        and unit * mesh.shape["dp"] == tokens.shape[1] == 12 * HEAD == w_up.shape[1]
    )


def vmem(count):
    return [pl.BlockSpec(memory_space=pltpu.VMEM)] * count


def on_device_fast(lines, tokens, seq_lens, block_sizes, w_query, b_query, w_key, w_value, b_value, w_out, b_out,
                   gain_one, shift_one, w_up, b_up, w_down, b_down, gain_two, shift_two, cotangent):
    bf16, f32 = jnp.bfloat16, jnp.float32
    y = lax.axis_index("tensor") // 2
    total = tokens.shape[0] // 2
    width = tokens.shape[1]
    unit = w_query.shape[0]
    slots = lines * 4
    rows_in = lax.dynamic_slice_in_dim(tokens, y * total, total)
    upstream = lax.dynamic_slice_in_dim(cotangent, y * total, total)
    places = jnp.arange(total, dtype=jnp.int32)
    size, length = block_sizes[y], seq_lens[y]
    limit = jnp.minimum((places // size + 1) * size, length)
    limit_rows = jnp.broadcast_to(limit.reshape(total // block, 1, block), (total // block, 8, block))
    limit = limit.reshape(total, 1)

    pair, single = slice(0, 2 * HEAD), slice(2 * HEAD, 3 * HEAD)
    turned = w_out.T
    firsts = [array[:, pair] for array in (w_query, w_key, w_value)]
    singles = [array[:, single] for array in (w_query, w_key, w_value)]
    outs = [turned[:, i * HEAD : (i + 1) * HEAD] for i in range(3)]
    mixed = lambda order: jnp.concatenate(firsts + [piece for two in zip(*order) for piece in two], axis=1)
    shard = jnp.stack([jnp.where(y == 0, mixed((singles, outs)), mixed((outs, singles))), w_up, w_down.T])
    zero, zeros = jnp.zeros((HEAD,), bf16), jnp.zeros((2 * HEAD,), bf16)
    near = jnp.concatenate([b_query[pair], zeros, b_value[pair], b_query[single], zero, zeros, b_value[single], zero])
    far = jnp.concatenate([b_query[pair], zeros, b_value[pair], zero, b_query[single], zeros, zero, b_value[single]])
    vectors = jnp.stack([b_out, gain_one, shift_one, b_down, gain_two, shift_two])
    extra = jnp.concatenate([
        jnp.where(y == 0, near, far)[None], b_up[None],
        jnp.pad(vectors, ((0, 0), (0, width - unit))), jnp.zeros((8, width), bf16)])

    dma = pltpu.SemaphoreType.DMA
    shape = jax.ShapeDtypeStruct
    half_width = width // 2
    whole, extras, query, key, value, context, log_sum = pl.pallas_call(
        functools.partial(attend_kernel, lines),
        out_shape=(
            shape((3, 2, width, width), bf16), shape((2, lines * 2 * 16, width), bf16),
            *[shape((total, half_width), bf16)] * 4, shape((total, lanes), f32)),
        in_specs=vmem(4), out_specs=tuple(vmem(7)),
        scratch_shapes=[dma((3, slots)), dma((3, 4, slots)), dma((slots,)), dma((4, slots))],
        compiler_params=pltpu.CompilerParams(collective_id=0, has_side_effects=True, vmem_limit_bytes=56 * 2**20),
    )(shard, extra, rows_in, limit)

    output, first_grad, context_grad, down_grad, up_grad, out_grad, sums = pl.pallas_call(
        functools.partial(feed_kernel, lines),
        out_shape=(
            shape((2 * total, width), bf16), shape((total // 2, width), f32), shape((total, half_width), bf16),
            shape((2, width, width), bf16), shape((2, width, width), bf16), shape((width, half_width), f32), shape((16, width), f32)),
        in_specs=vmem(5), out_specs=tuple(vmem(7)),
        scratch_shapes=[
            pltpu.VMEM((width, half_width), bf16), pltpu.VMEM((16, width), f32),
            pltpu.VMEM((3, total // 2, width), f32), pltpu.VMEM((3, total // 2, width), f32),
            pltpu.VMEM((total // 2, width), f32), pltpu.VMEM((total // 2, lanes), f32), pltpu.VMEM((total, width), bf16),
            pltpu.VMEM((total, 2 * width), f32), pltpu.VMEM((total, 2 * width), bf16),
            pltpu.VMEM((total // 2, width), f32), pltpu.VMEM((total, width), bf16), pltpu.VMEM((total, 2 * width), bf16),
            pltpu.VMEM((total, width), bf16), dma((2, 16))],
        compiler_params=pltpu.CompilerParams(collective_id=1, has_side_effects=True, vmem_limit_bytes=60 * 2**20),
    )(whole, extras, rows_in, context, upstream)

    own_sums, shards, input_grad = pl.pallas_call(
        functools.partial(back_kernel, lines),
        out_shape=(shape((16, width), f32), shape((3, unit, width), f32), shape((2 * total, width // 4), f32)),
        in_specs=vmem(14), out_specs=tuple(vmem(3)),
        scratch_shapes=[
            pltpu.VMEM((total // block, 8, block), f32), pltpu.VMEM((total // block, 8, block), f32),
            *[pltpu.VMEM((total, lanes), f32)] * 3, pltpu.VMEM((2, total, width), bf16),
            pltpu.VMEM((3, 2, width, width), bf16), pltpu.VMEM((3, 5, lines, unit, width), bf16),
            pltpu.VMEM((4 + lines, 16, width), f32),
            pltpu.VMEM((2, total, width // 4), bf16), pltpu.VMEM((2, total, width // 4), bf16),
            pltpu.VMEM((total, width // 4), bf16), pltpu.VMEM((total, width // 4), bf16),
            pltpu.VMEM((3, 16, width), f32),
            dma((3, 5, lines)), dma((3, 5, lines)), dma((2, 8 + lines))],
        compiler_params=pltpu.CompilerParams(collective_id=2, has_side_effects=True, vmem_limit_bytes=60 * 2**20),
    )(whole[0], rows_in, query, key, value, context, context_grad, log_sum, limit_rows, first_grad, down_grad, up_grad, out_grad, sums)

    mix = shards[0]
    def joined(which):
        first = mix[:, which * 2 * HEAD : (which + 1) * 2 * HEAD]
        start = (6 + 2 * which) * HEAD
        return jnp.concatenate([first, jnp.where(y == 0, mix[:, start : start + HEAD], mix[:, start + HEAD : start + 2 * HEAD])], axis=1)
    out_turned = jnp.concatenate([
        jnp.where(y == 0, mix[:, (7 + 2 * i) * HEAD : (8 + 2 * i) * HEAD], mix[:, (6 + 2 * i) * HEAD : (7 + 2 * i) * HEAD])
        for i in range(3)], axis=1)
    vector_grads = [
        lax.dynamic_slice_in_dim(own_sums[i], lax.axis_index("dp") * unit, unit) for i in range(6)]
    qkv = jnp.where(y == 0, own_sums[6], own_sums[7])
    up_bias_grad = jnp.where(y == 0, own_sums[8], own_sums[9])
    def bias_of(which):
        start = (6 + 2 * which) * HEAD
        return jnp.concatenate([
            qkv[which * 2 * HEAD : (which + 1) * 2 * HEAD],
            jnp.where(y == 0, qkv[start : start + HEAD], qkv[start + HEAD : start + 2 * HEAD])])
    return (
        output, input_grad,
        joined(0), bias_of(0), joined(1), joined(2), bias_of(2), out_turned.T,
        vector_grads[0], vector_grads[1], vector_grads[2],
        shards[1], up_bias_grad, shards[2].T,
        vector_grads[3], vector_grads[4], vector_grads[5])


def solution(mesh):
    in_specs = (
        P("dp", None),
        P("dp"),
        P("dp"),
        P("dp", "tensor"),
        P("tensor"),
        P("dp", "tensor"),
        P("dp", "tensor"),
        P("tensor"),
        P("tensor", "dp"),
        P("dp"),
        P("dp"),
        P("dp"),
        P("dp", "tensor"),
        P("tensor"),
        P("tensor", "dp"),
        P("dp"),
        P("dp"),
        P("dp"),
        P("dp", None),
    )
    out_specs = (
        P("dp", None),
        P("dp", "tensor"),
        P("dp", "tensor"),
        P("tensor"),
        P("dp", "tensor"),
        P("dp", "tensor"),
        P("tensor"),
        P("tensor", "dp"),
        P("dp"),
        P("dp"),
        P("dp"),
        P("dp", "tensor"),
        P("tensor"),
        P("tensor", "dp"),
        P("dp"),
        P("dp"),
        P("dp"),
    )
    lines = mesh.shape["dp"] // 2

    def on_device(*arrays):
        if fits(mesh, *arrays):
            return on_device_fast(lines, *arrays)
        return on_device_plain(*arrays)

    return jax.shard_map(
        on_device, mesh=mesh, in_specs=in_specs, out_specs=out_specs, check_vma=False
    )
```

```python
import functools

import jax
import jax.numpy as jnp
from jax import lax
from jax.experimental import pallas as pl
from jax.experimental.pallas import tpu as pltpu
from jax.sharding import PartitionSpec as P

HEAD = 64
MESH = pl.DeviceIdType.MESH

norm_epsilon = 1e-12
inv_root_two = 0.7071067811865476
inv_root_tau = 0.3989422804014327
masked_score = -1000000000.0


def matmul(first_operand, second_operand):
    return jnp.dot(first_operand, second_operand, preferred_element_type=jnp.float32)


def contract_rows(first_operand, second_operand):
    return lax.dot_general(
        first_operand, second_operand, (((0,), (0,)), ((), ())), preferred_element_type=jnp.float32
    )


def contract_cols(first_operand, second_operand):
    return lax.dot_general(
        first_operand, second_operand, (((1,), (1,)), ((), ())), preferred_element_type=jnp.float32
    )


def norm_forward(row_values, gain_row, offset_row):
    row_mean = jnp.mean(row_values, axis=-1, keepdims=True)
    centred = row_values - row_mean
    variance = jnp.mean(centred * centred, axis=-1, keepdims=True)
    inv_scale = lax.rsqrt(variance + norm_epsilon)
    normal_rows = centred * inv_scale
    return (normal_rows * gain_row + offset_row, normal_rows, inv_scale)


def norm_backward(upstream, normal_rows, inv_scale, gain_row):
    scaled = upstream * gain_row
    row_grad = inv_scale * (
        scaled
        - jnp.mean(scaled, axis=-1, keepdims=True)
        - normal_rows * jnp.mean(scaled * normal_rows, axis=-1, keepdims=True)
    )
    return (row_grad, jnp.sum(upstream * normal_rows, axis=0), jnp.sum(upstream, axis=0))


def allowed_mask(first_row, row_total, key_total, seq_length, block_size):
    row_pos = first_row + lax.broadcasted_iota(jnp.int32, (row_total, key_total), 0)
    key_pos = lax.broadcasted_iota(jnp.int32, (row_total, key_total), 1)
    return (key_pos // block_size <= row_pos // block_size) & (key_pos < seq_length)


def attend(query_rows, key_rows, value_rows, seq_length, block_size):
    row_total, local_heads, head_size = query_rows.shape
    block_rows = min(512, row_total)
    block_count = row_total // block_rows
    query_blocks = query_rows.reshape(block_count, block_rows, local_heads, head_size)

    def one_block(block_pair):
        block_index, query_block = block_pair
        scores = jnp.einsum(
            "qhd,khd->hqk", query_block, key_rows, preferred_element_type=jnp.float32
        )
        allowed = allowed_mask(
            block_index * block_rows, block_rows, row_total, seq_length, block_size
        )
        scores = jnp.where(allowed[None], scores, masked_score)
        top_score = jnp.max(scores, axis=-1, keepdims=True)
        exp_scores = jnp.exp(scores - top_score)
        exp_total = jnp.sum(exp_scores, axis=-1, keepdims=True)
        probabilities = (exp_scores / exp_total).astype(jnp.bfloat16)
        context = jnp.einsum(
            "hqk,khd->qhd", probabilities, value_rows, preferred_element_type=jnp.float32
        )
        return (context.astype(jnp.bfloat16), top_score[..., 0] + jnp.log(exp_total[..., 0]))

    contexts, log_sums = lax.map(
        one_block, (jnp.arange(block_count, dtype=jnp.int32), query_blocks)
    )
    return (contexts.reshape(row_total, local_heads * head_size), log_sums)


def attend_back(query_rows, key_rows, value_rows, context_grad, log_sums, seq_length, block_size):
    row_total, local_heads, head_size = query_rows.shape
    block_rows = min(512, row_total)
    block_count = row_total // block_rows
    query_blocks = query_rows.reshape(block_count, block_rows, local_heads, head_size)
    grad_blocks = context_grad.reshape(block_count, block_rows, local_heads, head_size)

    def one_block(running, block_pack):
        key_grad, value_grad = running
        block_index, query_block, grad_block, log_block = block_pack
        scores = jnp.einsum(
            "qhd,khd->hqk", query_block, key_rows, preferred_element_type=jnp.float32
        )
        allowed = allowed_mask(
            block_index * block_rows, block_rows, row_total, seq_length, block_size
        )
        probabilities = jnp.where(allowed[None], jnp.exp(scores - log_block[..., None]), 0.0)
        prob_grad = jnp.einsum(
            "qhd,khd->hqk", grad_block, value_rows, preferred_element_type=jnp.float32
        )
        row_dot = jnp.sum(prob_grad * probabilities, axis=-1, keepdims=True)
        score_grad = (probabilities * (prob_grad - row_dot)).astype(jnp.bfloat16)
        query_grad = jnp.einsum(
            "hqk,khd->qhd", score_grad, key_rows, preferred_element_type=jnp.float32
        )
        key_grad = key_grad + jnp.einsum(
            "hqk,qhd->khd", score_grad, query_block, preferred_element_type=jnp.float32
        )
        value_grad = value_grad + jnp.einsum(
            "hqk,qhd->khd",
            probabilities.astype(jnp.bfloat16),
            grad_block,
            preferred_element_type=jnp.float32,
        )
        return ((key_grad, value_grad), query_grad)

    empty = jnp.zeros((row_total, local_heads, head_size), jnp.float32)
    (key_grad, value_grad), query_grads = lax.scan(
        one_block,
        (empty, empty),
        (jnp.arange(block_count, dtype=jnp.int32), query_blocks, grad_blocks, log_sums),
    )
    width = local_heads * head_size
    return (
        query_grads.reshape(row_total, width),
        key_grad.reshape(row_total, width),
        value_grad.reshape(row_total, width),
    )


def on_device_plain(
    tokens,
    seq_lens,
    block_sizes,
    w_query,
    b_query,
    w_key,
    w_value,
    b_value,
    w_out,
    b_out,
    gain_one,
    shift_one,
    w_up,
    b_up,
    w_down,
    b_down,
    gain_two,
    shift_two,
    cotangent,
):
    micro_total = seq_lens.shape[0]
    seq_rows = tokens.shape[0] // micro_total
    head_cols = w_query.shape[1]
    local_heads = head_cols // HEAD
    model_width = tokens.shape[1]
    own_cols = model_width // lax.axis_size("tensor")
    column_start = lax.axis_index("tensor") * own_cols
    query_bias = b_query.astype(jnp.float32)
    value_bias = b_value.astype(jnp.float32)
    up_bias = b_up.astype(jnp.float32)
    owned = (
        w_query,
        w_key,
        w_value,
        w_out,
        w_up,
        w_down,
        b_out,
        gain_one,
        shift_one,
        b_down,
        gain_two,
        shift_two,
    )

    def shaped(flat_rows):
        return flat_rows.reshape(seq_rows, local_heads, HEAD)

    layer_outputs = []
    input_grads = []
    totals = None
    for micro_index in range(micro_total):
        rows_in = tokens[micro_index * seq_rows : (micro_index + 1) * seq_rows]
        upstream = cotangent[micro_index * seq_rows : (micro_index + 1) * seq_rows].astype(
            jnp.float32
        )
        seq_length = seq_lens[micro_index]
        block_size = block_sizes[micro_index]
        forward_set = (
            lax.all_gather(owned[0], "dp", axis=0, tiled=True),
            lax.all_gather(owned[1], "dp", axis=0, tiled=True),
            lax.all_gather(owned[2], "dp", axis=0, tiled=True),
            lax.all_gather(owned[3], "dp", axis=1, tiled=True),
            lax.all_gather(owned[4], "dp", axis=0, tiled=True),
            lax.all_gather(owned[5], "dp", axis=1, tiled=True),
            lax.all_gather(owned[6], "dp", axis=0, tiled=True),
            lax.all_gather(owned[7], "dp", axis=0, tiled=True),
            lax.all_gather(owned[8], "dp", axis=0, tiled=True),
            lax.all_gather(owned[9], "dp", axis=0, tiled=True),
            lax.all_gather(owned[10], "dp", axis=0, tiled=True),
            lax.all_gather(owned[11], "dp", axis=0, tiled=True),
        )
        (
            full_query,
            full_key,
            full_value,
            full_out,
            full_up,
            full_down,
            full_out_bias,
            full_gain_one,
            full_shift_one,
            full_down_bias,
            full_gain_two,
            full_shift_two,
        ) = forward_set
        out_bias = full_out_bias.astype(jnp.float32)
        down_bias = full_down_bias.astype(jnp.float32)
        first_gain = full_gain_one.astype(jnp.float32)
        first_shift = full_shift_one.astype(jnp.float32)
        second_gain = full_gain_two.astype(jnp.float32)
        second_shift = full_shift_two.astype(jnp.float32)
        query_rows = ((matmul(rows_in, full_query) + query_bias) * 0.125).astype(jnp.bfloat16)
        key_rows = matmul(rows_in, full_key).astype(jnp.bfloat16)
        value_rows = (matmul(rows_in, full_value) + value_bias).astype(jnp.bfloat16)
        context, log_sums = attend(
            shaped(query_rows), shaped(key_rows), shaped(value_rows), seq_length, block_size
        )
        attended = lax.psum(matmul(context, full_out), "tensor") + out_bias
        first_norm, first_hat, first_scale = norm_forward(
            rows_in.astype(jnp.float32) + attended, first_gain, first_shift
        )
        normed = first_norm.astype(jnp.bfloat16)
        expanded = matmul(normed, full_up) + up_bias
        normal_cdf = 0.5 * (1.0 + lax.erf(expanded * inv_root_two))
        hidden = (expanded * normal_cdf).astype(jnp.bfloat16)
        lowered = lax.psum(matmul(hidden, full_down), "tensor") + down_bias
        second_norm, second_hat, second_scale = norm_forward(
            normed.astype(jnp.float32) + lowered, second_gain, second_shift
        )
        layer_outputs.append(second_norm.astype(jnp.bfloat16))
        second_grad, grad_gain_two, grad_shift_two = norm_backward(
            upstream, second_hat, second_scale, second_gain
        )
        down_bias_grad = jnp.sum(second_grad, axis=0)
        second_low = second_grad.astype(jnp.bfloat16)
        down_grad = contract_rows(hidden, second_low)
        hidden_grad = contract_cols(second_low, full_down)
        expanded_grad = hidden_grad * (
            normal_cdf + expanded * jnp.exp(-0.5 * expanded * expanded) * inv_root_tau
        )
        up_bias_grad = jnp.sum(expanded_grad, axis=0)
        expanded_low = expanded_grad.astype(jnp.bfloat16)
        up_grad = contract_rows(normed, expanded_low)
        normed_grad = lax.psum(contract_cols(expanded_low, full_up), "tensor") + second_grad
        first_grad, grad_gain_one, grad_shift_one = norm_backward(
            normed_grad, first_hat, first_scale, first_gain
        )
        out_bias_grad = jnp.sum(first_grad, axis=0)
        first_low = first_grad.astype(jnp.bfloat16)
        out_grad = contract_rows(context, first_low)
        context_grad = contract_cols(first_low, full_out).astype(jnp.bfloat16)
        query_grad, key_grad, value_grad = attend_back(
            shaped(query_rows),
            shaped(key_rows),
            shaped(value_rows),
            shaped(context_grad),
            log_sums,
            seq_length,
            block_size,
        )
        query_grad = query_grad * 0.125
        query_bias_grad = jnp.sum(query_grad, axis=0)
        value_bias_grad = jnp.sum(value_grad, axis=0)
        query_low = query_grad.astype(jnp.bfloat16)
        key_low = key_grad.astype(jnp.bfloat16)
        value_low = value_grad.astype(jnp.bfloat16)
        query_w_grad = contract_rows(rows_in, query_low)
        key_w_grad = contract_rows(rows_in, key_low)
        value_w_grad = contract_rows(rows_in, value_low)
        input_term = (
            contract_cols(query_low, full_query)
            + contract_cols(key_low, full_key)
            + contract_cols(value_low, full_value)
        )
        own_grad = lax.psum_scatter(
            input_term.astype(jnp.bfloat16), "tensor", scatter_dimension=1, tiled=True
        ).astype(jnp.float32)
        input_grads.append(
            own_grad + lax.dynamic_slice_in_dim(first_grad, column_start, own_cols, 1)
        )
        terms = (
            query_w_grad,
            query_bias_grad,
            key_w_grad,
            value_w_grad,
            value_bias_grad,
            out_grad,
            out_bias_grad,
            grad_gain_one,
            grad_shift_one,
            up_grad,
            up_bias_grad,
            down_grad,
            down_bias_grad,
            grad_gain_two,
            grad_shift_two,
        )
        if totals is None:
            totals = terms
        else:
            totals = tuple((running + addend for running, addend in zip(totals, terms)))
    summed = (
        lax.psum_scatter(totals[0], "dp", scatter_dimension=0, tiled=True),
        lax.psum_scatter(totals[2], "dp", scatter_dimension=0, tiled=True),
        lax.psum_scatter(totals[3], "dp", scatter_dimension=0, tiled=True),
        lax.psum_scatter(totals[5], "dp", scatter_dimension=1, tiled=True),
        lax.psum_scatter(totals[9], "dp", scatter_dimension=0, tiled=True),
        lax.psum_scatter(totals[11], "dp", scatter_dimension=1, tiled=True),
        lax.psum_scatter(totals[6], "dp", scatter_dimension=0, tiled=True),
        lax.psum_scatter(totals[7], "dp", scatter_dimension=0, tiled=True),
        lax.psum_scatter(totals[8], "dp", scatter_dimension=0, tiled=True),
        lax.psum_scatter(totals[12], "dp", scatter_dimension=0, tiled=True),
        lax.psum_scatter(totals[13], "dp", scatter_dimension=0, tiled=True),
        lax.psum_scatter(totals[14], "dp", scatter_dimension=0, tiled=True),
    )
    bias_sums = lax.psum((totals[1], totals[4], totals[10]), "dp")
    return (
        jnp.concatenate(layer_outputs, 0),
        jnp.concatenate(input_grads, 0),
        summed[0],
        bias_sums[0],
        summed[1],
        summed[2],
        bias_sums[1],
        summed[3],
        summed[6],
        summed[7],
        summed[8],
        summed[4],
        bias_sums[2],
        summed[5],
        summed[9],
        summed[10],
        summed[11],
    )


def place():
    dp = lax.axis_index("dp")
    tensor = lax.axis_index("tensor")
    return dp // 2, dp % 2, tensor // 2, tensor % 2

def device(z, x, y, core):
    return (z * 2 + x, y * 2 + core)

def greet(lines, all_along=False):
    z, x, y, core = place()
    barrier = pltpu.get_barrier_semaphore()

    def signal(target):
        pl.semaphore_signal(barrier, inc=1, device_id=target, device_id_type=MESH)

    signal(device(z, 1 - x, y, core))
    signal(device(z, x, 1 - y, core))
    signal(device(z, x, y, 1 - core))
    for k in range(1, lines if all_along else 2):
        pl.when(z >= k)(lambda: signal(device(z - k, x, y, core)))
        pl.when(z + k < lines)(lambda: signal(device(z + k, x, y, core)))
    if all_along:
        ends = lines - 1
    else:
        ends = jnp.where(z > 0, 1, 0) + jnp.where(z < lines - 1, 1, 0)
    pl.semaphore_wait(barrier, 3 + ends)


class Gather:
    def __init__(self, lines, whole, recv_sem, send_sem, rows, corner=None):
        self.lines, self.whole, self.recv_sem, self.send_sem, self.rows = lines, whole, recv_sem, send_sem, rows
        self.corner = corner
        self.here = place()
        self.sent = []

    def view(self, z, x, y):
        start = (z * 2 + x) * self.rows
        if not isinstance(start, int):
            start = pl.multiple_of(start, self.rows)
        return self.whole.at[y, pl.ds(start, self.rows)]

    def copy(self, z, x, y, way):
        mz, mx, my, core = self.here
        target = {"up": (mz + 1, mx, my), "down": (mz - 1, mx, my), "x": (mz, 1 - mx, my), "y": (mz, mx, 1 - my)}[way]
        index = y * self.lines * 2 + z * 2 + x
        return pltpu.make_async_remote_copy(
            src_ref=self.view(z, x, y), dst_ref=self.view(z, x, y),
            send_sem=self.send_sem.at[("up", "down", "x", "y").index(way), index],
            recv_sem=self.recv_sem.at[index],
            device_id=device(*target, core), device_id_type=MESH)

    def send(self, z, x, y, way, ok=None):
        if ok is None:
            self.copy(z, x, y, way).start()
        else:
            @pl.when(ok)
            def _():
                self.copy(z, x, y, way).start()
        self.sent.append((z, x, y, way, ok))

    def take(self, z, x, y):
        self.copy(z, x, y, "x").wait_recv()

    def begin(self):
        z, x, y, core = self.here
        self.send(z, x, y, "x")
        self.send(z, x, y, "y")
        self.send(z, x, y, "up", z < self.lines - 1)
        self.send(z, x, y, "down", z > 0)

    def planes(self, k):
        z, x, y, core = self.here
        for zz, ok in (((z, None),) if k == 0 else ((z - k, z - k >= 0), (z + k, z + k < self.lines))):
            def arrive(zz=zz):
                self.take(zz, 1 - x, y)
                self.take(zz, x, 1 - y)
            if ok is None:
                arrive()
            else:
                pl.when(ok)(arrive)
            if self.corner is not None:
                if k == 0 and self.corner == "y":
                    self.send(zz, 1 - x, y, "y")
                if k == 0 and self.corner == "x":
                    self.send(zz, x, 1 - y, "x")
                continue
            even = zz % 2 == 0
            odd = zz % 2 == 1
            if ok is not None:
                even, odd = even & ok, odd & ok
            self.send(zz, 1 - x, y, "y", odd)
            self.send(zz, x, 1 - y, "x", even)

    def round(self, k):
        z, x, y, core = self.here
        if k < self.lines:
            for zz, ok, on, way in ((z - k, z - k >= 0, z < self.lines - 1, "up"), (z + k, z + k < self.lines, z > 0, "down")):
                pl.when(ok)(functools.partial(self.take, zz, x, y))
                self.send(zz, x, y, way, ok & on)
                self.send(zz, x, y, "x", ok)
                self.send(zz, x, y, "y", ok)
        self.planes(k - 1)

    def corners(self, k):
        z, x, y, core = self.here
        if k == 0:
            self.take(z, 1 - x, 1 - y)
            self.send(z, 1 - x, 1 - y, "up", z < self.lines - 1)
            self.send(z, 1 - x, 1 - y, "down", z > 0)
            return
        for zz, ok, on, way in ((z - k, z - k >= 0, z < self.lines - 1, "up"), (z + k, z + k < self.lines, z > 0, "down")):
            pl.when(ok)(functools.partial(self.take, zz, 1 - x, 1 - y))
            self.send(zz, 1 - x, 1 - y, way, ok & on)

    def last(self):
        z, x, y, core = self.here
        if self.corner is None:
            for zz in range(self.lines):
                self.take(zz, 1 - x, 1 - y)

    def drain(self):
        for z, x, y, way, ok in self.sent:
            if ok is None:
                self.copy(z, x, y, way).wait_send()
            else:
                pl.when(ok)(lambda: self.copy(z, x, y, way).wait_send())


lanes = 128
block = 256


def dot(first, second, dims):
    return lax.dot_general(first, second, ((dims[:1], dims[1:]), ((), ())), preferred_element_type=jnp.float32)


plain, right_turned, left_turned = (1, 0), (1, 1), (0, 0)


def rows_at(start, size):
    return pl.ds(pl.multiple_of(start, size), size)


def low_half(rows):
    return lax.broadcasted_iota(jnp.int32, (rows, lanes), 1) < HEAD


def tile(index):
    return slice(index * lanes, (index + 1) * lanes)


def swapped(values):
    return pltpu.roll(values, HEAD, 1)


def each(count, body):
    lax.fori_loop(0, count, lambda index, carry: (body(index), carry)[1], 0)


def norm_rows(values):
    centred = values - jnp.mean(values, axis=-1, keepdims=True)
    variance = jnp.mean(centred * centred, axis=-1, keepdims=True)
    scale = lax.rsqrt(variance + norm_epsilon)
    return centred * scale, scale


def norm_rows_back(upstream, hat, scale, gain):
    scaled = upstream * gain
    return scale * (scaled - jnp.mean(scaled, axis=-1, keepdims=True) - hat * jnp.mean(scaled * hat, axis=-1, keepdims=True))


def total_rows(values):
    return jnp.sum(values, axis=0, keepdims=True)


def swap_copy(src, dst, sems, index, near):
    z, x, y, core = place()
    target = device(z, x, y, 1 - core) if near else device(z, x, 1 - y, core)
    return pltpu.make_async_remote_copy(
        src_ref=src, dst_ref=dst, send_sem=sems.at[0, index], recv_sem=sems.at[1, index],
        device_id=target, device_id_type=MESH)


class Scatter:
    def __init__(self, lines, terms, slots, recv_sem, send_sem, rows, corner=None):
        self.corner = corner
        self.lines, self.terms, self.slots = lines, terms, slots
        self.recv_sem, self.send_sem, self.rows = recv_sem, send_sem, rows
        self.here = place()
        self.sent = []
        self.order = [z for pair in zip(range(lines // 2), reversed(range(lines // 2, lines))) for z in reversed(pair)]

    def view(self, z, x, y):
        return self.terms.at[y, rows_at((z * 2 + x) * self.rows, self.rows)]

    def copy(self, z, x, y, way, kind):
        mz, mx, my, core = self.here
        target = {"up": (mz + 1, mx, my), "down": (mz - 1, mx, my), "x": (mz, 1 - mx, my), "y": (mz, mx, 1 - my)}[way]
        return pltpu.make_async_remote_copy(
            src_ref=self.view(z, x, y), dst_ref=self.slots.at[kind, z],
            send_sem=self.send_sem.at[kind, z], recv_sem=self.recv_sem.at[kind, z],
            device_id=device(*target, core), device_id_type=MESH)

    def send(self, z, x, y, way, kind, ok=None):
        if ok is None:
            self.copy(z, x, y, way, kind).start()
        else:
            pl.when(ok)(lambda: self.copy(z, x, y, way, kind).start())
        self.sent.append((z, x, y, way, kind, ok))

    def taken(self, z, x, y, kind):
        self.copy(z, x, y, "x", kind).wait_recv()
        return self.slots[kind, z].astype(jnp.float32)

    def add(self, z, x, y, *kinds):
        start = rows_at((z * 2 + x) * self.rows, self.rows)
        result = self.terms[y, start].astype(jnp.float32)
        for kind in kinds:
            result = result + self.taken(z, x, y, kind)
        self.terms[y, start] = result.astype(jnp.bfloat16)

    def begin(self):
        z, x, y, core = self.here
        if self.corner is not None:
            self.opposite(self.lines - 1)
            for k in range(self.lines - 1, 0, -1):
                for zz, ok in ((z + k, z + k < self.lines), (z - k, z - k >= 0)):
                    self.send(zz, 1 - x, y, "x", 1, ok)
                    self.send(zz, x, 1 - y, "y", 2, ok)
            if self.corner == "x":
                self.send(z, 1 - x, y, "x", 1)
            else:
                self.send(z, x, 1 - y, "y", 2)
            return
        for zz in self.order:
            self.send(zz, 1 - x, 1 - y, "x" if zz % 2 == 0 else "y", 0)
        for zz in self.order:
            if zz % 2:
                self.send(zz, x, 1 - y, "y", 2)
            else:
                self.send(zz, 1 - x, y, "x", 1)

    def opposite(self, k):
        z, x, y, core = self.here
        if k == 0:
            pl.when(z > 0)(lambda: self.add(z, 1 - x, 1 - y, 5))
            pl.when(z < self.lines - 1)(lambda: self.add(z, 1 - x, 1 - y, 6))
            self.send(z, 1 - x, 1 - y, self.corner, 0)
            return
        for zz, ok, on, way, kind in ((z + k, z + k < self.lines, z > 0, "up", 5), (z - k, z - k >= 0, z < self.lines - 1, "down", 6)):
            pl.when(ok & on)(lambda: self.add(zz, 1 - x, 1 - y, kind))
            self.send(zz, 1 - x, 1 - y, way, kind, ok)

    def corners(self):
        z, x, y, core = self.here
        if self.corner == "x":
            self.add(z, x, 1 - y, 0)
            self.send(z, x, 1 - y, "y", 2)
            return
        if self.corner == "y":
            self.add(z, 1 - x, y, 0)
            self.send(z, 1 - x, y, "x", 1)
            return
        for zz in self.order:
            if zz % 2 == 0:
                self.add(zz, x, 1 - y, 0)
                self.send(zz, x, 1 - y, "y", 2)
            else:
                self.add(zz, 1 - x, y, 0)
                self.send(zz, 1 - x, y, "x", 1)

    def line(self, k):
        z, x, y, core = self.here
        for zz, ok, on, way, kind in ((z + k, z + k < self.lines, z > 0, "up", 3), (z - k, z - k >= 0, z < self.lines - 1, "down", 4)):
            pl.when(ok & on)(lambda: self.add(zz, x, y, 1, 2, kind))
            pl.when(ok & jnp.logical_not(on))(lambda: self.add(zz, x, y, 1, 2))
            self.send(zz, x, y, way, kind, ok)

    def own(self, target):
        z, x, y, core = self.here
        start = rows_at((z * 2 + x) * self.rows, self.rows)
        target[...] = self.terms[y, start].astype(jnp.float32) + self.taken(z, x, y, 1) + self.taken(z, x, y, 2)

        def more(kind):
            target[...] += self.taken(z, x, y, kind)

        pl.when(z > 0)(lambda: more(3))
        pl.when(z < self.lines - 1)(lambda: more(4))

    def drain(self):
        for z, x, y, way, kind, ok in self.sent:
            if ok is None:
                self.copy(z, x, y, way, kind).wait_send()
            else:
                pl.when(ok)(lambda: self.copy(z, x, y, way, kind).wait_send())


def pack_weights(y, own, unit, w_query, w_key, w_value, w_out, w_up, w_down, weights):
    here = rows_at(own * unit, unit)
    for which, array in enumerate((w_query, w_key, w_value)):
        weights[0][y, here, tile(which)] = array[:, 0 : 2 * HEAD]
        single = array[:, 2 * HEAD : 3 * HEAD]
        out = w_out[:, which * HEAD : (which + 1) * HEAD]
        weights[1][y, here, tile(which)] = jnp.where(
            y == 0, jnp.concatenate([single, out], axis=1), jnp.concatenate([out, single], axis=1))
    weights[2][y, here] = w_up[...]
    weights[3][y, here] = w_down[...]


def turn_out(mixed, target):
    low = low_half(mixed.shape[1])
    first = [mixed[0, :, tile(i)].astype(jnp.float32) for i in range(3)]
    second = [mixed[1, :, tile(i)].astype(jnp.float32) for i in range(3)]
    for pair, values in enumerate((
        jnp.where(low, swapped(first[0]), first[1]),
        jnp.where(low, second[0], swapped(second[1])),
        jnp.where(low, swapped(first[2]), swapped(second[2])),
    )):
        target[:, tile(pair)] = values.astype(jnp.bfloat16)


def spread_vectors(lines, unit, extras, vectors):
    width = vectors.shape[1]
    column = lax.broadcasted_iota(jnp.int32, (lanes, width), 1)
    row = lax.broadcasted_iota(jnp.int32, (lanes, width), 0)
    result = jnp.zeros((16, width), jnp.float32)
    for own in range(lines * 2):
        spot = ((column == row + own * unit) & (row < unit)).astype(jnp.bfloat16)
        result = result + dot(extras[0, own * 16 : own * 16 + 16, 0:lanes], spot, plain)
    vectors[...] = result


def key_limit(places, size, length):
    blocks = jnp.floor((places.astype(jnp.float32) + 0.5) / size.astype(jnp.float32)).astype(jnp.int32)
    return jnp.minimum((blocks + 1) * size, length)


def attend_head(head, query, key, value, limit, context, log_sum, keep):
    pair, upper = head // 2, head % 2
    total = query.shape[0]
    chosen = ~keep if upper else keep
    keys = jnp.where(chosen, key[:, tile(pair)], jnp.zeros((), jnp.bfloat16))
    values = value[:, tile(pair)]
    low = low_half(block)
    here = lax.broadcasted_iota(jnp.int32, (block, lanes), 1) == head
    places = lax.broadcasted_iota(jnp.int32, (block, total), 1)

    def one(index):
        rows = rows_at(index * block, block)
        scores = dot(query[rows, tile(pair)], keys, right_turned)
        scores = jnp.where(places < limit[rows], scores, masked_score)
        top = jnp.max(scores, axis=-1, keepdims=True)
        grown = jnp.exp(scores - top)
        sums = jnp.sum(grown, axis=-1, keepdims=True)
        probs = (grown * (1.0 / sums)).astype(jnp.bfloat16)
        result = dot(probs, values, plain).astype(jnp.bfloat16)
        logs = top + jnp.log(sums)
        if upper:
            context[rows, tile(pair)] = jnp.where(low, context[rows, tile(pair)], result)
        else:
            context[rows, tile(pair)] = result
        if head == 0:
            log_sum[rows] = jnp.where(here, logs, 0.0)
        else:
            log_sum[rows] = jnp.where(here, logs, log_sum[rows])

    each(total // block, one)


def back_head(head, query, key, value, context_grad, limit_rows, log_rows, dot_rows, keep, query_acc, key_acc, value_acc):
    pair, upper = head // 2, head % 2
    total = query.shape[0]
    chosen = ~keep if upper else keep
    nothing = jnp.zeros((), jnp.bfloat16)
    keys = jnp.where(chosen, key[:, tile(pair)], nothing)
    values = jnp.where(chosen, value[:, tile(pair)], nothing)
    low = low_half(block)
    low = ~low if upper else low
    places = lax.broadcasted_iota(jnp.int32, (total, block), 0)
    if not upper:
        value_acc[...] = jnp.zeros_like(value_acc)
        key_acc[...] = jnp.zeros_like(key_acc)

    def one(index):
        rows = rows_at(index * block, block)
        asked = query[rows, tile(pair)]
        wanted = context_grad[rows, tile(pair)]
        scores = dot(keys, asked, right_turned)
        grown = jnp.exp(scores - log_rows[index, head : head + 1])
        probs = jnp.where(places < limit_rows[index, 0:1], grown, 0.0)
        prob_grad = dot(values, wanted, right_turned)
        score_grad = (probs * (prob_grad - dot_rows[index, head : head + 1])).astype(jnp.bfloat16)
        value_acc[...] += dot(probs.astype(jnp.bfloat16), jnp.where(low, wanted, nothing), plain)
        key_acc[...] += dot(score_grad, jnp.where(low, asked, nothing), plain)
        query_term = dot(score_grad, keys, left_turned)
        if upper:
            query_acc[rows] += query_term
        else:
            query_acc[rows] = query_term

    each(total // block, one)


def layer_kernel(
    lines, tokens_all, cotangent_all, seq_lens, block_sizes,
    w_query, w_key, w_value, w_out, w_up, w_down, extra,
    output, input_own, input_far, grad_one, grad_two, grad_up, grad_down, own_sums,
    tokens, cotangent, w_first, w_second, w_wide, w_long, extras, vectors,
    query, key, value, context, log_sum, limit, limit_rows, log_rows, dot_rows,
    turned, sent, got, hat_one, scale_one, normed, slope, hidden, second_grad, second_low, first_low, context_grad, out_grad, out_rows, far_out,
    query_acc, key_acc, value_acc, terms_first, terms_second, slots_narrow, slots_wide,
    sums, vec_got, line_got, turn_sent, turn_got, far_sent,
    local, gather_recv, gather_send, extra_recv, extra_send, scatter_recv, scatter_send, sems,
):
    z, x, y, core = place()
    own = z * 2 + x
    total, width = tokens.shape
    half = total // 2
    mine, theirs = core * half, (1 - core) * half
    unit = w_query.shape[0]
    blocks = total // block
    weights = (w_first, w_second, w_wide, w_long)

    load_tokens = pltpu.make_async_copy(tokens_all.at[rows_at(y * total, total)], tokens, local.at[0])
    load_tokens.start()
    load_cotangent = pltpu.make_async_copy(cotangent_all.at[rows_at(y * total + mine, half)], cotangent, local.at[1])
    load_cotangent.start()
    pack_weights(y, own, unit, w_query, w_key, w_value, w_out, w_up, w_down, weights)
    extras[y, rows_at(own * 16, 16)] = extra[...]
    greet(lines, True)
    gathers = [
        Gather(lines, weights[part], gather_recv.at[part], gather_send.at[part], unit, corner)
        for part, corner in enumerate((None, None, None, None))]
    small = Gather(lines, extras, extra_recv, extra_send, 16)
    first, second, wide, long = gathers
    small.begin()
    first.begin()
    size, length = block_sizes[y], seq_lens[y]
    limit[...] = key_limit(lax.broadcasted_iota(jnp.int32, (total, 1), 0), size, length)
    for index in range(blocks):
        limit_rows[index] = key_limit(index * block + lax.broadcasted_iota(jnp.int32, (8, block), 1), size, length)
    for step in range(1, lines + 1):
        small.round(step)
        first.round(step)
        if step == 2:
            second.begin()
    load_tokens.wait()
    small.last()
    first.last()
    bias = [extras[near, rows_at(own * 16, 16)].astype(jnp.float32)[0:1] for near in range(2)]
    low = low_half(block)

    def project(index):
        rows = rows_at(index * block, block)
        inputs = tokens[rows]
        for near in range(2):
            found = dot(inputs, w_first[near], plain) + bias[near][:, 0 : 3 * lanes]
            query[rows, tile(near)] = (found[:, tile(0)] * 0.125).astype(jnp.bfloat16)
            key[rows, tile(near)] = found[:, tile(1)].astype(jnp.bfloat16)
            value[rows, tile(near)] = found[:, tile(2)].astype(jnp.bfloat16)

    def project_mixed(index):
        rows = rows_at(index * block, block)
        inputs = tokens[rows]
        found = [dot(inputs, w_second[near], plain) + bias[near][:, 3 * lanes :] for near in range(2)]
        mixed = [jnp.where(low, found[0][:, tile(which)], found[1][:, tile(which)]) for which in range(3)]
        query[rows, tile(2)] = (mixed[0] * 0.125).astype(jnp.bfloat16)
        key[rows, tile(2)] = mixed[1].astype(jnp.bfloat16)
        value[rows, tile(2)] = mixed[2].astype(jnp.bfloat16)

    each(blocks, project)
    keep = low_half(total)

    def attend(head):
        attend_head(head, query, key, value, limit, context, log_sum, keep)

    second.round(1)
    wide.begin()
    second.round(2)
    attend(0)
    second.round(3)
    wide.round(1)
    second.round(4)
    wide.round(2)
    attend(1)
    long.begin()
    second.last()
    wide.round(3)
    attend(2)
    wide.round(4)
    long.round(1)
    attend(3)
    each(blocks, project_mixed)
    long.round(2)
    attend(4)
    long.round(3)
    attend(5)
    long.round(4)
    turn_out(w_second, turned)
    spread_vectors(lines, unit, extras, vectors)
    vector = lambda index: vectors[2 + index : 3 + index]
    up_bias = [extras[near, rows_at(own * 16, 16)].astype(jnp.float32)[1:2] for near in range(2)]
    sums[0] = jnp.zeros_like(sums.at[0])
    count = half // block

    def add_sum(index, values):
        sums[0, index : index + 1] += total_rows(values)

    def away(term, index):
        def body(step):
            sent[rows_at(step * block, block)] = term(rows_at(theirs + step * block, block))

        each(count, body)
        copy = swap_copy(sent, got, sems, index, True)
        copy.start()
        return copy

    def attended(rows):
        return dot(context[rows], turned[...], right_turned)

    copy = away(attended, 0)

    def stay_a(step):
        hat_one[rows_at(step * block, block)] = attended(rows_at(mine + step * block, block))

    each(count, stay_a)
    copy.wait()

    def first_norm(step):
        rows = rows_at(step * block, block)
        full = rows_at(mine + step * block, block)
        values = tokens[full].astype(jnp.float32) + ((hat_one[rows] + got[rows]) + vector(0))
        hat, scale = norm_rows(values)
        hat_one[rows] = hat
        scale_one[rows] = jnp.broadcast_to(scale, (block, lanes))
        normed[full] = (hat * vector(1) + vector(2)).astype(jnp.bfloat16)

    each(count, first_norm)
    copy_n = swap_copy(normed.at[rows_at(mine, half)], normed.at[rows_at(mine, half)], sems, 3, True)
    copy_n.start()
    wide.last()

    def expand(base):
        def body(step):
            rows = rows_at(base + step * block, block)
            inputs = normed[rows]
            for near in range(2):
                columns = slice(near * width, (near + 1) * width)
                expanded = dot(inputs, w_wide[near], plain) + up_bias[near]
                cdf = 0.5 * (1.0 + lax.erf(expanded * inv_root_two))
                hidden[rows, columns] = (expanded * cdf).astype(jnp.bfloat16)
                slope[rows, columns] = (cdf + expanded * jnp.exp(-0.5 * expanded * expanded) * inv_root_tau).astype(jnp.bfloat16)

        each(count, body)

    expand(mine)
    copy_n.wait()
    expand(theirs)
    long.last()
    for gather in gathers:
        gather.drain()
    small.drain()

    def lowered(rows):
        return dot(hidden[rows, 0:width], w_long[0], right_turned) + dot(hidden[rows, width : 2 * width], w_long[1], right_turned)

    copy = away(lowered, 1)

    def stay_b(step):
        second_grad[rows_at(step * block, block)] = lowered(rows_at(mine + step * block, block))

    each(count, stay_b)
    copy.wait()
    load_cotangent.wait()

    def second_norm(step):
        rows = rows_at(step * block, block)
        full = rows_at(mine + step * block, block)
        values = normed[full].astype(jnp.float32) + ((second_grad[rows] + got[rows]) + vector(3))
        hat, scale = norm_rows(values)
        out_rows[rows] = (hat * vector(4) + vector(5)).astype(jnp.bfloat16)
        upstream = cotangent[rows].astype(jnp.float32)
        grad = norm_rows_back(upstream, hat, scale, vector(4))
        second_grad[rows] = grad
        second_low[full] = grad.astype(jnp.bfloat16)
        add_sum(3, grad)
        add_sum(4, upstream * hat)
        add_sum(5, upstream)

    each(count, second_norm)
    copy_s = swap_copy(second_low.at[rows_at(mine, half)], second_low.at[rows_at(mine, half)], sems, 4, True)
    copy_s.start()
    near_rows = output.at[rows_at(y * total + mine, half)]
    store_out = pltpu.make_async_copy(out_rows, near_rows, local.at[2])
    store_out.start()
    copy_o = swap_copy(out_rows, near_rows, sems, 5, True)
    copy_o.start()
    copy_p = swap_copy(out_rows, far_out, sems, 6, False)
    copy_p.start()

    def contract(base):
        def body(step):
            rows = rows_at(base + step * block, block)
            inputs = second_low[rows]
            for near in range(2):
                columns = slice(near * width, (near + 1) * width)
                grad = dot(inputs, w_long[near], plain) * slope[rows, columns].astype(jnp.float32)
                add_sum(8 + near, grad)
                slope[rows, columns] = grad.astype(jnp.bfloat16)

        each(count, body)

    contract(mine)
    copy_s.wait()
    contract(theirs)
    expanded_low = slope

    def normed_term(rows):
        return dot(expanded_low[rows, 0:width], w_wide[0], right_turned) + dot(expanded_low[rows, width : 2 * width], w_wide[1], right_turned)

    copy = away(normed_term, 2)

    def stay_c(step):
        rows = rows_at(step * block, block)
        second_grad[rows] = second_grad[rows] + normed_term(rows_at(mine + step * block, block))

    each(count, stay_c)

    def weight_terms(left, right, target):
        def body(step):
            rows = rows_at(step * block, block)
            for near in range(2):
                target[near, rows] = dot(left[:, rows], right[:, near * width : (near + 1) * width], left_turned).astype(jnp.bfloat16)

        each(width // block, body)

    weight_terms(second_low, hidden, w_long)
    scatters = [
        Scatter(lines, terms, slots, scatter_recv.at[part], scatter_send.at[part], unit, corner)
        for part, (terms, slots, corner) in enumerate((
            (terms_first, slots_narrow.at[0], None), (terms_second, slots_narrow.at[1], None),
            (w_wide, slots_wide.at[0], None), (w_long, slots_wide.at[1], None)))]
    first, second, wide, long = scatters
    long.begin()
    copy.wait()

    def first_norm_back(step):
        rows = rows_at(step * block, block)
        full = rows_at(mine + step * block, block)
        upstream = second_grad[rows] + got[rows]
        hat = hat_one[rows]
        grad = norm_rows_back(upstream, hat, scale_one[rows][:, 0:1], vector(1))
        second_grad[rows] = grad
        first_low[full] = grad.astype(jnp.bfloat16)
        add_sum(0, grad)
        add_sum(1, upstream * hat)
        add_sum(2, upstream)

    each(count, first_norm_back)
    first_grad = second_grad
    copy_f = swap_copy(first_low.at[rows_at(mine, half)], first_low.at[rows_at(mine, half)], sems, 7, True)
    copy_f.start()
    weight_terms(normed, expanded_low, w_wide)
    long.corners()
    wide.begin()
    copy_f.wait()

    def back_out(step):
        rows = rows_at(step * block, block)
        context_grad[rows] = dot(first_low[rows], turned[...], plain).astype(jnp.bfloat16)

    each(blocks, back_out)
    out_grad[...] = dot(first_low[...], context[...], left_turned)

    lane = lax.broadcasted_iota(jnp.int32, (block, lanes), 1)
    for index in range(blocks):
        rows = slice(index * block, (index + 1) * block)
        stats = jnp.zeros((block, lanes), jnp.float32)
        for pair in range(3):
            product = context_grad[rows, tile(pair)].astype(jnp.float32) * context[rows, tile(pair)].astype(jnp.float32)
            lower = jnp.sum(jnp.where(low, product, 0.0), axis=-1, keepdims=True)
            upper = jnp.sum(jnp.where(low, 0.0, product), axis=-1, keepdims=True)
            stats = jnp.where(lane == 2 * pair, lower, jnp.where(lane == 2 * pair + 1, upper, stats))
        dot_rows[index] = stats.T[0:8]
        log_rows[index] = log_sum[rows].T[0:8]
    packed = hidden

    def columns_of(part, near):
        return slice((2 * near + part) * 3 * lanes, (2 * near + part + 1) * 3 * lanes)

    def back(head):
        back_head(head, query, key, value, context_grad, limit_rows, log_rows, dot_rows, keep, query_acc, key_acc, value_acc)

    query_sums, value_sums = [], []

    def place_pair(pair):
        def body(index, carry):
            rows = rows_at(index * block, block)
            asked = query_acc[rows] * 0.125
            valued = value_acc[rows]
            for which, values in enumerate((asked, key_acc[rows], valued)):
                if pair < 2:
                    packed[rows, pl.ds(2 * pair * 3 * lanes + which * lanes, lanes)] = values.astype(jnp.bfloat16)
                else:
                    packed[rows, pl.ds(3 * lanes + which * lanes, lanes)] = jnp.where(low, values, 0.0).astype(jnp.bfloat16)
                    packed[rows, pl.ds(9 * lanes + which * lanes, lanes)] = jnp.where(low, 0.0, values).astype(jnp.bfloat16)
            return carry[0] + total_rows(asked), carry[1] + total_rows(valued)

        empty = jnp.zeros((1, lanes), jnp.float32)
        asked_sum, valued_sum = lax.fori_loop(0, blocks, body, (empty, empty))
        query_sums.append(asked_sum)
        value_sums.append(valued_sum)

    outs = [out_grad[:, tile(pair)] for pair in range(3)]
    homes = (
        (swapped(outs[0]), outs[0], swapped(outs[2])),
        (outs[1], swapped(outs[1]), swapped(outs[2])),
    )
    low_wide = low_half(width)

    def first_terms(near):
        terms_first[near] = dot(tokens[...], packed[:, columns_of(0, near)], left_turned).astype(jnp.bfloat16)

    def second_terms(near):
        grads = dot(tokens[...], packed[:, columns_of(1, near)], left_turned)
        for which in range(3):
            values, home = grads[:, tile(which)], homes[near][which]
            values = jnp.where(low_wide, values, home) if near == 0 else jnp.where(low_wide, home, values)
            terms_second[near, :, tile(which)] = values.astype(jnp.bfloat16)

    long.line(3)
    back(0)
    long.line(2)
    wide.corners()
    back(1)
    place_pair(0)
    first_terms(0)
    long.line(1)
    wide.line(3)
    back(2)
    copy_p.wait()
    far_rows = output.at[rows_at((1 - y) * total + mine, half)]
    copy_q = swap_copy(far_out, far_rows, sems, 8, True)
    copy_q.start()
    store_far = pltpu.make_async_copy(far_out, far_rows, local.at[1])
    store_far.start()
    long.own(grad_down)
    wide.line(2)
    back(3)
    place_pair(1)
    first_terms(1)
    first.begin()
    wide.line(1)
    back(4)
    wide.own(grad_up)
    first.corners()
    back(5)
    place_pair(2)
    second_terms(0)
    second_terms(1)
    second.begin()
    first.line(3)
    narrow = width // 4

    def columns(near, which, rows):
        spot = rows_at((2 * near + which) * narrow, narrow)
        result = dot(packed[rows, columns_of(0, 0)], w_first[0, spot], right_turned)
        result = result + dot(packed[rows, columns_of(1, 0)], w_second[0, spot], right_turned)
        result = result + dot(packed[rows, columns_of(0, 1)], w_first[1, spot], right_turned)
        return result + dot(packed[rows, columns_of(1, 1)], w_second[1, spot], right_turned)

    def pick(values, near, which):
        pieces = [values[:, i * narrow : (i + 1) * narrow] for i in range(4)]
        found = [jnp.where(which == 0, pieces[2 * i], pieces[2 * i + 1]) for i in range(2)]
        return found[near] if isinstance(near, int) else jnp.where(near == 0, found[0], found[1])

    def across(index):
        for near in range(2):
            rows = rows_at(mine + index * block, block)
            term = pick(first_grad[rows_at(index * block, block)], near, 1 - core)
            turn_sent[near, rows] = (columns(near, 1 - core, rows) + term).astype(jnp.bfloat16)
            rows = rows_at(theirs + index * block, block)
            turn_sent[near, rows] = columns(near, 1 - core, rows).astype(jnp.bfloat16)

    each(count, across)
    copy_t = swap_copy(turn_sent, turn_got, sems, 9, True)
    copy_t.start()
    second.corners()
    first.line(2)
    copy_t.wait()

    def finish(near, rows, step):
        values = columns(near, core, rows) + turn_got[near, rows].astype(jnp.float32)
        return values if step is None else values + pick(first_grad[rows_at(step * block, block)], near, core)

    def far(index):
        for base, step in ((mine, index), (theirs, None)):
            rows = rows_at(base + index * block, block)
            far_sent[:, rows] = finish(1 - y, rows, step).T.astype(jnp.bfloat16)

    each(count, far)
    copy_u = swap_copy(far_sent, input_far, sems, 10, False)
    copy_u.start()
    first.line(1)
    second.line(3)

    nothing = jnp.zeros((1, lanes), jnp.float32)
    for near in range(2):
        sums[0, 6 + near : 7 + near] = jnp.concatenate(
            [query_sums[near], nothing, value_sums[near], query_sums[2], nothing, value_sums[2]], axis=1)

    def vector_step(step, target):
        copy = pltpu.make_async_remote_copy(
            src_ref=sums.at[step], dst_ref=vec_got.at[step], send_sem=sems.at[0, 11 + step], recv_sem=sems.at[1, 11 + step],
            device_id=target, device_id_type=MESH)
        copy.start()
        return copy

    copy = vector_step(0, device(z, x, y, 1 - core))

    def close(index):
        for base, step in ((mine, index), (theirs, None)):
            rows = rows_at(base + index * block, block)
            input_own[:, rows] = finish(y, rows, step).T

    each(count, close)
    copy.wait()
    shared = lax.broadcasted_iota(jnp.int32, vec_got.shape[1:], 0) < 6
    sums[1] = sums[0] + jnp.where(shared, vec_got[0], 0.0)
    copy = vector_step(1, device(z, 1 - x, y, core))
    second.line(2)
    first.own(grad_one)
    copy.wait()
    sums[2] = sums[1] + vec_got[1]
    copy = vector_step(2, device(z, x, 1 - y, core))
    second.line(1)
    copy.wait()
    line_got[z] = sums[2] + vec_got[2]

    def line_copy(there, arrives):
        return pltpu.make_async_remote_copy(
            src_ref=line_got.at[z], dst_ref=line_got.at[arrives], send_sem=sems.at[0, 16 + there], recv_sem=sems.at[1, 16 + arrives],
            device_id=device(there, x, y, core), device_id_type=MESH)

    others = [(there, ok) for k in range(1, lines) for there, ok in ((z + k, z + k < lines), (z - k, z - k >= 0))]
    for there, ok in others:
        pl.when(ok)(lambda: line_copy(there, z).start())
    second.own(grad_two)
    for there, ok in others:
        pl.when(ok)(lambda: line_copy(there, there).wait())
    result = line_got[0]
    for line in range(1, lines):
        result = result + line_got[line]
    own_sums[...] = result
    store_out.wait()
    store_far.wait()
    for copy in (copy_o, copy_q, copy_u):
        copy.wait()
    for scatter in scatters:
        scatter.drain()


def close_kernel(
    unit, output_in, input_own, input_far, grad_one, grad_two, grad_up, grad_down, own_sums,
    output, input_grad, g_query, g_key, g_value, g_out, g_up, g_down, gb_query, gb_value, gb_up, *rest,
):
    vector_grads, (staged, sem) = rest[:-2], rest[-2:]
    z, x, y, core = place()
    own = lax.axis_index("dp")
    total = input_own.shape[1]
    half = total // 2
    loads = [pltpu.make_async_copy(output_in.at[i * half : (i + 1) * half], staged.at[i], sem.at[i]) for i in range(4)]
    stores = [pltpu.make_async_copy(staged.at[i], output.at[i * half : (i + 1) * half], sem.at[4 + i]) for i in range(4)]
    for copy in loads:
        copy.start()
    input_grad[:, rows_at(y * total, total)] = input_own[...]
    input_grad[:, rows_at((1 - y) * total, total)] = input_far[...].astype(jnp.float32)

    for load, store in zip(loads, stores):
        load.wait()
        store.start()

    def third(values, which):
        start = which * 2 * HEAD
        return jnp.where(y == 0, values[:, start : start + HEAD], values[:, start + HEAD : start + 2 * HEAD])

    def free(values, which):
        start = which * 2 * HEAD
        return jnp.where(y == 0, values[:, start + HEAD : start + 2 * HEAD], values[:, start : start + HEAD])

    one, two = grad_one[...], grad_two[...]
    for which, target in enumerate((g_query, g_key, g_value)):
        target[:, 0 : 2 * HEAD] = one[:, tile(which)]
        target[:, 2 * HEAD : 3 * HEAD] = third(two, which)
    for which in range(3):
        g_out[which * HEAD : (which + 1) * HEAD] = free(two, which).T
    g_up[...] = grad_up[...]
    g_down[...] = grad_down[...]
    sums = own_sums[...]
    rows = jnp.where(y == 0, sums[6:7], sums[7:8])
    for which, target in ((0, gb_query), (2, gb_value)):
        target[:, 0 : 2 * HEAD] = rows[:, tile(which)]
        target[:, 2 * HEAD : 3 * HEAD] = third(rows[:, 3 * lanes :], which)
    gb_up[...] = jnp.where(y == 0, sums[8:9], sums[9:10])
    kept = jnp.zeros((8, unit), jnp.float32)
    for part in range(sums.shape[1] // unit):
        kept = jnp.where(own == part, sums[0:8, part * unit : (part + 1) * unit], kept)
    for index, target in enumerate(vector_grads):
        target[...] = kept[index : index + 1]
    for copy in stores:
        copy.wait()


def fits(mesh, tokens, seq_lens, block_sizes, w_query, *others):
    unit, columns = w_query.shape
    w_up = others[8]
    return (
        mesh.shape["tensor"] == 4
        and mesh.shape["dp"] % 4 == 0
        and seq_lens.shape[0] == 2
        and tokens.shape[0] % (4 * block) == 0
        and columns == 3 * HEAD
        and unit % 16 == 0
        and unit <= lanes
        and unit * mesh.shape["dp"] == tokens.shape[1] == 12 * HEAD == w_up.shape[1]
    )


def on_device_fast(lines, tokens, seq_lens, block_sizes, w_query, b_query, w_key, w_value, b_value, w_out, b_out,
                   gain_one, shift_one, w_up, b_up, w_down, b_down, gain_two, shift_two, cotangent):
    bf16, f32 = jnp.bfloat16, jnp.float32
    total, width = tokens.shape[0] // 2, tokens.shape[1]
    half, pairs = total // 2, width // 2
    unit = w_query.shape[0]
    slots = lines * 4
    blocks = total // block
    dma = pltpu.SemaphoreType.DMA
    shape = jax.ShapeDtypeStruct
    anywhere, on_chip = pl.BlockSpec(memory_space=pl.ANY), pl.BlockSpec(memory_space=pltpu.VMEM)
    scalars = pl.BlockSpec(memory_space=pltpu.SMEM)
    pair, single = slice(0, 2 * HEAD), slice(2 * HEAD, 3 * HEAD)
    zero, zeros = jnp.zeros((HEAD,), bf16), jnp.zeros((2 * HEAD,), bf16)
    near = jnp.concatenate([b_query[pair], zeros, b_value[pair], b_query[single], zero, zeros, b_value[single], zero])
    far = jnp.concatenate([b_query[pair], zeros, b_value[pair], zero, b_query[single], zeros, zero, b_value[single]])
    vectors = jnp.stack([b_out, gain_one, shift_one, b_down, gain_two, shift_two])
    extra = jnp.concatenate([
        jnp.where(lax.axis_index("tensor") // 2 == 0, near, far)[None], b_up[None],
        jnp.pad(vectors, ((0, 0), (0, width - unit))), jnp.zeros((8, width), bf16)])
    raw = pl.pallas_call(
        functools.partial(layer_kernel, lines),
        out_shape=(
            shape((2 * total, width), bf16), shape((width // 4, total), f32), shape((width // 4, total), bf16),
            shape((unit, pairs), f32), shape((unit, pairs), f32), shape((unit, width), f32), shape((unit, width), f32),
            shape((16, width), f32)),
        in_specs=[anywhere] * 2 + [scalars] * 2 + [on_chip] * 7,
        out_specs=(anywhere,) + (on_chip,) * 7,
        scratch_shapes=[
            pltpu.VMEM((total, width), bf16), pltpu.VMEM((half, width), bf16),
            pltpu.VMEM((2, width, pairs), bf16), pltpu.VMEM((2, width, pairs), bf16),
            pltpu.VMEM((2, width, width), bf16), pltpu.VMEM((2, width, width), bf16),
            pltpu.VMEM((2, lines * 2 * 16, width), bf16), pltpu.VMEM((16, width), f32),
            *[pltpu.VMEM((total, pairs), bf16)] * 4, pltpu.VMEM((total, lanes), f32),
            pltpu.VMEM((total, 1), jnp.int32), pltpu.VMEM((blocks, 8, block), jnp.int32),
            *[pltpu.VMEM((blocks, 8, block), f32)] * 2,
            pltpu.VMEM((width, pairs), bf16), *[pltpu.VMEM((half, width), f32)] * 3, pltpu.VMEM((half, lanes), f32),
            pltpu.VMEM((total, width), bf16), *[pltpu.VMEM((total, 2 * width), bf16)] * 2,
            pltpu.VMEM((half, width), f32), *[pltpu.VMEM((total, width), bf16)] * 2,
            pltpu.VMEM((total, pairs), bf16), pltpu.VMEM((width, pairs), f32), *[pltpu.VMEM((half, width), bf16)] * 2,
            *[pltpu.VMEM((total, lanes), f32)] * 3, *[pltpu.VMEM((2, width, pairs), bf16)] * 2,
            pltpu.VMEM((2, 5, lines, unit, pairs), bf16), pltpu.VMEM((2, 7, lines, unit, width), bf16),
            *[pltpu.VMEM((3, 16, width), f32)] * 2, pltpu.VMEM((lines, 16, width), f32),
            *[pltpu.VMEM((2, total, width // 4), bf16)] * 2, pltpu.VMEM((width // 4, total), bf16),
            dma((3,)), dma((4, slots)), dma((4, 4, slots)), dma((slots,)), dma((4, slots)),
            dma((4, 7, lines)), dma((4, 7, lines)), dma((2, 16 + lines))],
        compiler_params=pltpu.CompilerParams(collective_id=0, has_side_effects=True, vmem_limit_bytes=62 * 2**20),
    )(tokens, cotangent, seq_lens, block_sizes, w_query, w_key, w_value, w_out.T, w_up, w_down.T, extra)

    small = [3 * HEAD, 3 * HEAD, width] + [unit] * 6
    done = pl.pallas_call(
        functools.partial(close_kernel, unit),
        out_shape=(
            shape((2 * total, width), bf16), shape((width // 4, 2 * total), f32),
            *[shape((unit, 3 * HEAD), f32)] * 3, shape((3 * HEAD, unit), f32), shape((unit, width), f32), shape((unit, width), f32),
            *[shape((1, size), f32) for size in small]),
        in_specs=[anywhere] + [on_chip] * 7,
        out_specs=(anywhere,) + (on_chip,) * 16,
        scratch_shapes=[pltpu.VMEM((4, half, width), bf16), dma((8,))],
        compiler_params=pltpu.CompilerParams(vmem_limit_bytes=62 * 2**20),
    )(*raw)
    output, input_grad, g_query, g_key, g_value, g_out, g_up, g_down = done[:8]
    gb_query, gb_value, gb_up, gb_out, g_gain_one, g_shift_one, gb_down, g_gain_two, g_shift_two = [array.reshape(-1) for array in done[8:]]
    return (output, input_grad.T, g_query, gb_query, g_key, g_value, gb_value, g_out, gb_out, g_gain_one, g_shift_one,
            g_up, gb_up, g_down.T, gb_down, g_gain_two, g_shift_two)


def solution(mesh):
    in_specs = (
        P("dp", None),
        P("dp"),
        P("dp"),
        P("dp", "tensor"),
        P("tensor"),
        P("dp", "tensor"),
        P("dp", "tensor"),
        P("tensor"),
        P("tensor", "dp"),
        P("dp"),
        P("dp"),
        P("dp"),
        P("dp", "tensor"),
        P("tensor"),
        P("tensor", "dp"),
        P("dp"),
        P("dp"),
        P("dp"),
        P("dp", None),
    )
    out_specs = (
        P("dp", None),
        P("dp", "tensor"),
        P("dp", "tensor"),
        P("tensor"),
        P("dp", "tensor"),
        P("dp", "tensor"),
        P("tensor"),
        P("tensor", "dp"),
        P("dp"),
        P("dp"),
        P("dp"),
        P("dp", "tensor"),
        P("tensor"),
        P("tensor", "dp"),
        P("dp"),
        P("dp"),
        P("dp"),
    )
    lines = mesh.shape["dp"] // 2

    def on_device(*arrays):
        if fits(mesh, *arrays):
            return on_device_fast(lines, *arrays)
        return on_device_plain(*arrays)

    return jax.shard_map(
        on_device, mesh=mesh, in_specs=in_specs, out_specs=out_specs, check_vma=False
    )
```

```python
import functools

import jax
import jax.numpy as jnp
from jax import lax
from jax.experimental import pallas as pl
from jax.experimental.pallas import tpu as pltpu
from jax.sharding import PartitionSpec as P

HEAD = 64
MESH = pl.DeviceIdType.MESH

norm_epsilon = 1e-12
inv_root_two = 0.7071067811865476
inv_root_tau = 0.3989422804014327
masked_score = -1000000000.0


def matmul(first_operand, second_operand):
    return jnp.dot(first_operand, second_operand, preferred_element_type=jnp.float32)


def contract_rows(first_operand, second_operand):
    return lax.dot_general(
        first_operand, second_operand, (((0,), (0,)), ((), ())), preferred_element_type=jnp.float32
    )


def contract_cols(first_operand, second_operand):
    return lax.dot_general(
        first_operand, second_operand, (((1,), (1,)), ((), ())), preferred_element_type=jnp.float32
    )


def norm_forward(row_values, gain_row, offset_row):
    row_mean = jnp.mean(row_values, axis=-1, keepdims=True)
    centred = row_values - row_mean
    variance = jnp.mean(centred * centred, axis=-1, keepdims=True)
    inv_scale = lax.rsqrt(variance + norm_epsilon)
    normal_rows = centred * inv_scale
    return (normal_rows * gain_row + offset_row, normal_rows, inv_scale)


def norm_backward(upstream, normal_rows, inv_scale, gain_row):
    scaled = upstream * gain_row
    row_grad = inv_scale * (
        scaled
        - jnp.mean(scaled, axis=-1, keepdims=True)
        - normal_rows * jnp.mean(scaled * normal_rows, axis=-1, keepdims=True)
    )
    return (row_grad, jnp.sum(upstream * normal_rows, axis=0), jnp.sum(upstream, axis=0))


def allowed_mask(first_row, row_total, key_total, seq_length, block_size):
    row_pos = first_row + lax.broadcasted_iota(jnp.int32, (row_total, key_total), 0)
    key_pos = lax.broadcasted_iota(jnp.int32, (row_total, key_total), 1)
    return (key_pos // block_size <= row_pos // block_size) & (key_pos < seq_length)


def attend(query_rows, key_rows, value_rows, seq_length, block_size):
    row_total, local_heads, head_size = query_rows.shape
    block_rows = min(512, row_total)
    block_count = row_total // block_rows
    query_blocks = query_rows.reshape(block_count, block_rows, local_heads, head_size)

    def one_block(block_pair):
        block_index, query_block = block_pair
        scores = jnp.einsum(
            "qhd,khd->hqk", query_block, key_rows, preferred_element_type=jnp.float32
        )
        allowed = allowed_mask(
            block_index * block_rows, block_rows, row_total, seq_length, block_size
        )
        scores = jnp.where(allowed[None], scores, masked_score)
        top_score = jnp.max(scores, axis=-1, keepdims=True)
        exp_scores = jnp.exp(scores - top_score)
        exp_total = jnp.sum(exp_scores, axis=-1, keepdims=True)
        probabilities = (exp_scores / exp_total).astype(jnp.bfloat16)
        context = jnp.einsum(
            "hqk,khd->qhd", probabilities, value_rows, preferred_element_type=jnp.float32
        )
        return (context.astype(jnp.bfloat16), top_score[..., 0] + jnp.log(exp_total[..., 0]))

    contexts, log_sums = lax.map(
        one_block, (jnp.arange(block_count, dtype=jnp.int32), query_blocks)
    )
    return (contexts.reshape(row_total, local_heads * head_size), log_sums)


def attend_back(query_rows, key_rows, value_rows, context_grad, log_sums, seq_length, block_size):
    row_total, local_heads, head_size = query_rows.shape
    block_rows = min(512, row_total)
    block_count = row_total // block_rows
    query_blocks = query_rows.reshape(block_count, block_rows, local_heads, head_size)
    grad_blocks = context_grad.reshape(block_count, block_rows, local_heads, head_size)

    def one_block(running, block_pack):
        key_grad, value_grad = running
        block_index, query_block, grad_block, log_block = block_pack
        scores = jnp.einsum(
            "qhd,khd->hqk", query_block, key_rows, preferred_element_type=jnp.float32
        )
        allowed = allowed_mask(
            block_index * block_rows, block_rows, row_total, seq_length, block_size
        )
        probabilities = jnp.where(allowed[None], jnp.exp(scores - log_block[..., None]), 0.0)
        prob_grad = jnp.einsum(
            "qhd,khd->hqk", grad_block, value_rows, preferred_element_type=jnp.float32
        )
        row_dot = jnp.sum(prob_grad * probabilities, axis=-1, keepdims=True)
        score_grad = (probabilities * (prob_grad - row_dot)).astype(jnp.bfloat16)
        query_grad = jnp.einsum(
            "hqk,khd->qhd", score_grad, key_rows, preferred_element_type=jnp.float32
        )
        key_grad = key_grad + jnp.einsum(
            "hqk,qhd->khd", score_grad, query_block, preferred_element_type=jnp.float32
        )
        value_grad = value_grad + jnp.einsum(
            "hqk,qhd->khd",
            probabilities.astype(jnp.bfloat16),
            grad_block,
            preferred_element_type=jnp.float32,
        )
        return ((key_grad, value_grad), query_grad)

    empty = jnp.zeros((row_total, local_heads, head_size), jnp.float32)
    (key_grad, value_grad), query_grads = lax.scan(
        one_block,
        (empty, empty),
        (jnp.arange(block_count, dtype=jnp.int32), query_blocks, grad_blocks, log_sums),
    )
    width = local_heads * head_size
    return (
        query_grads.reshape(row_total, width),
        key_grad.reshape(row_total, width),
        value_grad.reshape(row_total, width),
    )


def on_device_plain(
    tokens,
    seq_lens,
    block_sizes,
    w_query,
    b_query,
    w_key,
    w_value,
    b_value,
    w_out,
    b_out,
    gain_one,
    shift_one,
    w_up,
    b_up,
    w_down,
    b_down,
    gain_two,
    shift_two,
    cotangent,
):
    micro_total = seq_lens.shape[0]
    seq_rows = tokens.shape[0] // micro_total
    head_cols = w_query.shape[1]
    local_heads = head_cols // HEAD
    model_width = tokens.shape[1]
    own_cols = model_width // lax.axis_size("tensor")
    column_start = lax.axis_index("tensor") * own_cols
    query_bias = b_query.astype(jnp.float32)
    value_bias = b_value.astype(jnp.float32)
    up_bias = b_up.astype(jnp.float32)
    owned = (
        w_query,
        w_key,
        w_value,
        w_out,
        w_up,
        w_down,
        b_out,
        gain_one,
        shift_one,
        b_down,
        gain_two,
        shift_two,
    )

    def shaped(flat_rows):
        return flat_rows.reshape(seq_rows, local_heads, HEAD)

    layer_outputs = []
    input_grads = []
    totals = None
    for micro_index in range(micro_total):
        rows_in = tokens[micro_index * seq_rows : (micro_index + 1) * seq_rows]
        upstream = cotangent[micro_index * seq_rows : (micro_index + 1) * seq_rows].astype(
            jnp.float32
        )
        seq_length = seq_lens[micro_index]
        block_size = block_sizes[micro_index]
        forward_set = (
            lax.all_gather(owned[0], "dp", axis=0, tiled=True),
            lax.all_gather(owned[1], "dp", axis=0, tiled=True),
            lax.all_gather(owned[2], "dp", axis=0, tiled=True),
            lax.all_gather(owned[3], "dp", axis=1, tiled=True),
            lax.all_gather(owned[4], "dp", axis=0, tiled=True),
            lax.all_gather(owned[5], "dp", axis=1, tiled=True),
            lax.all_gather(owned[6], "dp", axis=0, tiled=True),
            lax.all_gather(owned[7], "dp", axis=0, tiled=True),
            lax.all_gather(owned[8], "dp", axis=0, tiled=True),
            lax.all_gather(owned[9], "dp", axis=0, tiled=True),
            lax.all_gather(owned[10], "dp", axis=0, tiled=True),
            lax.all_gather(owned[11], "dp", axis=0, tiled=True),
        )
        (
            full_query,
            full_key,
            full_value,
            full_out,
            full_up,
            full_down,
            full_out_bias,
            full_gain_one,
            full_shift_one,
            full_down_bias,
            full_gain_two,
            full_shift_two,
        ) = forward_set
        out_bias = full_out_bias.astype(jnp.float32)
        down_bias = full_down_bias.astype(jnp.float32)
        first_gain = full_gain_one.astype(jnp.float32)
        first_shift = full_shift_one.astype(jnp.float32)
        second_gain = full_gain_two.astype(jnp.float32)
        second_shift = full_shift_two.astype(jnp.float32)
        query_rows = ((matmul(rows_in, full_query) + query_bias) * 0.125).astype(jnp.bfloat16)
        key_rows = matmul(rows_in, full_key).astype(jnp.bfloat16)
        value_rows = (matmul(rows_in, full_value) + value_bias).astype(jnp.bfloat16)
        context, log_sums = attend(
            shaped(query_rows), shaped(key_rows), shaped(value_rows), seq_length, block_size
        )
        attended = lax.psum(matmul(context, full_out), "tensor") + out_bias
        first_norm, first_hat, first_scale = norm_forward(
            rows_in.astype(jnp.float32) + attended, first_gain, first_shift
        )
        normed = first_norm.astype(jnp.bfloat16)
        expanded = matmul(normed, full_up) + up_bias
        normal_cdf = 0.5 * (1.0 + lax.erf(expanded * inv_root_two))
        hidden = (expanded * normal_cdf).astype(jnp.bfloat16)
        lowered = lax.psum(matmul(hidden, full_down), "tensor") + down_bias
        second_norm, second_hat, second_scale = norm_forward(
            normed.astype(jnp.float32) + lowered, second_gain, second_shift
        )
        layer_outputs.append(second_norm.astype(jnp.bfloat16))
        second_grad, grad_gain_two, grad_shift_two = norm_backward(
            upstream, second_hat, second_scale, second_gain
        )
        down_bias_grad = jnp.sum(second_grad, axis=0)
        second_low = second_grad.astype(jnp.bfloat16)
        down_grad = contract_rows(hidden, second_low)
        hidden_grad = contract_cols(second_low, full_down)
        expanded_grad = hidden_grad * (
            normal_cdf + expanded * jnp.exp(-0.5 * expanded * expanded) * inv_root_tau
        )
        up_bias_grad = jnp.sum(expanded_grad, axis=0)
        expanded_low = expanded_grad.astype(jnp.bfloat16)
        up_grad = contract_rows(normed, expanded_low)
        normed_grad = lax.psum(contract_cols(expanded_low, full_up), "tensor") + second_grad
        first_grad, grad_gain_one, grad_shift_one = norm_backward(
            normed_grad, first_hat, first_scale, first_gain
        )
        out_bias_grad = jnp.sum(first_grad, axis=0)
        first_low = first_grad.astype(jnp.bfloat16)
        out_grad = contract_rows(context, first_low)
        context_grad = contract_cols(first_low, full_out).astype(jnp.bfloat16)
        query_grad, key_grad, value_grad = attend_back(
            shaped(query_rows),
            shaped(key_rows),
            shaped(value_rows),
            shaped(context_grad),
            log_sums,
            seq_length,
            block_size,
        )
        query_grad = query_grad * 0.125
        query_bias_grad = jnp.sum(query_grad, axis=0)
        value_bias_grad = jnp.sum(value_grad, axis=0)
        query_low = query_grad.astype(jnp.bfloat16)
        key_low = key_grad.astype(jnp.bfloat16)
        value_low = value_grad.astype(jnp.bfloat16)
        query_w_grad = contract_rows(rows_in, query_low)
        key_w_grad = contract_rows(rows_in, key_low)
        value_w_grad = contract_rows(rows_in, value_low)
        input_term = (
            contract_cols(query_low, full_query)
            + contract_cols(key_low, full_key)
            + contract_cols(value_low, full_value)
        )
        own_grad = lax.psum_scatter(
            input_term.astype(jnp.bfloat16), "tensor", scatter_dimension=1, tiled=True
        ).astype(jnp.float32)
        input_grads.append(
            own_grad + lax.dynamic_slice_in_dim(first_grad, column_start, own_cols, 1)
        )
        terms = (
            query_w_grad,
            query_bias_grad,
            key_w_grad,
            value_w_grad,
            value_bias_grad,
            out_grad,
            out_bias_grad,
            grad_gain_one,
            grad_shift_one,
            up_grad,
            up_bias_grad,
            down_grad,
            down_bias_grad,
            grad_gain_two,
            grad_shift_two,
        )
        if totals is None:
            totals = terms
        else:
            totals = tuple((running + addend for running, addend in zip(totals, terms)))
    summed = (
        lax.psum_scatter(totals[0], "dp", scatter_dimension=0, tiled=True),
        lax.psum_scatter(totals[2], "dp", scatter_dimension=0, tiled=True),
        lax.psum_scatter(totals[3], "dp", scatter_dimension=0, tiled=True),
        lax.psum_scatter(totals[5], "dp", scatter_dimension=1, tiled=True),
        lax.psum_scatter(totals[9], "dp", scatter_dimension=0, tiled=True),
        lax.psum_scatter(totals[11], "dp", scatter_dimension=1, tiled=True),
        lax.psum_scatter(totals[6], "dp", scatter_dimension=0, tiled=True),
        lax.psum_scatter(totals[7], "dp", scatter_dimension=0, tiled=True),
        lax.psum_scatter(totals[8], "dp", scatter_dimension=0, tiled=True),
        lax.psum_scatter(totals[12], "dp", scatter_dimension=0, tiled=True),
        lax.psum_scatter(totals[13], "dp", scatter_dimension=0, tiled=True),
        lax.psum_scatter(totals[14], "dp", scatter_dimension=0, tiled=True),
    )
    bias_sums = lax.psum((totals[1], totals[4], totals[10]), "dp")
    return (
        jnp.concatenate(layer_outputs, 0),
        jnp.concatenate(input_grads, 0),
        summed[0],
        bias_sums[0],
        summed[1],
        summed[2],
        bias_sums[1],
        summed[3],
        summed[6],
        summed[7],
        summed[8],
        summed[4],
        bias_sums[2],
        summed[5],
        summed[9],
        summed[10],
        summed[11],
    )


def place():
    dp = lax.axis_index("dp")
    tensor = lax.axis_index("tensor")
    return dp // 2, dp % 2, tensor // 2, tensor % 2


def device(z, x, y, core):
    return (z * 2 + x, y * 2 + core)


def when(ok, body):
    if ok is None:
        body()
    else:
        pl.when(ok)(body)


def both(*conditions):
    result = None
    for condition in conditions:
        if condition is not None:
            result = condition if result is None else result & condition
    return result


def greet(lines):
    z, x, y, core = place()
    barrier = pltpu.get_barrier_semaphore()

    def signal(target):
        pl.semaphore_signal(barrier, inc=1, device_id=target, device_id_type=MESH)

    signal(device(z, 1 - x, y, core))
    signal(device(z, x, 1 - y, core))
    signal(device(z, x, y, 1 - core))
    for k in range(1, lines):
        pl.when(z >= k)(lambda: signal(device(z - k, x, y, core)))
        pl.when(z + k < lines)(lambda: signal(device(z + k, x, y, core)))
    pl.semaphore_wait(barrier, 3 + lines - 1)


class Mover:
    def __init__(self, lines, array, recv_sem, send_sem, rows, corner):
        self.lines, self.array, self.recv_sem, self.send_sem = lines, array, recv_sem, send_sem
        self.rows, self.corner = rows, corner
        self.here = place()
        self.sent = []

    def owner(self, k, dx, dy):
        z, x, y, core = self.here
        return z + k, (1 - x if dx else x), (1 - y if dy else y)

    def start(self, k, dx, dy):
        z, x, y = self.owner(k, dx, dy)
        return y, pl.ds(pl.multiple_of((z * 2 + x) * self.rows, self.rows), self.rows)

    def view(self, k, dx, dy):
        return self.array.at[self.start(k, dx, dy)]

    def there(self, k):
        z = self.here[0]
        if k == 0:
            return None
        return z + k < self.lines if k > 0 else z + k >= 0

    def target(self, way):
        z, x, y, core = self.here
        moved = {"up": (z + 1, x, y), "down": (z - 1, x, y), "x": (z, 1 - x, y), "y": (z, x, 1 - y)}[way]
        return device(*moved, core)

    def allowed(self, k, way, parity):
        z = self.here[0]
        line = {"up": self.there(1), "down": self.there(-1)}.get(way)
        even = None if parity is None else (z + k) % 2 == parity
        return both(self.there(k), line, even)

    def send(self, k, dx, dy, way, parity=None, kind=None):
        when(self.allowed(k, way, parity), lambda: self.copy(k, dx, dy, way, kind).start())
        self.sent.append((k, dx, dy, way, parity, kind))

    def drain(self):
        for k, dx, dy, way, parity, kind in self.sent:
            when(self.allowed(k, way, parity), lambda: self.copy(k, dx, dy, way, kind).wait_send())


class Gather(Mover):
    def copy(self, k, dx, dy, way, kind=None):
        z, x, y = self.owner(k, dx, dy)
        index = y * self.lines * 2 + z * 2 + x
        return pltpu.make_async_remote_copy(
            src_ref=self.view(k, dx, dy), dst_ref=self.view(k, dx, dy),
            send_sem=self.send_sem.at[("up", "down", "x", "y").index(way), index], recv_sem=self.recv_sem.at[index],
            device_id=self.target(way), device_id_type=MESH)

    def take(self, k, dx, dy):
        when(self.there(k), lambda: self.copy(k, dx, dy, "x").wait_recv())

    def begin(self):
        for way in ("x", "y", "up", "down"):
            self.send(0, 0, 0, way)

    def planes(self, k):
        self.take(k, 1, 0)
        self.take(k, 0, 1)
        if self.corner is None:
            self.send(k, 1, 0, "y", 1)
            self.send(k, 0, 1, "x", 0)
        elif k == 0:
            self.send(0, *((1, 0) if self.corner == "y" else (0, 1)), self.corner)

    def column(self, k, dx=0, dy=0):
        self.take(k, dx, dy)
        self.send(k, dx, dy, "up" if k < 0 else "down")
        if not dx:
            self.send(k, 0, 0, "x")
            self.send(k, 0, 0, "y")

    def opposite(self, k):
        if k == 0:
            self.take(0, 1, 1)
            self.send(0, 1, 1, "up")
            self.send(0, 1, 1, "down")
        else:
            self.column(k, 1, 1)

    def events(self):
        last = self.lines - 1
        found = [(0, self.begin)]
        for k in range(1, self.lines):
            found += [(k, lambda s=s: self.column(s)) for s in (-k, k)]
            found += [(k, lambda s=s: self.planes(s)) for s in ((0,) if k == 1 else (1 - k, k - 1))]
            if self.corner is not None:
                found += [(k + 0.5, lambda s=s: self.opposite(s)) for s in ((0,) if k == 1 else (1 - k, k - 1))]
        found += [(self.lines, lambda s=s: self.planes(s)) for s in (-last, last)]
        if self.corner is None:
            found += [(self.lines + 1, lambda s=s: self.take(s, 1, 1)) for s in [0] + [s for k in range(1, self.lines) for s in (-k, k)]]
        else:
            found += [(self.lines + 0.5, lambda s=s: self.opposite(s)) for s in (-last, last)]
        return found


class Scatter(Mover):
    def __init__(self, lines, array, slots, recv_sem, send_sem, rows, corner):
        super().__init__(lines, array, recv_sem, send_sem, rows, corner)
        self.slots = slots

    def copy(self, k, dx, dy, way, kind):
        z = self.here[0] + k
        return pltpu.make_async_remote_copy(
            src_ref=self.view(k, dx, dy), dst_ref=self.slots.at[kind, z],
            send_sem=self.send_sem.at[kind, z], recv_sem=self.recv_sem.at[kind, z],
            device_id=self.target(way), device_id_type=MESH)

    def taken(self, k, kind):
        self.copy(k, 0, 0, "x", kind).wait_recv()
        return self.slots[kind, self.here[0] + k].astype(jnp.float32)

    def add(self, k, dx, dy, *kinds):
        start = self.start(k, dx, dy)
        result = self.array[start].astype(jnp.float32)
        for kind in kinds:
            result = result + self.taken(k, kind)
        self.array[start] = result.astype(jnp.bfloat16)

    def distances(self):
        return [s for k in range(self.lines - 1, 0, -1) for s in (k, -k)]

    def begin(self):
        if self.corner is None:
            for k in self.distances() + [0]:
                self.send(k, 1, 1, "x", 0, 0)
                self.send(k, 1, 1, "y", 1, 0)
            for k in self.distances() + [0]:
                self.send(k, 0, 1, "y", 1, 2)
                self.send(k, 1, 0, "x", 0, 1)
            return
        if self.corner == "planes":
            for k in self.distances() + [0]:
                self.send(k, 1, 1, "x", None, 0)
            for k in self.distances() + [0]:
                self.send(k, 1, 0, "x", None, 1)
            return
        for s in (self.lines - 1, 1 - self.lines):
            self.opposite(s)
        for k in self.distances():
            self.send(k, 1, 0, "x", None, 1)
            self.send(k, 0, 1, "y", None, 2)
        if self.corner == "x":
            self.send(0, 1, 0, "x", None, 1)
        else:
            self.send(0, 0, 1, "y", None, 2)

    def opposite(self, k):
        if k == 0:
            pl.when(self.there(-1))(lambda: self.add(0, 1, 1, 5))
            pl.when(self.there(1))(lambda: self.add(0, 1, 1, 6))
            self.send(0, 1, 1, self.corner, None, 0)
            return
        behind, way, kind = (self.there(-1), "up", 5) if k > 0 else (self.there(1), "down", 6)
        pl.when(self.there(k) & behind)(lambda: self.add(k, 1, 1, kind))
        self.send(k, 1, 1, way, None, kind)

    def corners(self, k):
        for dx, dy, way, kind, parity in ((0, 1, "y", 2, 0), (1, 0, "x", 1, 1)):
            if self.corner is None:
                pl.when(both(self.there(k), (self.here[0] + k) % 2 == parity))(lambda: self.add(k, dx, dy, 0))
                self.send(k, dx, dy, way, parity, kind)
            elif self.corner == "planes":
                if dy:
                    when(self.there(k), lambda: self.add(k, dx, dy, 0))
                    self.send(k, dx, dy, way, None, kind)
            elif k == 0 and self.corner != way:
                self.add(0, dx, dy, 0)
                self.send(0, dx, dy, way, None, kind)

    def line(self, k):
        behind, way, kind = (self.there(-1), "up", 3) if k > 0 else (self.there(1), "down", 4)
        pl.when(self.there(k) & behind)(lambda: self.add(k, 0, 0, 1, 2, kind))
        pl.when(self.there(k) & jnp.logical_not(behind))(lambda: self.add(k, 0, 0, 1, 2))
        self.send(k, 0, 0, way, None, kind)

    def own(self, target):
        start = self.start(0, 0, 0)
        target[...] = self.array[start].astype(jnp.float32) + self.taken(0, 1) + self.taken(0, 2)

        def more(kind):
            target[...] += self.taken(0, kind)

        pl.when(self.there(-1))(lambda: more(3))
        pl.when(self.there(1))(lambda: more(4))

    def events(self, target):
        found = [(0, self.begin)]
        if self.corner in (None, "planes"):
            found += [(1, lambda s=s: self.corners(s)) for s in self.distances() + [0]]
            base = 1
        else:
            found += [(self.lines - abs(s), lambda s=s: self.opposite(s)) for s in self.distances() + [0] if abs(s) < self.lines - 1]
            found += [(self.lines + 1, lambda: self.corners(0))]
            base = 1
        found += [(base + self.lines - abs(s), lambda s=s: self.line(s)) for s in self.distances()]
        found += [(self.lines + base + 1, lambda: self.own(target))]
        return sorted(found, key=lambda event: event[0])


def merged(*lists):
    found = [(stage + first, order, step) for order, (first, events) in enumerate(lists) for stage, step in events]
    return sorted(found, key=lambda event: event[:2])


def until_done(events, orders):
    last = max(place for place, event in enumerate(events) if event[1] in orders)
    return [step for _, _, step in events[: last + 1]], events[last + 1 :]


def steps_of(events):
    return [step for _, _, step in events]


def portions(steps, count):
    cuts = [round(i * len(steps) / count) for i in range(count + 1)]
    return [steps[first:last] for first, last in zip(cuts, cuts[1:])]


def run(steps):
    for step in steps:
        step()


lanes = 128
block = 256


def dot(first, second, dims):
    return lax.dot_general(first, second, ((dims[:1], dims[1:]), ((), ())), preferred_element_type=jnp.float32)


plain, right_turned, left_turned = (1, 0), (1, 1), (0, 0)


def rows_at(start, size):
    return pl.ds(pl.multiple_of(start, size), size)


def low_half(rows):
    return lax.broadcasted_iota(jnp.int32, (rows, lanes), 1) < HEAD


def tile(index):
    return slice(index * lanes, (index + 1) * lanes)


def swapped(values):
    return pltpu.roll(values, HEAD, 1)


def each(count, body):
    lax.fori_loop(0, count, lambda index, carry: (body(index), carry)[1], 0)


def norm_rows(values):
    centred = values - jnp.mean(values, axis=-1, keepdims=True)
    variance = jnp.mean(centred * centred, axis=-1, keepdims=True)
    scale = lax.rsqrt(variance + norm_epsilon)
    return centred * scale, scale


def norm_rows_back(upstream, hat, scale, gain):
    scaled = upstream * gain
    return scale * (scaled - jnp.mean(scaled, axis=-1, keepdims=True) - hat * jnp.mean(scaled * hat, axis=-1, keepdims=True))


def total_rows(values):
    return jnp.sum(values, axis=0, keepdims=True)


def swap_copy(src, dst, sems, index, near):
    z, x, y, core = place()
    target = device(z, x, y, 1 - core) if near else device(z, x, 1 - y, core)
    return pltpu.make_async_remote_copy(
        src_ref=src, dst_ref=dst, send_sem=sems.at[0, index], recv_sem=sems.at[1, index],
        device_id=target, device_id_type=MESH)


def pack_weights(y, own, unit, w_query, w_key, w_value, w_out, w_up, w_down, weights):
    here = rows_at(own * unit, unit)
    turned = w_out[...].astype(jnp.float32).T.astype(jnp.bfloat16)
    for which, array in enumerate((w_query, w_key, w_value)):
        weights[0][y, here, tile(which)] = array[:, 0 : 2 * HEAD]
        single = array[:, 2 * HEAD : 3 * HEAD]
        out = turned[:, which * HEAD : (which + 1) * HEAD]
        weights[1][y, here, tile(which)] = jnp.where(
            y == 0, jnp.concatenate([single, out], axis=1), jnp.concatenate([out, single], axis=1))
    weights[2][y, here] = w_up[...]
    weights[3][y, here] = w_down[...]


def turn_out(mixed, target):
    low = low_half(mixed.shape[1])
    first = [mixed[0, :, tile(i)].astype(jnp.float32) for i in range(3)]
    second = [mixed[1, :, tile(i)].astype(jnp.float32) for i in range(3)]
    for pair, values in enumerate((
        jnp.where(low, swapped(first[0]), first[1]),
        jnp.where(low, second[0], swapped(second[1])),
        jnp.where(low, swapped(first[2]), swapped(second[2])),
    )):
        target[:, tile(pair)] = values.astype(jnp.bfloat16)


def spread_vectors(lines, unit, extras, vectors):
    width = vectors.shape[1]
    column = lax.broadcasted_iota(jnp.int32, (lanes, width), 1)
    row = lax.broadcasted_iota(jnp.int32, (lanes, width), 0)

    def add(own, result):
        spot = ((column == row + own * unit) & (row < unit)).astype(jnp.bfloat16)
        return result + dot(extras[0, rows_at(own * 16, 16), 0:lanes], spot, plain)

    result = lax.fori_loop(0, lines * 2, add, jnp.zeros((16, width), jnp.float32))
    vectors[...] = result


def key_limit(places, size, length):
    blocks = jnp.floor((places.astype(jnp.float32) + 0.5) / size.astype(jnp.float32)).astype(jnp.int32)
    return jnp.minimum((blocks + 1) * size, length)


def attend_pair(pair, query, key, value, limit, context, log_sum, steps):
    total = query.shape[0]
    keep = low_half(total)
    nothing = jnp.zeros((), jnp.bfloat16)
    keys = [jnp.where(chosen, key[:, tile(pair)], nothing) for chosen in (keep, ~keep)]
    values = jnp.concatenate([jnp.where(chosen, value[:, tile(pair)], nothing) for chosen in (keep, ~keep)], axis=0)
    lane = lax.broadcasted_iota(jnp.int32, (block, lanes), 1)
    places = lax.broadcasted_iota(jnp.int32, (block, total), 1)

    def one(index):
        for number, group in enumerate(steps):
            if group:
                pl.when(index == number)(functools.partial(run, group))
        rows = rows_at(index * block, block)
        asked = query[rows, tile(pair)]
        allowed = places < limit[rows]
        logs = log_sum[rows] if pair else jnp.zeros((block, lanes), jnp.float32)
        probs = []
        for half in range(2):
            scores = jnp.where(allowed, dot(asked, keys[half], right_turned), masked_score)
            top = jnp.max(scores, axis=-1, keepdims=True)
            grown = jnp.exp(scores - top)
            sums = jnp.sum(grown, axis=-1, keepdims=True)
            probs.append((grown * (1.0 / sums)).astype(jnp.bfloat16))
            logs = jnp.where(lane == 2 * pair + half, top + jnp.log(sums), logs)
        context[rows, tile(pair)] = dot(jnp.concatenate(probs, axis=1), values, plain).astype(jnp.bfloat16)
        log_sum[rows] = logs

    each(total // block, one)


def back_pair(pair, query, key, value, context_grad, limit_rows, log_rows, dot_rows, query_acc, key_acc, value_acc, steps):
    total = query.shape[0]
    keep = low_half(total)
    low = low_half(block)
    nothing = jnp.zeros((), jnp.bfloat16)
    keys = [jnp.where(chosen, key[:, tile(pair)], nothing) for chosen in (keep, ~keep)]
    values = [jnp.where(chosen, value[:, tile(pair)], nothing) for chosen in (keep, ~keep)]
    key_pile = jnp.concatenate(keys, axis=0)
    places = lax.broadcasted_iota(jnp.int32, (total, block), 0)
    value_acc[...] = jnp.zeros_like(value_acc)
    key_acc[...] = jnp.zeros_like(key_acc)

    def halves(rows):
        return jnp.concatenate([jnp.where(low, rows, nothing), jnp.where(low, nothing, rows)], axis=0)

    def one(index):
        for number, group in enumerate(steps):
            if group:
                pl.when(index == number)(functools.partial(run, group))
        rows = rows_at(index * block, block)
        asked = query[rows, tile(pair)]
        wanted = context_grad[rows, tile(pair)]
        allowed = places < limit_rows[index, 0:1]
        all_probs, all_grads = [], []
        for half in range(2):
            head = 2 * pair + half
            grown = jnp.exp(dot(keys[half], asked, right_turned) - log_rows[index, head : head + 1])
            probs = jnp.where(allowed, grown, 0.0)
            prob_grad = dot(values[half], wanted, right_turned)
            all_grads.append((probs * (prob_grad - dot_rows[index, head : head + 1])).astype(jnp.bfloat16))
            all_probs.append(probs.astype(jnp.bfloat16))
        value_acc[...] += dot(jnp.concatenate(all_probs, axis=1), halves(wanted), plain)
        key_acc[...] += dot(jnp.concatenate(all_grads, axis=1), halves(asked), plain)
        query_acc[rows] = dot(jnp.concatenate(all_grads, axis=0), key_pile, left_turned)

    each(total // block, one)


def layer_kernel(
    lines, tokens_all, cotangent_all, seq_lens, block_sizes,
    w_query, w_key, w_value, w_out, w_up, w_down, extra,
    output, input_own, input_far, grad_one, grad_two, grad_up, grad_down, own_sums,
    tokens, cotangent, w_first, w_second, w_wide, w_long, extras, vectors,
    query, key, value, context, log_sum, limit, limit_rows, log_rows, dot_rows,
    turned, sent, got, hat_one, scale_one, normed, slope, hidden, second_grad, second_low, first_low, context_grad, out_grad, out_rows, far_out,
    query_acc, key_acc, value_acc, terms_first, terms_second, slots_narrow, slots_wide,
    sums, vec_got, line_got, turn_sent, turn_got, far_sent,
    local, gather_recv, gather_send, extra_recv, extra_send, scatter_recv, scatter_send, sems,
):
    z, x, y, core = place()
    own = z * 2 + x
    total, width = tokens.shape
    half = total // 2
    mine, theirs = core * half, (1 - core) * half
    unit = w_query.shape[0]
    blocks = total // block
    weights = (w_first, w_second, w_wide, w_long)

    load_tokens = pltpu.make_async_copy(tokens_all.at[rows_at(y * total, total)], tokens, local.at[0])
    load_tokens.start()
    load_cotangent = pltpu.make_async_copy(cotangent_all.at[rows_at(y * total + mine, half)], cotangent, local.at[1])
    load_cotangent.start()
    pack_weights(y, own, unit, w_query, w_key, w_value, w_out, w_up, w_down, weights)
    extras[y, rows_at(own * 16, 16)] = extra[...]
    greet(lines)
    gathers = [
        Gather(lines, weights[part], gather_recv.at[part], gather_send.at[part], unit, corner)
        for part, corner in enumerate((None, None, None, None))]
    small = Gather(lines, extras, extra_recv, extra_send, 16, None)
    first, second, wide, long = gathers
    offsets = (0, 0, 2, 4, 6)
    gathering = merged(*zip(offsets, [mover.events() for mover in (small, *gathers)]))
    opening, gathering = until_done(gathering, (0, 1))
    early, gathering = until_done(gathering, (2,))
    later, gathering = until_done(gathering, (3,))
    early, later, ending = portions(early, 9), portions(later, 6), portions(steps_of(gathering), 3)
    run(opening[:2])
    size, length = block_sizes[y], seq_lens[y]
    limit[...] = key_limit(lax.broadcasted_iota(jnp.int32, (total, 1), 0), size, length)
    for index in range(blocks):
        limit_rows[index] = key_limit(index * block + lax.broadcasted_iota(jnp.int32, (8, block), 1), size, length)
    run(opening[2:])
    load_tokens.wait()
    bias = [extras[near, rows_at(own * 16, 16)].astype(jnp.float32)[0:1] for near in range(2)]
    low = low_half(block)

    def project(index):
        rows = rows_at(index * block, block)
        inputs = tokens[rows]
        for near in range(2):
            found = dot(inputs, w_first[near], plain) + bias[near][:, 0 : 3 * lanes]
            query[rows, tile(near)] = (found[:, tile(0)] * 0.125).astype(jnp.bfloat16)
            key[rows, tile(near)] = found[:, tile(1)].astype(jnp.bfloat16)
            value[rows, tile(near)] = found[:, tile(2)].astype(jnp.bfloat16)

    def project_mixed(index):
        rows = rows_at(index * block, block)
        inputs = tokens[rows]
        found = [dot(inputs, w_second[near], plain) + bias[near][:, 3 * lanes :] for near in range(2)]
        mixed = [jnp.where(low, found[0][:, tile(which)], found[1][:, tile(which)]) for which in range(3)]
        query[rows, tile(2)] = (mixed[0] * 0.125).astype(jnp.bfloat16)
        key[rows, tile(2)] = mixed[1].astype(jnp.bfloat16)
        value[rows, tile(2)] = mixed[2].astype(jnp.bfloat16)

    each(blocks, project)
    def attend(pair, steps):
        attend_pair(pair, query, key, value, limit, context, log_sum, steps)

    attend(0, early[0:4])
    attend(1, early[4:8])
    run(early[8])
    each(blocks, project_mixed)
    attend(2, later[0:4])
    run(later[4])
    turn_out(w_second, turned)
    spread_vectors(lines, unit, extras, vectors)
    vector = lambda index: vectors[2 + index : 3 + index]
    up_bias = [extras[near, rows_at(own * 16, 16)].astype(jnp.float32)[1:2] for near in range(2)]
    sums[0] = jnp.zeros_like(sums.at[0])
    count = half // block

    def add_sum(index, values):
        sums[0, index : index + 1] += total_rows(values)

    def away(term, index):
        def body(step):
            sent[rows_at(step * block, block)] = term(rows_at(theirs + step * block, block))

        each(count, body)
        copy = swap_copy(sent, got, sems, index, True)
        copy.start()
        return copy

    def attended(rows):
        return dot(context[rows], turned[...], right_turned)

    copy = away(attended, 0)

    def stay_a(step):
        hat_one[rows_at(step * block, block)] = attended(rows_at(mine + step * block, block))

    each(count, stay_a)
    copy.wait()

    def first_norm(step):
        rows = rows_at(step * block, block)
        full = rows_at(mine + step * block, block)
        values = tokens[full].astype(jnp.float32) + ((hat_one[rows] + got[rows]) + vector(0))
        hat, scale = norm_rows(values)
        hat_one[rows] = hat
        scale_one[rows] = jnp.broadcast_to(scale, (block, lanes))
        normed[full] = (hat * vector(1) + vector(2)).astype(jnp.bfloat16)

    each(count, first_norm)
    copy_n = swap_copy(normed.at[rows_at(mine, half)], normed.at[rows_at(mine, half)], sems, 3, True)
    copy_n.start()
    run(later[5])
    run(ending[0])

    def expand(base):
        def body(index):
            rows = rows_at(base + index // 2 * block, block)
            near = lax.rem(index, 2)
            columns = rows_at(near * width, width)
            expanded = dot(normed[rows], w_wide[near], plain) + jnp.where(near == 0, up_bias[0], up_bias[1])
            cdf = 0.5 * (1.0 + lax.erf(expanded * inv_root_two))
            hidden[rows, columns] = (expanded * cdf).astype(jnp.bfloat16)
            slope[rows, columns] = (cdf + expanded * jnp.exp(-0.5 * expanded * expanded) * inv_root_tau).astype(jnp.bfloat16)

        each(2 * count, body)

    expand(mine)
    copy_n.wait()
    run(ending[1])
    expand(theirs)
    run(ending[2])
    for gather in gathers:
        gather.drain()
    small.drain()

    def lowered(rows):
        return dot(hidden[rows, 0:width], w_long[0], right_turned) + dot(hidden[rows, width : 2 * width], w_long[1], right_turned)

    copy = away(lowered, 1)

    def stay_b(step):
        second_grad[rows_at(step * block, block)] = lowered(rows_at(mine + step * block, block))

    each(count, stay_b)
    copy.wait()
    load_cotangent.wait()

    def second_norm(step):
        rows = rows_at(step * block, block)
        full = rows_at(mine + step * block, block)
        values = normed[full].astype(jnp.float32) + ((second_grad[rows] + got[rows]) + vector(3))
        hat, scale = norm_rows(values)
        out_rows[rows] = (hat * vector(4) + vector(5)).astype(jnp.bfloat16)
        upstream = cotangent[rows].astype(jnp.float32)
        grad = norm_rows_back(upstream, hat, scale, vector(4))
        second_grad[rows] = grad
        second_low[full] = grad.astype(jnp.bfloat16)
        add_sum(3, grad)
        add_sum(4, upstream * hat)
        add_sum(5, upstream)

    each(count, second_norm)
    copy_s = swap_copy(second_low.at[rows_at(mine, half)], second_low.at[rows_at(mine, half)], sems, 4, True)
    copy_s.start()
    near_rows = output.at[rows_at(y * total + mine, half)]
    store_out = pltpu.make_async_copy(out_rows, near_rows, local.at[2])
    store_out.start()
    copy_o = swap_copy(out_rows, near_rows, sems, 5, True)
    copy_o.start()
    copy_p = swap_copy(out_rows, far_out, sems, 6, False)
    copy_p.start()

    def contract(base):
        def body(step):
            rows = rows_at(base + step * block, block)
            inputs = second_low[rows]
            for near in range(2):
                columns = slice(near * width, (near + 1) * width)
                grad = dot(inputs, w_long[near], plain) * slope[rows, columns].astype(jnp.float32)
                add_sum(8 + near, grad)
                slope[rows, columns] = grad.astype(jnp.bfloat16)

        each(count, body)

    contract(mine)
    copy_s.wait()
    contract(theirs)
    expanded_low = slope

    def weight_terms(left, right, target):
        def body(step):
            rows = rows_at(step * block, block)
            for near in range(2):
                target[near, rows] = dot(left[:, rows], right[:, near * width : (near + 1) * width], left_turned).astype(jnp.bfloat16)

        each(width // block, body)

    weight_terms(second_low, hidden, w_long)
    scatters = [
        Scatter(lines, terms, slots, scatter_recv.at[part], scatter_send.at[part], unit, corner)
        for part, (terms, slots, corner) in enumerate((
            (terms_first, slots_narrow.at[0], None), (terms_second, slots_narrow.at[1], None),
            (w_wide, slots_wide.at[0], "x"), (w_long, slots_wide.at[1], "y")))]
    first, second, wide, long = scatters
    long.begin()
    ready = portions(steps_of(merged((0, long.events(grad_down)[1:]), (1, wide.events(grad_up)[1:]))), 15)
    ready = [[]] * (15 - 15) + ready

    def normed_term(rows):
        return dot(expanded_low[rows, 0:width], w_wide[0], right_turned) + dot(expanded_low[rows, width : 2 * width], w_wide[1], right_turned)

    copy = away(normed_term, 2)

    def stay_c(step):
        rows = rows_at(step * block, block)
        second_grad[rows] = second_grad[rows] + normed_term(rows_at(mine + step * block, block))

    each(count, stay_c)

    copy.wait()

    def first_norm_back(step):
        rows = rows_at(step * block, block)
        full = rows_at(mine + step * block, block)
        upstream = second_grad[rows] + got[rows]
        hat = hat_one[rows]
        grad = norm_rows_back(upstream, hat, scale_one[rows][:, 0:1], vector(1))
        second_grad[rows] = grad
        first_low[full] = grad.astype(jnp.bfloat16)
        add_sum(0, grad)
        add_sum(1, upstream * hat)
        add_sum(2, upstream)

    each(count, first_norm_back)
    first_grad = second_grad
    copy_f = swap_copy(first_low.at[rows_at(mine, half)], first_low.at[rows_at(mine, half)], sems, 7, True)
    copy_f.start()
    weight_terms(normed, expanded_low, w_wide)
    wide.begin()
    copy_f.wait()

    def back_out(step):
        rows = rows_at(step * block, block)
        context_grad[rows] = dot(first_low[rows], turned[...], plain).astype(jnp.bfloat16)

    each(blocks, back_out)

    def out_terms(step):
        rows = rows_at(step * block, block)
        out_grad[rows] = dot(first_low[:, rows], context[...], left_turned)

    each(width // block, out_terms)

    lane = lax.broadcasted_iota(jnp.int32, (block, lanes), 1)
    for index in range(blocks):
        rows = slice(index * block, (index + 1) * block)
        stats = jnp.zeros((block, lanes), jnp.float32)
        for pair in range(3):
            product = context_grad[rows, tile(pair)].astype(jnp.float32) * context[rows, tile(pair)].astype(jnp.float32)
            lower = jnp.sum(jnp.where(low, product, 0.0), axis=-1, keepdims=True)
            upper = jnp.sum(jnp.where(low, 0.0, product), axis=-1, keepdims=True)
            stats = jnp.where(lane == 2 * pair, lower, jnp.where(lane == 2 * pair + 1, upper, stats))
        dot_rows[index] = stats.T[0:8]
        log_rows[index] = log_sum[rows].T[0:8]
    packed = hidden

    def columns_of(part, near):
        return slice((2 * near + part) * 3 * lanes, (2 * near + part + 1) * 3 * lanes)

    def back(pair, steps):
        back_pair(pair, query, key, value, context_grad, limit_rows, log_rows, dot_rows, query_acc, key_acc, value_acc, steps)

    query_sums, value_sums = [], []

    def place_pair(pair):
        def body(index, carry):
            rows = rows_at(index * block, block)
            asked = query_acc[rows] * 0.125
            valued = value_acc[rows]
            for which, values in enumerate((asked, key_acc[rows], valued)):
                if pair < 2:
                    packed[rows, pl.ds(2 * pair * 3 * lanes + which * lanes, lanes)] = values.astype(jnp.bfloat16)
                else:
                    packed[rows, pl.ds(3 * lanes + which * lanes, lanes)] = jnp.where(low, values, 0.0).astype(jnp.bfloat16)
                    packed[rows, pl.ds(9 * lanes + which * lanes, lanes)] = jnp.where(low, 0.0, values).astype(jnp.bfloat16)
            return carry[0] + total_rows(asked), carry[1] + total_rows(valued)

        empty = jnp.zeros((1, lanes), jnp.float32)
        asked_sum, valued_sum = lax.fori_loop(0, blocks, body, (empty, empty))
        query_sums.append(asked_sum)
        value_sums.append(valued_sum)

    def first_terms(near):
        def body(step):
            rows = rows_at(step * block, block)
            terms_first[near, rows] = dot(tokens[:, rows], packed[:, columns_of(0, near)], left_turned).astype(jnp.bfloat16)

        each(width // block, body)

    def second_terms(step):
        rows = rows_at(step * block, block)
        outs = [out_grad[rows, tile(pair)] for pair in range(3)]
        homes = (
            (swapped(outs[0]), outs[0], swapped(outs[2])),
            (outs[1], swapped(outs[1]), swapped(outs[2])),
        )
        for near in range(2):
            grads = dot(tokens[:, rows], packed[:, columns_of(1, near)], left_turned)
            for which in range(3):
                values, home = grads[:, tile(which)], homes[near][which]
                values = jnp.where(low, values, home) if near == 0 else jnp.where(low, home, values)
                terms_second[near, rows, tile(which)] = values.astype(jnp.bfloat16)

    run(ready[0])
    back(0, ready[1:5])
    place_pair(0)
    first_terms(0)
    run(ready[5])
    copy_p.wait()
    far_rows = output.at[rows_at((1 - y) * total + mine, half)]
    copy_q = swap_copy(far_out, far_rows, sems, 8, True)
    copy_q.start()
    store_far = pltpu.make_async_copy(far_out, far_rows, local.at[1])
    store_far.start()
    back(1, ready[6:10])
    place_pair(1)
    first_terms(1)
    first.begin()
    run(ready[10])
    back(2, ready[11:15])
    place_pair(2)
    each(width // block, second_terms)
    second.begin()
    tail = portions(steps_of(merged((0, first.events(grad_one)[1:]), (1, second.events(grad_two)[1:]))), 5)
    run(tail[0])
    narrow = width // 4

    def columns(near, which, rows):
        spot = rows_at((2 * near + which) * narrow, narrow)
        result = dot(packed[rows, columns_of(0, 0)], w_first[0, spot], right_turned)
        result = result + dot(packed[rows, columns_of(1, 0)], w_second[0, spot], right_turned)
        result = result + dot(packed[rows, columns_of(0, 1)], w_first[1, spot], right_turned)
        return result + dot(packed[rows, columns_of(1, 1)], w_second[1, spot], right_turned)

    def pick(values, near, which):
        pieces = [values[:, i * narrow : (i + 1) * narrow] for i in range(4)]
        found = [jnp.where(which == 0, pieces[2 * i], pieces[2 * i + 1]) for i in range(2)]
        return found[near] if isinstance(near, int) else jnp.where(near == 0, found[0], found[1])

    def kept(index, near, which):
        rows = rows_at(lax.rem(index, count) * block, block)
        return jnp.where(index // count == core, pick(first_grad[rows], near, which), 0.0)

    def across(index):
        rows = rows_at(index * block, block)
        for near in range(2):
            turn_sent[near, rows] = (columns(near, 1 - core, rows) + kept(index, near, 1 - core)).astype(jnp.bfloat16)

    each(blocks, across)
    copy_t = swap_copy(turn_sent, turn_got, sems, 9, True)
    copy_t.start()
    run(tail[1])
    copy_t.wait()

    def finish(near, index):
        rows = rows_at(index * block, block)
        return columns(near, core, rows) + turn_got[near, rows].astype(jnp.float32) + kept(index, near, core)

    def far(index):
        far_sent[:, rows_at(index * block, block)] = finish(1 - y, index).T.astype(jnp.bfloat16)

    each(blocks, far)
    copy_u = swap_copy(far_sent, input_far, sems, 10, False)
    copy_u.start()
    run(tail[2])

    nothing = jnp.zeros((1, lanes), jnp.float32)
    for near in range(2):
        sums[0, 6 + near : 7 + near] = jnp.concatenate(
            [query_sums[near], nothing, value_sums[near], query_sums[2], nothing, value_sums[2]], axis=1)

    def vector_step(step, target):
        copy = pltpu.make_async_remote_copy(
            src_ref=sums.at[step], dst_ref=vec_got.at[step], send_sem=sems.at[0, 11 + step], recv_sem=sems.at[1, 11 + step],
            device_id=target, device_id_type=MESH)
        copy.start()
        return copy

    copy = vector_step(0, device(z, x, y, 1 - core))

    def close(index):
        input_own[:, rows_at(index * block, block)] = finish(y, index).T

    each(blocks, close)
    copy.wait()
    shared = lax.broadcasted_iota(jnp.int32, vec_got.shape[1:], 0) < 6
    sums[1] = sums[0] + jnp.where(shared, vec_got[0], 0.0)
    copy = vector_step(1, device(z, 1 - x, y, core))
    run(tail[3])
    copy.wait()
    sums[2] = sums[1] + vec_got[1]
    copy = vector_step(2, device(z, x, 1 - y, core))
    copy.wait()
    line_got[z] = sums[2] + vec_got[2]

    def line_copy(there, arrives):
        return pltpu.make_async_remote_copy(
            src_ref=line_got.at[z], dst_ref=line_got.at[arrives], send_sem=sems.at[0, 16 + there], recv_sem=sems.at[1, 16 + arrives],
            device_id=device(there, x, y, core), device_id_type=MESH)

    others = [(there, ok) for k in range(1, lines) for there, ok in ((z + k, z + k < lines), (z - k, z - k >= 0))]
    for there, ok in others:
        pl.when(ok)(lambda: line_copy(there, z).start())
    run(tail[4])
    for there, ok in others:
        pl.when(ok)(lambda: line_copy(there, there).wait())
    result = line_got[0]
    for line in range(1, lines):
        result = result + line_got[line]
    own_sums[...] = result
    store_out.wait()
    store_far.wait()
    for copy in (copy_o, copy_q, copy_u):
        copy.wait()
    for scatter in scatters:
        scatter.drain()


def close_kernel(
    unit, output_in, input_own, input_far, grad_one, grad_two, grad_up, grad_down, own_sums,
    output, input_grad, g_query, g_key, g_value, g_out, g_up, g_down, gb_query, gb_value, gb_up, *rest,
):
    vector_grads, (staged, sem) = rest[:-2], rest[-2:]
    z, x, y, core = place()
    own = lax.axis_index("dp")
    total = input_own.shape[1]
    half = total // 2
    loads = [pltpu.make_async_copy(output_in.at[i * half : (i + 1) * half], staged.at[i], sem.at[i]) for i in range(4)]
    stores = [pltpu.make_async_copy(staged.at[i], output.at[i * half : (i + 1) * half], sem.at[4 + i]) for i in range(4)]
    for copy in loads:
        copy.start()
    input_grad[:, rows_at(y * total, total)] = input_own[...]
    input_grad[:, rows_at((1 - y) * total, total)] = input_far[...].astype(jnp.float32)

    for load, store in zip(loads, stores):
        load.wait()
        store.start()

    def third(values, which):
        start = which * 2 * HEAD
        return jnp.where(y == 0, values[:, start : start + HEAD], values[:, start + HEAD : start + 2 * HEAD])

    def free(values, which):
        start = which * 2 * HEAD
        return jnp.where(y == 0, values[:, start + HEAD : start + 2 * HEAD], values[:, start : start + HEAD])

    one, two = grad_one[...], grad_two[...]
    for which, target in enumerate((g_query, g_key, g_value)):
        target[:, 0 : 2 * HEAD] = one[:, tile(which)]
        target[:, 2 * HEAD : 3 * HEAD] = third(two, which)
    for which in range(3):
        g_out[which * HEAD : (which + 1) * HEAD] = free(two, which).T
    g_up[...] = grad_up[...]
    g_down[...] = grad_down[...]
    sums = own_sums[...]
    rows = jnp.where(y == 0, sums[6:7], sums[7:8])
    for which, target in ((0, gb_query), (2, gb_value)):
        target[:, 0 : 2 * HEAD] = rows[:, tile(which)]
        target[:, 2 * HEAD : 3 * HEAD] = third(rows[:, 3 * lanes :], which)
    gb_up[...] = jnp.where(y == 0, sums[8:9], sums[9:10])
    kept = jnp.zeros((8, unit), jnp.float32)
    for part in range(sums.shape[1] // unit):
        kept = jnp.where(own == part, sums[0:8, part * unit : (part + 1) * unit], kept)
    for index, target in enumerate(vector_grads):
        target[...] = kept[index : index + 1]
    for copy in stores:
        copy.wait()


def fits(mesh, tokens, seq_lens, block_sizes, w_query, *others):
    unit, columns = w_query.shape
    w_up = others[8]
    return (
        mesh.shape["tensor"] == 4
        and mesh.shape["dp"] % 4 == 0
        and seq_lens.shape[0] == 2
        and tokens.shape[0] % (4 * block) == 0
        and columns == 3 * HEAD
        and unit % 16 == 0
        and unit <= lanes
        and unit * mesh.shape["dp"] == tokens.shape[1] == 12 * HEAD == w_up.shape[1]
    )


def on_device_fast(lines, tokens, seq_lens, block_sizes, w_query, b_query, w_key, w_value, b_value, w_out, b_out,
                   gain_one, shift_one, w_up, b_up, w_down, b_down, gain_two, shift_two, cotangent):
    bf16, f32 = jnp.bfloat16, jnp.float32
    total, width = tokens.shape[0] // 2, tokens.shape[1]
    half, pairs = total // 2, width // 2
    unit = w_query.shape[0]
    slots = lines * 4
    blocks = total // block
    dma = pltpu.SemaphoreType.DMA
    shape = jax.ShapeDtypeStruct
    anywhere, on_chip = pl.BlockSpec(memory_space=pl.ANY), pl.BlockSpec(memory_space=pltpu.VMEM)
    scalars = pl.BlockSpec(memory_space=pltpu.SMEM)
    pair, single = slice(0, 2 * HEAD), slice(2 * HEAD, 3 * HEAD)
    zero, zeros = jnp.zeros((HEAD,), bf16), jnp.zeros((2 * HEAD,), bf16)
    near = jnp.concatenate([b_query[pair], zeros, b_value[pair], b_query[single], zero, zeros, b_value[single], zero])
    far = jnp.concatenate([b_query[pair], zeros, b_value[pair], zero, b_query[single], zeros, zero, b_value[single]])
    vectors = jnp.stack([b_out, gain_one, shift_one, b_down, gain_two, shift_two])
    extra = jnp.concatenate([
        jnp.where(lax.axis_index("tensor") // 2 == 0, near, far)[None], b_up[None],
        jnp.pad(vectors, ((0, 0), (0, width - unit))), jnp.zeros((8, width), bf16)])
    raw = pl.pallas_call(
        functools.partial(layer_kernel, lines),
        out_shape=(
            shape((2 * total, width), bf16), shape((width // 4, total), f32), shape((width // 4, total), bf16),
            shape((unit, pairs), f32), shape((unit, pairs), f32), shape((unit, width), f32), shape((unit, width), f32),
            shape((16, width), f32)),
        in_specs=[anywhere] * 2 + [scalars] * 2 + [on_chip] * 7,
        out_specs=(anywhere,) + (on_chip,) * 7,
        scratch_shapes=[
            pltpu.VMEM((total, width), bf16), pltpu.VMEM((half, width), bf16),
            pltpu.VMEM((2, width, pairs), bf16), pltpu.VMEM((2, width, pairs), bf16),
            pltpu.VMEM((2, width, width), bf16), pltpu.VMEM((2, width, width), bf16),
            pltpu.VMEM((2, lines * 2 * 16, width), bf16), pltpu.VMEM((16, width), f32),
            *[pltpu.VMEM((total, pairs), bf16)] * 4, pltpu.VMEM((total, lanes), f32),
            pltpu.VMEM((total, 1), jnp.int32), pltpu.VMEM((blocks, 8, block), jnp.int32),
            *[pltpu.VMEM((blocks, 8, block), f32)] * 2,
            pltpu.VMEM((width, pairs), bf16), *[pltpu.VMEM((half, width), f32)] * 3, pltpu.VMEM((half, lanes), f32),
            pltpu.VMEM((total, width), bf16), *[pltpu.VMEM((total, 2 * width), bf16)] * 2,
            pltpu.VMEM((half, width), f32), *[pltpu.VMEM((total, width), bf16)] * 2,
            pltpu.VMEM((total, pairs), bf16), pltpu.VMEM((width, pairs), f32), *[pltpu.VMEM((half, width), bf16)] * 2,
            *[pltpu.VMEM((total, lanes), f32)] * 3, *[pltpu.VMEM((2, width, pairs), bf16)] * 2,
            pltpu.VMEM((2, 5, lines, unit, pairs), bf16), pltpu.VMEM((2, 7, lines, unit, width), bf16),
            *[pltpu.VMEM((3, 16, width), f32)] * 2, pltpu.VMEM((lines, 16, width), f32),
            *[pltpu.VMEM((2, total, width // 4), bf16)] * 2, pltpu.VMEM((width // 4, total), bf16),
            dma((3,)), dma((4, slots)), dma((4, 4, slots)), dma((slots,)), dma((4, slots)),
            dma((4, 7, lines)), dma((4, 7, lines)), dma((2, 16 + lines))],
        compiler_params=pltpu.CompilerParams(collective_id=0, has_side_effects=True, vmem_limit_bytes=62 * 2**20),
    )(tokens, cotangent, seq_lens, block_sizes, w_query, w_key, w_value, w_out, w_up, w_down.T, extra)

    small = [3 * HEAD, 3 * HEAD, width] + [unit] * 6
    done = pl.pallas_call(
        functools.partial(close_kernel, unit),
        out_shape=(
            shape((2 * total, width), bf16), shape((width // 4, 2 * total), f32),
            *[shape((unit, 3 * HEAD), f32)] * 3, shape((3 * HEAD, unit), f32), shape((unit, width), f32), shape((unit, width), f32),
            *[shape((1, size), f32) for size in small]),
        in_specs=[anywhere] + [on_chip] * 7,
        out_specs=(anywhere,) + (on_chip,) * 16,
        scratch_shapes=[pltpu.VMEM((4, half, width), bf16), dma((8,))],
        compiler_params=pltpu.CompilerParams(vmem_limit_bytes=62 * 2**20),
    )(*raw)
    output, input_grad, g_query, g_key, g_value, g_out, g_up, g_down = done[:8]
    gb_query, gb_value, gb_up, gb_out, g_gain_one, g_shift_one, gb_down, g_gain_two, g_shift_two = [array.reshape(-1) for array in done[8:]]
    return (output, input_grad.T, g_query, gb_query, g_key, g_value, gb_value, g_out, gb_out, g_gain_one, g_shift_one,
            g_up, gb_up, g_down.T, gb_down, g_gain_two, g_shift_two)


def solution(mesh):
    in_specs = (
        P("dp", None),
        P("dp"),
        P("dp"),
        P("dp", "tensor"),
        P("tensor"),
        P("dp", "tensor"),
        P("dp", "tensor"),
        P("tensor"),
        P("tensor", "dp"),
        P("dp"),
        P("dp"),
        P("dp"),
        P("dp", "tensor"),
        P("tensor"),
        P("tensor", "dp"),
        P("dp"),
        P("dp"),
        P("dp"),
        P("dp", None),
    )
    out_specs = (
        P("dp", None),
        P("dp", "tensor"),
        P("dp", "tensor"),
        P("tensor"),
        P("dp", "tensor"),
        P("dp", "tensor"),
        P("tensor"),
        P("tensor", "dp"),
        P("dp"),
        P("dp"),
        P("dp"),
        P("dp", "tensor"),
        P("tensor"),
        P("tensor", "dp"),
        P("dp"),
        P("dp"),
        P("dp"),
    )
    lines = mesh.shape["dp"] // 2

    def on_device(*arrays):
        if fits(mesh, *arrays):
            return on_device_fast(lines, *arrays)
        return on_device_plain(*arrays)

    return jax.shard_map(
        on_device, mesh=mesh, in_specs=in_specs, out_specs=out_specs, check_vma=False
    )
```

```python
import functools

import jax
import jax.numpy as jnp
from jax import lax
from jax.experimental import pallas as pl
from jax.experimental.pallas import tpu as pltpu
from jax.sharding import PartitionSpec as P

HEAD = 64
MESH = pl.DeviceIdType.MESH

norm_epsilon = 1e-12
inv_root_two = 0.7071067811865476
inv_root_tau = 0.3989422804014327
masked_score = -1000000000.0


def matmul(first_operand, second_operand):
    return jnp.dot(first_operand, second_operand, preferred_element_type=jnp.float32)


def contract_rows(first_operand, second_operand):
    return lax.dot_general(
        first_operand, second_operand, (((0,), (0,)), ((), ())), preferred_element_type=jnp.float32
    )


def contract_cols(first_operand, second_operand):
    return lax.dot_general(
        first_operand, second_operand, (((1,), (1,)), ((), ())), preferred_element_type=jnp.float32
    )


def norm_forward(row_values, gain_row, offset_row):
    row_mean = jnp.mean(row_values, axis=-1, keepdims=True)
    centred = row_values - row_mean
    variance = jnp.mean(centred * centred, axis=-1, keepdims=True)
    inv_scale = lax.rsqrt(variance + norm_epsilon)
    normal_rows = centred * inv_scale
    return (normal_rows * gain_row + offset_row, normal_rows, inv_scale)


def norm_backward(upstream, normal_rows, inv_scale, gain_row):
    scaled = upstream * gain_row
    row_grad = inv_scale * (
        scaled
        - jnp.mean(scaled, axis=-1, keepdims=True)
        - normal_rows * jnp.mean(scaled * normal_rows, axis=-1, keepdims=True)
    )
    return (row_grad, jnp.sum(upstream * normal_rows, axis=0), jnp.sum(upstream, axis=0))


def allowed_mask(first_row, row_total, key_total, seq_length, block_size):
    row_pos = first_row + lax.broadcasted_iota(jnp.int32, (row_total, key_total), 0)
    key_pos = lax.broadcasted_iota(jnp.int32, (row_total, key_total), 1)
    return (key_pos // block_size <= row_pos // block_size) & (key_pos < seq_length)


def attend(query_rows, key_rows, value_rows, seq_length, block_size):
    row_total, local_heads, head_size = query_rows.shape
    block_rows = min(512, row_total)
    block_count = row_total // block_rows
    query_blocks = query_rows.reshape(block_count, block_rows, local_heads, head_size)

    def one_block(block_pair):
        block_index, query_block = block_pair
        scores = jnp.einsum(
            "qhd,khd->hqk", query_block, key_rows, preferred_element_type=jnp.float32
        )
        allowed = allowed_mask(
            block_index * block_rows, block_rows, row_total, seq_length, block_size
        )
        scores = jnp.where(allowed[None], scores, masked_score)
        top_score = jnp.max(scores, axis=-1, keepdims=True)
        exp_scores = jnp.exp(scores - top_score)
        exp_total = jnp.sum(exp_scores, axis=-1, keepdims=True)
        probabilities = (exp_scores / exp_total).astype(jnp.bfloat16)
        context = jnp.einsum(
            "hqk,khd->qhd", probabilities, value_rows, preferred_element_type=jnp.float32
        )
        return (context.astype(jnp.bfloat16), top_score[..., 0] + jnp.log(exp_total[..., 0]))

    contexts, log_sums = lax.map(
        one_block, (jnp.arange(block_count, dtype=jnp.int32), query_blocks)
    )
    return (contexts.reshape(row_total, local_heads * head_size), log_sums)


def attend_back(query_rows, key_rows, value_rows, context_grad, log_sums, seq_length, block_size):
    row_total, local_heads, head_size = query_rows.shape
    block_rows = min(512, row_total)
    block_count = row_total // block_rows
    query_blocks = query_rows.reshape(block_count, block_rows, local_heads, head_size)
    grad_blocks = context_grad.reshape(block_count, block_rows, local_heads, head_size)

    def one_block(running, block_pack):
        key_grad, value_grad = running
        block_index, query_block, grad_block, log_block = block_pack
        scores = jnp.einsum(
            "qhd,khd->hqk", query_block, key_rows, preferred_element_type=jnp.float32
        )
        allowed = allowed_mask(
            block_index * block_rows, block_rows, row_total, seq_length, block_size
        )
        probabilities = jnp.where(allowed[None], jnp.exp(scores - log_block[..., None]), 0.0)
        prob_grad = jnp.einsum(
            "qhd,khd->hqk", grad_block, value_rows, preferred_element_type=jnp.float32
        )
        row_dot = jnp.sum(prob_grad * probabilities, axis=-1, keepdims=True)
        score_grad = (probabilities * (prob_grad - row_dot)).astype(jnp.bfloat16)
        query_grad = jnp.einsum(
            "hqk,khd->qhd", score_grad, key_rows, preferred_element_type=jnp.float32
        )
        key_grad = key_grad + jnp.einsum(
            "hqk,qhd->khd", score_grad, query_block, preferred_element_type=jnp.float32
        )
        value_grad = value_grad + jnp.einsum(
            "hqk,qhd->khd",
            probabilities.astype(jnp.bfloat16),
            grad_block,
            preferred_element_type=jnp.float32,
        )
        return ((key_grad, value_grad), query_grad)

    empty = jnp.zeros((row_total, local_heads, head_size), jnp.float32)
    (key_grad, value_grad), query_grads = lax.scan(
        one_block,
        (empty, empty),
        (jnp.arange(block_count, dtype=jnp.int32), query_blocks, grad_blocks, log_sums),
    )
    width = local_heads * head_size
    return (
        query_grads.reshape(row_total, width),
        key_grad.reshape(row_total, width),
        value_grad.reshape(row_total, width),
    )


def on_device_plain(
    tokens,
    seq_lens,
    block_sizes,
    w_query,
    b_query,
    w_key,
    w_value,
    b_value,
    w_out,
    b_out,
    gain_one,
    shift_one,
    w_up,
    b_up,
    w_down,
    b_down,
    gain_two,
    shift_two,
    cotangent,
):
    micro_total = seq_lens.shape[0]
    seq_rows = tokens.shape[0] // micro_total
    head_cols = w_query.shape[1]
    local_heads = head_cols // HEAD
    model_width = tokens.shape[1]
    own_cols = model_width // lax.axis_size("tensor")
    column_start = lax.axis_index("tensor") * own_cols
    query_bias = b_query.astype(jnp.float32)
    value_bias = b_value.astype(jnp.float32)
    up_bias = b_up.astype(jnp.float32)
    owned = (
        w_query,
        w_key,
        w_value,
        w_out,
        w_up,
        w_down,
        b_out,
        gain_one,
        shift_one,
        b_down,
        gain_two,
        shift_two,
    )

    def shaped(flat_rows):
        return flat_rows.reshape(seq_rows, local_heads, HEAD)

    layer_outputs = []
    input_grads = []
    totals = None
    for micro_index in range(micro_total):
        rows_in = tokens[micro_index * seq_rows : (micro_index + 1) * seq_rows]
        upstream = cotangent[micro_index * seq_rows : (micro_index + 1) * seq_rows].astype(
            jnp.float32
        )
        seq_length = seq_lens[micro_index]
        block_size = block_sizes[micro_index]
        forward_set = (
            lax.all_gather(owned[0], "dp", axis=0, tiled=True),
            lax.all_gather(owned[1], "dp", axis=0, tiled=True),
            lax.all_gather(owned[2], "dp", axis=0, tiled=True),
            lax.all_gather(owned[3], "dp", axis=1, tiled=True),
            lax.all_gather(owned[4], "dp", axis=0, tiled=True),
            lax.all_gather(owned[5], "dp", axis=1, tiled=True),
            lax.all_gather(owned[6], "dp", axis=0, tiled=True),
            lax.all_gather(owned[7], "dp", axis=0, tiled=True),
            lax.all_gather(owned[8], "dp", axis=0, tiled=True),
            lax.all_gather(owned[9], "dp", axis=0, tiled=True),
            lax.all_gather(owned[10], "dp", axis=0, tiled=True),
            lax.all_gather(owned[11], "dp", axis=0, tiled=True),
        )
        (
            full_query,
            full_key,
            full_value,
            full_out,
            full_up,
            full_down,
            full_out_bias,
            full_gain_one,
            full_shift_one,
            full_down_bias,
            full_gain_two,
            full_shift_two,
        ) = forward_set
        out_bias = full_out_bias.astype(jnp.float32)
        down_bias = full_down_bias.astype(jnp.float32)
        first_gain = full_gain_one.astype(jnp.float32)
        first_shift = full_shift_one.astype(jnp.float32)
        second_gain = full_gain_two.astype(jnp.float32)
        second_shift = full_shift_two.astype(jnp.float32)
        query_rows = ((matmul(rows_in, full_query) + query_bias) * 0.125).astype(jnp.bfloat16)
        key_rows = matmul(rows_in, full_key).astype(jnp.bfloat16)
        value_rows = (matmul(rows_in, full_value) + value_bias).astype(jnp.bfloat16)
        context, log_sums = attend(
            shaped(query_rows), shaped(key_rows), shaped(value_rows), seq_length, block_size
        )
        attended = lax.psum(matmul(context, full_out), "tensor") + out_bias
        first_norm, first_hat, first_scale = norm_forward(
            rows_in.astype(jnp.float32) + attended, first_gain, first_shift
        )
        normed = first_norm.astype(jnp.bfloat16)
        expanded = matmul(normed, full_up) + up_bias
        normal_cdf = 0.5 * (1.0 + lax.erf(expanded * inv_root_two))
        hidden = (expanded * normal_cdf).astype(jnp.bfloat16)
        lowered = lax.psum(matmul(hidden, full_down), "tensor") + down_bias
        second_norm, second_hat, second_scale = norm_forward(
            normed.astype(jnp.float32) + lowered, second_gain, second_shift
        )
        layer_outputs.append(second_norm.astype(jnp.bfloat16))
        second_grad, grad_gain_two, grad_shift_two = norm_backward(
            upstream, second_hat, second_scale, second_gain
        )
        down_bias_grad = jnp.sum(second_grad, axis=0)
        second_low = second_grad.astype(jnp.bfloat16)
        down_grad = contract_rows(hidden, second_low)
        hidden_grad = contract_cols(second_low, full_down)
        expanded_grad = hidden_grad * (
            normal_cdf + expanded * jnp.exp(-0.5 * expanded * expanded) * inv_root_tau
        )
        up_bias_grad = jnp.sum(expanded_grad, axis=0)
        expanded_low = expanded_grad.astype(jnp.bfloat16)
        up_grad = contract_rows(normed, expanded_low)
        normed_grad = lax.psum(contract_cols(expanded_low, full_up), "tensor") + second_grad
        first_grad, grad_gain_one, grad_shift_one = norm_backward(
            normed_grad, first_hat, first_scale, first_gain
        )
        out_bias_grad = jnp.sum(first_grad, axis=0)
        first_low = first_grad.astype(jnp.bfloat16)
        out_grad = contract_rows(context, first_low)
        context_grad = contract_cols(first_low, full_out).astype(jnp.bfloat16)
        query_grad, key_grad, value_grad = attend_back(
            shaped(query_rows),
            shaped(key_rows),
            shaped(value_rows),
            shaped(context_grad),
            log_sums,
            seq_length,
            block_size,
        )
        query_grad = query_grad * 0.125
        query_bias_grad = jnp.sum(query_grad, axis=0)
        value_bias_grad = jnp.sum(value_grad, axis=0)
        query_low = query_grad.astype(jnp.bfloat16)
        key_low = key_grad.astype(jnp.bfloat16)
        value_low = value_grad.astype(jnp.bfloat16)
        query_w_grad = contract_rows(rows_in, query_low)
        key_w_grad = contract_rows(rows_in, key_low)
        value_w_grad = contract_rows(rows_in, value_low)
        input_term = (
            contract_cols(query_low, full_query)
            + contract_cols(key_low, full_key)
            + contract_cols(value_low, full_value)
        )
        own_grad = lax.psum_scatter(
            input_term.astype(jnp.bfloat16), "tensor", scatter_dimension=1, tiled=True
        ).astype(jnp.float32)
        input_grads.append(
            own_grad + lax.dynamic_slice_in_dim(first_grad, column_start, own_cols, 1)
        )
        terms = (
            query_w_grad,
            query_bias_grad,
            key_w_grad,
            value_w_grad,
            value_bias_grad,
            out_grad,
            out_bias_grad,
            grad_gain_one,
            grad_shift_one,
            up_grad,
            up_bias_grad,
            down_grad,
            down_bias_grad,
            grad_gain_two,
            grad_shift_two,
        )
        if totals is None:
            totals = terms
        else:
            totals = tuple((running + addend for running, addend in zip(totals, terms)))
    summed = (
        lax.psum_scatter(totals[0], "dp", scatter_dimension=0, tiled=True),
        lax.psum_scatter(totals[2], "dp", scatter_dimension=0, tiled=True),
        lax.psum_scatter(totals[3], "dp", scatter_dimension=0, tiled=True),
        lax.psum_scatter(totals[5], "dp", scatter_dimension=1, tiled=True),
        lax.psum_scatter(totals[9], "dp", scatter_dimension=0, tiled=True),
        lax.psum_scatter(totals[11], "dp", scatter_dimension=1, tiled=True),
        lax.psum_scatter(totals[6], "dp", scatter_dimension=0, tiled=True),
        lax.psum_scatter(totals[7], "dp", scatter_dimension=0, tiled=True),
        lax.psum_scatter(totals[8], "dp", scatter_dimension=0, tiled=True),
        lax.psum_scatter(totals[12], "dp", scatter_dimension=0, tiled=True),
        lax.psum_scatter(totals[13], "dp", scatter_dimension=0, tiled=True),
        lax.psum_scatter(totals[14], "dp", scatter_dimension=0, tiled=True),
    )
    bias_sums = lax.psum((totals[1], totals[4], totals[10]), "dp")
    return (
        jnp.concatenate(layer_outputs, 0),
        jnp.concatenate(input_grads, 0),
        summed[0],
        bias_sums[0],
        summed[1],
        summed[2],
        bias_sums[1],
        summed[3],
        summed[6],
        summed[7],
        summed[8],
        summed[4],
        bias_sums[2],
        summed[5],
        summed[9],
        summed[10],
        summed[11],
    )


def place():
    dp = lax.axis_index("dp")
    tensor = lax.axis_index("tensor")
    return dp // 2, dp % 2, tensor // 2, tensor % 2


def device(z, x, y, core):
    return (z * 2 + x, y * 2 + core)


def when(ok, body):
    if ok is None:
        body()
    else:
        pl.when(ok)(body)


def both(*conditions):
    result = None
    for condition in conditions:
        if condition is not None:
            result = condition if result is None else result & condition
    return result


def greet(lines):
    z, x, y, core = place()
    barrier = pltpu.get_barrier_semaphore()

    def signal(target):
        pl.semaphore_signal(barrier, inc=1, device_id=target, device_id_type=MESH)

    signal(device(z, 1 - x, y, core))
    signal(device(z, x, 1 - y, core))
    signal(device(z, x, y, 1 - core))
    for k in range(1, lines):
        pl.when(z >= k)(lambda: signal(device(z - k, x, y, core)))
        pl.when(z + k < lines)(lambda: signal(device(z + k, x, y, core)))
    pl.semaphore_wait(barrier, 3 + lines - 1)


class Mover:
    def __init__(self, lines, array, recv_sem, send_sem, rows, corner):
        self.lines, self.array, self.recv_sem, self.send_sem = lines, array, recv_sem, send_sem
        self.rows, self.corner = rows, corner
        self.here = place()
        self.sent = []

    def owner(self, k, dx, dy):
        z, x, y, core = self.here
        return z + k, (1 - x if dx else x), (1 - y if dy else y)

    def start(self, k, dx, dy):
        z, x, y = self.owner(k, dx, dy)
        return y, pl.ds(pl.multiple_of((z * 2 + x) * self.rows, self.rows), self.rows)

    def view(self, k, dx, dy):
        return self.array.at[self.start(k, dx, dy)]

    def there(self, k):
        z = self.here[0]
        if k == 0:
            return None
        return z + k < self.lines if k > 0 else z + k >= 0

    def target(self, way):
        z, x, y, core = self.here
        moved = {"up": (z + 1, x, y), "down": (z - 1, x, y), "x": (z, 1 - x, y), "y": (z, x, 1 - y)}[way]
        return device(*moved, core)

    def allowed(self, k, way, parity):
        z = self.here[0]
        line = {"up": self.there(1), "down": self.there(-1)}.get(way)
        even = None if parity is None else (z + k) % 2 == parity
        return both(self.there(k), line, even)

    def send(self, k, dx, dy, way, parity=None, kind=None):
        when(self.allowed(k, way, parity), lambda: self.copy(k, dx, dy, way, kind).start())
        self.sent.append((k, dx, dy, way, parity, kind))

    def drain(self):
        for k, dx, dy, way, parity, kind in self.sent:
            when(self.allowed(k, way, parity), lambda: self.copy(k, dx, dy, way, kind).wait_send())


class Gather(Mover):
    def copy(self, k, dx, dy, way, kind=None):
        z, x, y = self.owner(k, dx, dy)
        index = y * self.lines * 2 + z * 2 + x
        return pltpu.make_async_remote_copy(
            src_ref=self.view(k, dx, dy), dst_ref=self.view(k, dx, dy),
            send_sem=self.send_sem.at[("up", "down", "x", "y").index(way), index], recv_sem=self.recv_sem.at[index],
            device_id=self.target(way), device_id_type=MESH)

    def take(self, k, dx, dy):
        when(self.there(k), lambda: self.copy(k, dx, dy, "x").wait_recv())

    def begin(self):
        for way in ("x", "y", "up", "down"):
            self.send(0, 0, 0, way)

    def planes(self, k):
        self.take(k, 1, 0)
        self.take(k, 0, 1)
        if self.corner is None:
            self.send(k, 1, 0, "y", 1)
            self.send(k, 0, 1, "x", 0)
        elif k == 0:
            self.send(0, *((1, 0) if self.corner == "y" else (0, 1)), self.corner)

    def column(self, k, dx=0, dy=0):
        self.take(k, dx, dy)
        self.send(k, dx, dy, "up" if k < 0 else "down")
        if not dx:
            self.send(k, 0, 0, "x")
            self.send(k, 0, 0, "y")

    def opposite(self, k):
        if k == 0:
            self.take(0, 1, 1)
            self.send(0, 1, 1, "up")
            self.send(0, 1, 1, "down")
        else:
            self.column(k, 1, 1)

    def events(self):
        last = self.lines - 1
        found = [(0, self.begin)]
        for k in range(1, self.lines):
            found += [(k, lambda s=s: self.column(s)) for s in (-k, k)]
            found += [(k, lambda s=s: self.planes(s)) for s in ((0,) if k == 1 else (1 - k, k - 1))]
            if self.corner is not None:
                found += [(k + 0.5, lambda s=s: self.opposite(s)) for s in ((0,) if k == 1 else (1 - k, k - 1))]
        found += [(self.lines, lambda s=s: self.planes(s)) for s in (-last, last)]
        if self.corner is None:
            found += [(self.lines + 1, lambda s=s: self.take(s, 1, 1)) for s in [0] + [s for k in range(1, self.lines) for s in (-k, k)]]
        else:
            found += [(self.lines + 0.5, lambda s=s: self.opposite(s)) for s in (-last, last)]
        return found


class Scatter(Mover):
    def __init__(self, lines, array, slots, recv_sem, send_sem, rows, corner):
        super().__init__(lines, array, recv_sem, send_sem, rows, corner)
        self.slots = slots

    def copy(self, k, dx, dy, way, kind):
        z = self.here[0] + k
        return pltpu.make_async_remote_copy(
            src_ref=self.view(k, dx, dy), dst_ref=self.slots.at[kind, z],
            send_sem=self.send_sem.at[kind, z], recv_sem=self.recv_sem.at[kind, z],
            device_id=self.target(way), device_id_type=MESH)

    def taken(self, k, kind):
        self.copy(k, 0, 0, "x", kind).wait_recv()
        return self.slots[kind, self.here[0] + k].astype(jnp.float32)

    def add(self, k, dx, dy, *kinds):
        start = self.start(k, dx, dy)
        result = self.array[start].astype(jnp.float32)
        for kind in kinds:
            result = result + self.taken(k, kind)
        self.array[start] = result.astype(jnp.bfloat16)

    def distances(self):
        return [s for k in range(self.lines - 1, 0, -1) for s in (k, -k)]

    def begin(self):
        if self.corner is None:
            for k in self.distances() + [0]:
                self.send(k, 1, 1, "x", 0, 0)
                self.send(k, 1, 1, "y", 1, 0)
            for k in self.distances() + [0]:
                self.send(k, 0, 1, "y", 1, 2)
                self.send(k, 1, 0, "x", 0, 1)
            return
        if self.corner == "planes":
            for k in self.distances() + [0]:
                self.send(k, 1, 1, "x", None, 0)
            for k in self.distances() + [0]:
                self.send(k, 1, 0, "x", None, 1)
            return
        for s in (self.lines - 1, 1 - self.lines):
            self.opposite(s)
        for k in self.distances():
            self.send(k, 1, 0, "x", None, 1)
            self.send(k, 0, 1, "y", None, 2)
        if self.corner == "x":
            self.send(0, 1, 0, "x", None, 1)
        else:
            self.send(0, 0, 1, "y", None, 2)

    def opposite(self, k):
        if k == 0:
            pl.when(self.there(-1))(lambda: self.add(0, 1, 1, 5))
            pl.when(self.there(1))(lambda: self.add(0, 1, 1, 6))
            self.send(0, 1, 1, self.corner, None, 0)
            return
        behind, way, kind = (self.there(-1), "up", 5) if k > 0 else (self.there(1), "down", 6)
        pl.when(self.there(k) & behind)(lambda: self.add(k, 1, 1, kind))
        self.send(k, 1, 1, way, None, kind)

    def corners(self, k):
        for dx, dy, way, kind, parity in ((0, 1, "y", 2, 0), (1, 0, "x", 1, 1)):
            if self.corner is None:
                pl.when(both(self.there(k), (self.here[0] + k) % 2 == parity))(lambda: self.add(k, dx, dy, 0))
                self.send(k, dx, dy, way, parity, kind)
            elif self.corner == "planes":
                if dy:
                    when(self.there(k), lambda: self.add(k, dx, dy, 0))
                    self.send(k, dx, dy, way, None, kind)
            elif k == 0 and self.corner != way:
                self.add(0, dx, dy, 0)
                self.send(0, dx, dy, way, None, kind)

    def line(self, k):
        behind, way, kind = (self.there(-1), "up", 3) if k > 0 else (self.there(1), "down", 4)
        pl.when(self.there(k) & behind)(lambda: self.add(k, 0, 0, 1, 2, kind))
        pl.when(self.there(k) & jnp.logical_not(behind))(lambda: self.add(k, 0, 0, 1, 2))
        self.send(k, 0, 0, way, None, kind)

    def own(self, target):
        start = self.start(0, 0, 0)
        target[...] = self.array[start].astype(jnp.float32) + self.taken(0, 1) + self.taken(0, 2)

        def more(kind):
            target[...] += self.taken(0, kind)

        pl.when(self.there(-1))(lambda: more(3))
        pl.when(self.there(1))(lambda: more(4))

    def events(self, target):
        found = [(0, self.begin)]
        if self.corner in (None, "planes"):
            found += [(1, lambda s=s: self.corners(s)) for s in self.distances() + [0]]
            base = 1
        else:
            found += [(self.lines - abs(s), lambda s=s: self.opposite(s)) for s in self.distances() + [0] if abs(s) < self.lines - 1]
            found += [(self.lines + 1, lambda: self.corners(0))]
            base = 1
        found += [(base + self.lines - abs(s), lambda s=s: self.line(s)) for s in self.distances()]
        found += [(self.lines + base + 1, lambda: self.own(target))]
        return sorted(found, key=lambda event: event[0])


def merged(*lists):
    found = [(stage + first, order, step) for order, (first, events) in enumerate(lists) for stage, step in events]
    return sorted(found, key=lambda event: event[:2])


def until_done(events, orders):
    last = max(place for place, event in enumerate(events) if event[1] in orders)
    return [step for _, _, step in events[: last + 1]], events[last + 1 :]


def steps_of(events):
    return [step for _, _, step in events]


def portions(steps, count):
    cuts = [round(i * len(steps) / count) for i in range(count + 1)]
    return [steps[first:last] for first, last in zip(cuts, cuts[1:])]


def run(steps):
    for step in steps:
        step()


lanes = 128
block = 256


def dot(first, second, dims):
    return lax.dot_general(first, second, ((dims[:1], dims[1:]), ((), ())), preferred_element_type=jnp.float32)


plain, right_turned, left_turned = (1, 0), (1, 1), (0, 0)


def rows_at(start, size):
    return pl.ds(pl.multiple_of(start, size), size)


def low_half(rows):
    return lax.broadcasted_iota(jnp.int32, (rows, lanes), 1) < HEAD


def tile(index):
    return slice(index * lanes, (index + 1) * lanes)


def swapped(values):
    return pltpu.roll(values, HEAD, 1)


def each(count, body):
    lax.fori_loop(0, count, lambda index, carry: (body(index), carry)[1], 0)


def norm_rows(values):
    centred = values - jnp.mean(values, axis=-1, keepdims=True)
    variance = jnp.mean(centred * centred, axis=-1, keepdims=True)
    scale = lax.rsqrt(variance + norm_epsilon)
    return centred * scale, scale


def norm_rows_back(upstream, hat, scale, gain):
    scaled = upstream * gain
    return scale * (scaled - jnp.mean(scaled, axis=-1, keepdims=True) - hat * jnp.mean(scaled * hat, axis=-1, keepdims=True))


def total_rows(values):
    return jnp.sum(values, axis=0, keepdims=True)


def swap_copy(src, dst, sems, index, near):
    z, x, y, core = place()
    target = device(z, x, y, 1 - core) if near else device(z, x, 1 - y, core)
    return pltpu.make_async_remote_copy(
        src_ref=src, dst_ref=dst, send_sem=sems.at[0, index], recv_sem=sems.at[1, index],
        device_id=target, device_id_type=MESH)


def pack_weights(y, own, unit, w_query, w_key, w_value, w_out, w_up, w_down, weights):
    here = rows_at(own * unit, unit)
    turned = w_out[...].astype(jnp.float32).T.astype(jnp.bfloat16)
    for which, array in enumerate((w_query, w_key, w_value)):
        weights[0][y, here, tile(which)] = array[:, 0 : 2 * HEAD]
        single = array[:, 2 * HEAD : 3 * HEAD]
        out = turned[:, which * HEAD : (which + 1) * HEAD]
        weights[1][y, here, tile(which)] = jnp.where(
            y == 0, jnp.concatenate([single, out], axis=1), jnp.concatenate([out, single], axis=1))
    weights[2][y, here] = w_up[...]
    weights[3][y, here] = w_down[...]


def turn_out(mixed, target):
    low = low_half(mixed.shape[1])
    first = [mixed[0, :, tile(i)].astype(jnp.float32) for i in range(3)]
    second = [mixed[1, :, tile(i)].astype(jnp.float32) for i in range(3)]
    for pair, values in enumerate((
        jnp.where(low, swapped(first[0]), first[1]),
        jnp.where(low, second[0], swapped(second[1])),
        jnp.where(low, swapped(first[2]), swapped(second[2])),
    )):
        target[:, tile(pair)] = values.astype(jnp.bfloat16)


def spread_vectors(lines, unit, extras, vectors):
    width = vectors.shape[1]
    column = lax.broadcasted_iota(jnp.int32, (lanes, width), 1)
    row = lax.broadcasted_iota(jnp.int32, (lanes, width), 0)

    def add(own, result):
        spot = ((column == row + own * unit) & (row < unit)).astype(jnp.bfloat16)
        return result + dot(extras[0, rows_at(own * 16, 16), 0:lanes], spot, plain)

    result = lax.fori_loop(0, lines * 2, add, jnp.zeros((16, width), jnp.float32))
    vectors[...] = result


def key_limit(places, size, length):
    blocks = jnp.floor((places.astype(jnp.float32) + 0.5) / size.astype(jnp.float32)).astype(jnp.int32)
    return jnp.minimum((blocks + 1) * size, length)


def attend_pair(pair, query, key, value, limit, context, log_sum, steps):
    total = query.shape[0]
    keep = low_half(total)
    nothing = jnp.zeros((), jnp.bfloat16)
    keys = [jnp.where(chosen, key[:, tile(pair)], nothing) for chosen in (keep, ~keep)]
    values = jnp.concatenate([jnp.where(chosen, value[:, tile(pair)], nothing) for chosen in (keep, ~keep)], axis=0)
    lane = lax.broadcasted_iota(jnp.int32, (block, lanes), 1)
    places = lax.broadcasted_iota(jnp.int32, (block, total), 1)

    def one(index):
        for number, group in enumerate(steps):
            if group:
                pl.when(index == number)(functools.partial(run, group))
        rows = rows_at(index * block, block)
        asked = query[rows, tile(pair)]
        allowed = places < limit[rows]
        logs = log_sum[rows] if pair else jnp.zeros((block, lanes), jnp.float32)
        probs = []
        for half in range(2):
            scores = jnp.where(allowed, dot(asked, keys[half], right_turned), masked_score)
            top = jnp.max(scores, axis=-1, keepdims=True)
            grown = jnp.exp(scores - top)
            sums = jnp.sum(grown, axis=-1, keepdims=True)
            probs.append((grown * (1.0 / sums)).astype(jnp.bfloat16))
            logs = jnp.where(lane == 2 * pair + half, top + jnp.log(sums), logs)
        context[rows, tile(pair)] = dot(jnp.concatenate(probs, axis=1), values, plain).astype(jnp.bfloat16)
        log_sum[rows] = logs

    each(total // block, one)


def back_pair(pair, query, key, value, context_grad, limit_rows, log_rows, dot_rows, query_acc, key_acc, value_acc, steps):
    total = query.shape[0]
    keep = low_half(total)
    low = low_half(block)
    nothing = jnp.zeros((), jnp.bfloat16)
    keys = [jnp.where(chosen, key[:, tile(pair)], nothing) for chosen in (keep, ~keep)]
    values = [jnp.where(chosen, value[:, tile(pair)], nothing) for chosen in (keep, ~keep)]
    key_pile = jnp.concatenate(keys, axis=0)
    places = lax.broadcasted_iota(jnp.int32, (total, block), 0)
    value_acc[...] = jnp.zeros_like(value_acc)
    key_acc[...] = jnp.zeros_like(key_acc)

    def halves(rows):
        return jnp.concatenate([jnp.where(low, rows, nothing), jnp.where(low, nothing, rows)], axis=0)

    def one(index):
        for number, group in enumerate(steps):
            if group:
                pl.when(index == number)(functools.partial(run, group))
        rows = rows_at(index * block, block)
        asked = query[rows, tile(pair)]
        wanted = context_grad[rows, tile(pair)]
        allowed = places < limit_rows[index, 0:1]
        all_probs, all_grads = [], []
        for half in range(2):
            head = 2 * pair + half
            grown = jnp.exp(dot(keys[half], asked, right_turned) - log_rows[index, head : head + 1])
            probs = jnp.where(allowed, grown, 0.0)
            prob_grad = dot(values[half], wanted, right_turned)
            all_grads.append((probs * (prob_grad - dot_rows[index, head : head + 1])).astype(jnp.bfloat16))
            all_probs.append(probs.astype(jnp.bfloat16))
        value_acc[...] += dot(jnp.concatenate(all_probs, axis=1), halves(wanted), plain)
        key_acc[...] += dot(jnp.concatenate(all_grads, axis=1), halves(asked), plain)
        query_acc[rows] = dot(jnp.concatenate(all_grads, axis=0), key_pile, left_turned)

    each(total // block, one)


def layer_kernel(
    lines, tokens_all, cotangent_all, seq_lens, block_sizes,
    w_query, w_key, w_value, w_out, w_up, w_down, extra,
    output, input_own, input_far, grad_one, grad_two, grad_up, grad_down, own_sums,
    tokens, cotangent, w_first, w_second, w_wide, w_long, extras, vectors,
    query, key, value, context, log_sum, limit, limit_rows, log_rows, dot_rows,
    turned, sent, got, hat_one, scale_one, normed, slope, hidden, second_grad, second_low, first_low, context_grad, out_grad, out_rows, far_out,
    query_acc, key_acc, value_acc, terms_first, terms_second, slots_narrow, slots_wide,
    sums, vec_got, line_got, turn_sent, turn_got, far_sent,
    local, gather_recv, gather_send, extra_recv, extra_send, scatter_recv, scatter_send, sems,
):
    z, x, y, core = place()
    own = z * 2 + x
    total, width = tokens.shape
    half = total // 2
    mine, theirs = core * half, (1 - core) * half
    unit = w_query.shape[0]
    blocks = total // block
    weights = (w_first, w_second, w_wide, w_long)

    load_tokens = pltpu.make_async_copy(tokens_all.at[rows_at(y * total, total)], tokens, local.at[0])
    load_tokens.start()
    load_cotangent = pltpu.make_async_copy(cotangent_all.at[rows_at(y * total + mine, half)], cotangent, local.at[1])
    load_cotangent.start()
    pack_weights(y, own, unit, w_query, w_key, w_value, w_out, w_up, w_down, weights)
    extras[y, rows_at(own * 16, 16)] = extra[...]
    greet(lines)
    gathers = [
        Gather(lines, weights[part], gather_recv.at[part], gather_send.at[part], unit, corner)
        for part, corner in enumerate((None, None, None, None))]
    small = Gather(lines, extras, extra_recv, extra_send, 16, None)
    first, second, wide, long = gathers
    offsets = (0, 0, 2, 4, 6)
    gathering = merged(*zip(offsets, [mover.events() for mover in (small, *gathers)]))
    opening, gathering = until_done(gathering, (0, 1))
    early, gathering = until_done(gathering, (2,))
    later, gathering = until_done(gathering, (3,))
    early, later, ending = portions(early, 9), portions(later, 6), portions(steps_of(gathering), 3)
    run(opening[:2])
    size, length = block_sizes[y], seq_lens[y]
    limit[...] = key_limit(lax.broadcasted_iota(jnp.int32, (total, 1), 0), size, length)
    for index in range(blocks):
        limit_rows[index] = key_limit(index * block + lax.broadcasted_iota(jnp.int32, (8, block), 1), size, length)
    run(opening[2:])
    load_tokens.wait()
    bias = [extras[near, rows_at(own * 16, 16)].astype(jnp.float32)[0:1] for near in range(2)]
    low = low_half(block)

    def project(index):
        rows = rows_at(index * block, block)
        inputs = tokens[rows]
        for near in range(2):
            found = dot(inputs, w_first[near], plain) + bias[near][:, 0 : 3 * lanes]
            query[rows, tile(near)] = (found[:, tile(0)] * 0.125).astype(jnp.bfloat16)
            key[rows, tile(near)] = found[:, tile(1)].astype(jnp.bfloat16)
            value[rows, tile(near)] = found[:, tile(2)].astype(jnp.bfloat16)

    def project_mixed(index):
        rows = rows_at(index * block, block)
        inputs = tokens[rows]
        found = [dot(inputs, w_second[near], plain) + bias[near][:, 3 * lanes :] for near in range(2)]
        mixed = [jnp.where(low, found[0][:, tile(which)], found[1][:, tile(which)]) for which in range(3)]
        query[rows, tile(2)] = (mixed[0] * 0.125).astype(jnp.bfloat16)
        key[rows, tile(2)] = mixed[1].astype(jnp.bfloat16)
        value[rows, tile(2)] = mixed[2].astype(jnp.bfloat16)

    each(blocks, project)
    def attend(pair, steps):
        attend_pair(pair, query, key, value, limit, context, log_sum, steps)

    attend(0, early[0:4])
    attend(1, early[4:8])
    run(early[8])
    each(blocks, project_mixed)
    attend(2, later[0:4])
    run(later[4])
    turn_out(w_second, turned)
    spread_vectors(lines, unit, extras, vectors)
    vector = lambda index: vectors[2 + index : 3 + index]
    up_bias = [extras[near, rows_at(own * 16, 16)].astype(jnp.float32)[1:2] for near in range(2)]
    sums[0] = jnp.zeros_like(sums.at[0])
    count = half // block

    def add_sum(index, values):
        sums[0, index : index + 1] += total_rows(values)

    def away(term, index):
        def body(step):
            sent[rows_at(step * block, block)] = term(rows_at(theirs + step * block, block))

        each(count, body)
        copy = swap_copy(sent, got, sems, index, True)
        copy.start()
        return copy

    def attended(rows):
        return dot(context[rows], turned[...], right_turned)

    copy = away(attended, 0)

    def stay_a(step):
        hat_one[rows_at(step * block, block)] = attended(rows_at(mine + step * block, block))

    each(count, stay_a)
    copy.wait()

    def first_norm(step):
        rows = rows_at(step * block, block)
        full = rows_at(mine + step * block, block)
        values = tokens[full].astype(jnp.float32) + ((hat_one[rows] + got[rows]) + vector(0))
        hat, scale = norm_rows(values)
        hat_one[rows] = hat
        scale_one[rows] = jnp.broadcast_to(scale, (block, lanes))
        normed[full] = (hat * vector(1) + vector(2)).astype(jnp.bfloat16)

    each(count, first_norm)
    copy_n = swap_copy(normed.at[rows_at(mine, half)], normed.at[rows_at(mine, half)], sems, 3, True)
    copy_n.start()
    run(later[5])
    run(ending[0])

    def expand(base):
        def body(index):
            rows = rows_at(base + index // 2 * block, block)
            near = lax.rem(index, 2)
            columns = rows_at(near * width, width)
            expanded = dot(normed[rows], w_wide[near], plain) + jnp.where(near == 0, up_bias[0], up_bias[1])
            cdf = 0.5 * (1.0 + lax.erf(expanded * inv_root_two))
            hidden[rows, columns] = (expanded * cdf).astype(jnp.bfloat16)
            slope[rows, columns] = (cdf + expanded * jnp.exp(-0.5 * expanded * expanded) * inv_root_tau).astype(jnp.bfloat16)

        each(2 * count, body)

    expand(mine)
    copy_n.wait()
    run(ending[1])
    expand(theirs)
    run(ending[2])
    for gather in gathers:
        gather.drain()
    small.drain()

    def lowered(rows):
        return dot(hidden[rows, 0:width], w_long[0], right_turned) + dot(hidden[rows, width : 2 * width], w_long[1], right_turned)

    copy = away(lowered, 1)

    def stay_b(step):
        second_grad[rows_at(step * block, block)] = lowered(rows_at(mine + step * block, block))

    each(count, stay_b)
    copy.wait()
    load_cotangent.wait()

    def second_norm(step):
        rows = rows_at(step * block, block)
        full = rows_at(mine + step * block, block)
        values = normed[full].astype(jnp.float32) + ((second_grad[rows] + got[rows]) + vector(3))
        hat, scale = norm_rows(values)
        out_rows[rows] = (hat * vector(4) + vector(5)).astype(jnp.bfloat16)
        upstream = cotangent[rows].astype(jnp.float32)
        grad = norm_rows_back(upstream, hat, scale, vector(4))
        second_grad[rows] = grad
        second_low[full] = grad.astype(jnp.bfloat16)
        add_sum(3, grad)
        add_sum(4, upstream * hat)
        add_sum(5, upstream)

    each(count, second_norm)
    copy_s = swap_copy(second_low.at[rows_at(mine, half)], second_low.at[rows_at(mine, half)], sems, 4, True)
    copy_s.start()
    near_rows = output.at[rows_at(y * total + mine, half)]
    store_out = pltpu.make_async_copy(out_rows, near_rows, local.at[2])
    store_out.start()
    copy_o = swap_copy(out_rows, near_rows, sems, 5, True)
    copy_o.start()
    copy_p = swap_copy(out_rows, far_out, sems, 6, False)
    copy_p.start()

    def contract(base):
        def body(step):
            rows = rows_at(base + step * block, block)
            inputs = second_low[rows]
            for near in range(2):
                columns = slice(near * width, (near + 1) * width)
                grad = dot(inputs, w_long[near], plain) * slope[rows, columns].astype(jnp.float32)
                add_sum(8 + near, grad)
                slope[rows, columns] = grad.astype(jnp.bfloat16)

        each(count, body)

    contract(mine)
    copy_s.wait()
    contract(theirs)
    expanded_low = slope

    def weight_terms(left, right, target):
        def body(step):
            rows = rows_at(step * block, block)
            for near in range(2):
                target[near, rows] = dot(left[:, rows], right[:, near * width : (near + 1) * width], left_turned).astype(jnp.bfloat16)

        each(width // block, body)

    weight_terms(second_low, hidden, w_long)
    scatters = [
        Scatter(lines, terms, slots, scatter_recv.at[part], scatter_send.at[part], unit, corner)
        for part, (terms, slots, corner) in enumerate((
            (terms_first, slots_narrow.at[0], None), (terms_second, slots_narrow.at[1], None),
            (w_wide, slots_wide.at[0], "y"), (w_long, slots_wide.at[1], "x")))]
    first, second, wide, long = scatters
    long.begin()
    ready = portions(steps_of(merged((0, long.events(grad_down)[1:]), (1, wide.events(grad_up)[1:]))), 15)
    ready = [[]] * (15 - 15) + ready

    def normed_term(rows):
        return dot(expanded_low[rows, 0:width], w_wide[0], right_turned) + dot(expanded_low[rows, width : 2 * width], w_wide[1], right_turned)

    copy = away(normed_term, 2)

    def stay_c(step):
        rows = rows_at(step * block, block)
        second_grad[rows] = second_grad[rows] + normed_term(rows_at(mine + step * block, block))

    each(count, stay_c)

    copy.wait()

    def first_norm_back(step):
        rows = rows_at(step * block, block)
        full = rows_at(mine + step * block, block)
        upstream = second_grad[rows] + got[rows]
        hat = hat_one[rows]
        grad = norm_rows_back(upstream, hat, scale_one[rows][:, 0:1], vector(1))
        second_grad[rows] = grad
        first_low[full] = grad.astype(jnp.bfloat16)
        add_sum(0, grad)
        add_sum(1, upstream * hat)
        add_sum(2, upstream)

    each(count, first_norm_back)
    first_grad = second_grad
    copy_f = swap_copy(first_low.at[rows_at(mine, half)], first_low.at[rows_at(mine, half)], sems, 7, True)
    copy_f.start()
    weight_terms(normed, expanded_low, w_wide)
    wide.begin()
    copy_f.wait()

    def back_out(step):
        rows = rows_at(step * block, block)
        context_grad[rows] = dot(first_low[rows], turned[...], plain).astype(jnp.bfloat16)

    each(blocks, back_out)

    def out_terms(step):
        rows = rows_at(step * block, block)
        out_grad[rows] = dot(first_low[:, rows], context[...], left_turned)

    each(width // block, out_terms)

    lane = lax.broadcasted_iota(jnp.int32, (block, lanes), 1)
    for index in range(blocks):
        rows = slice(index * block, (index + 1) * block)
        stats = jnp.zeros((block, lanes), jnp.float32)
        for pair in range(3):
            product = context_grad[rows, tile(pair)].astype(jnp.float32) * context[rows, tile(pair)].astype(jnp.float32)
            lower = jnp.sum(jnp.where(low, product, 0.0), axis=-1, keepdims=True)
            upper = jnp.sum(jnp.where(low, 0.0, product), axis=-1, keepdims=True)
            stats = jnp.where(lane == 2 * pair, lower, jnp.where(lane == 2 * pair + 1, upper, stats))
        dot_rows[index] = stats.T[0:8]
        log_rows[index] = log_sum[rows].T[0:8]
    packed = hidden

    def columns_of(part, near):
        return slice((2 * near + part) * 3 * lanes, (2 * near + part + 1) * 3 * lanes)

    def back(pair, steps):
        back_pair(pair, query, key, value, context_grad, limit_rows, log_rows, dot_rows, query_acc, key_acc, value_acc, steps)

    query_sums, value_sums = [], []

    def place_pair(pair):
        def body(index, carry):
            rows = rows_at(index * block, block)
            asked = query_acc[rows] * 0.125
            valued = value_acc[rows]
            for which, values in enumerate((asked, key_acc[rows], valued)):
                if pair < 2:
                    packed[rows, pl.ds(2 * pair * 3 * lanes + which * lanes, lanes)] = values.astype(jnp.bfloat16)
                else:
                    packed[rows, pl.ds(3 * lanes + which * lanes, lanes)] = jnp.where(low, values, 0.0).astype(jnp.bfloat16)
                    packed[rows, pl.ds(9 * lanes + which * lanes, lanes)] = jnp.where(low, 0.0, values).astype(jnp.bfloat16)
            return carry[0] + total_rows(asked), carry[1] + total_rows(valued)

        empty = jnp.zeros((1, lanes), jnp.float32)
        asked_sum, valued_sum = lax.fori_loop(0, blocks, body, (empty, empty))
        query_sums.append(asked_sum)
        value_sums.append(valued_sum)

    def first_terms(near):
        def body(step):
            rows = rows_at(step * block, block)
            terms_first[near, rows] = dot(tokens[:, rows], packed[:, columns_of(0, near)], left_turned).astype(jnp.bfloat16)

        each(width // block, body)

    def second_terms(step):
        rows = rows_at(step * block, block)
        outs = [out_grad[rows, tile(pair)] for pair in range(3)]
        homes = (
            (swapped(outs[0]), outs[0], swapped(outs[2])),
            (outs[1], swapped(outs[1]), swapped(outs[2])),
        )
        for near in range(2):
            grads = dot(tokens[:, rows], packed[:, columns_of(1, near)], left_turned)
            for which in range(3):
                values, home = grads[:, tile(which)], homes[near][which]
                values = jnp.where(low, values, home) if near == 0 else jnp.where(low, home, values)
                terms_second[near, rows, tile(which)] = values.astype(jnp.bfloat16)

    run(ready[0])
    back(0, ready[1:5])
    place_pair(0)
    first_terms(0)
    run(ready[5])
    copy_p.wait()
    far_rows = output.at[rows_at((1 - y) * total + mine, half)]
    copy_q = swap_copy(far_out, far_rows, sems, 8, True)
    copy_q.start()
    store_far = pltpu.make_async_copy(far_out, far_rows, local.at[1])
    store_far.start()
    back(1, ready[6:10])
    place_pair(1)
    first_terms(1)
    first.begin()
    run(ready[10])
    back(2, ready[11:15])
    place_pair(2)
    each(width // block, second_terms)
    second.begin()
    tail = portions(steps_of(merged((0, first.events(grad_one)[1:]), (1, second.events(grad_two)[1:]))), 5)
    run(tail[0])
    narrow = width // 4

    def columns(near, which, rows):
        spot = rows_at((2 * near + which) * narrow, narrow)
        result = dot(packed[rows, columns_of(0, 0)], w_first[0, spot], right_turned)
        result = result + dot(packed[rows, columns_of(1, 0)], w_second[0, spot], right_turned)
        result = result + dot(packed[rows, columns_of(0, 1)], w_first[1, spot], right_turned)
        return result + dot(packed[rows, columns_of(1, 1)], w_second[1, spot], right_turned)

    def pick(values, near, which):
        pieces = [values[:, i * narrow : (i + 1) * narrow] for i in range(4)]
        found = [jnp.where(which == 0, pieces[2 * i], pieces[2 * i + 1]) for i in range(2)]
        return found[near] if isinstance(near, int) else jnp.where(near == 0, found[0], found[1])

    def kept(index, near, which):
        rows = rows_at(lax.rem(index, count) * block, block)
        return jnp.where(index // count == core, pick(first_grad[rows], near, which), 0.0)

    def across(index):
        rows = rows_at(index * block, block)
        for near in range(2):
            turn_sent[near, rows] = (columns(near, 1 - core, rows) + kept(index, near, 1 - core)).astype(jnp.bfloat16)

    each(blocks, across)
    copy_t = swap_copy(turn_sent, turn_got, sems, 9, True)
    copy_t.start()
    run(tail[1])
    copy_t.wait()

    def finish(near, index):
        rows = rows_at(index * block, block)
        return columns(near, core, rows) + turn_got[near, rows].astype(jnp.float32) + kept(index, near, core)

    def far(index):
        far_sent[:, rows_at(index * block, block)] = finish(1 - y, index).T.astype(jnp.bfloat16)

    each(blocks, far)
    copy_u = swap_copy(far_sent, input_far, sems, 10, False)
    copy_u.start()
    run(tail[2])

    nothing = jnp.zeros((1, lanes), jnp.float32)
    for near in range(2):
        sums[0, 6 + near : 7 + near] = jnp.concatenate(
            [query_sums[near], nothing, value_sums[near], query_sums[2], nothing, value_sums[2]], axis=1)

    def vector_step(step, target):
        copy = pltpu.make_async_remote_copy(
            src_ref=sums.at[step], dst_ref=vec_got.at[step], send_sem=sems.at[0, 11 + step], recv_sem=sems.at[1, 11 + step],
            device_id=target, device_id_type=MESH)
        copy.start()
        return copy

    copy = vector_step(0, device(z, x, y, 1 - core))

    def close(index):
        input_own[:, rows_at(index * block, block)] = finish(y, index).T

    each(blocks, close)
    copy.wait()
    shared = lax.broadcasted_iota(jnp.int32, vec_got.shape[1:], 0) < 6
    sums[1] = sums[0] + jnp.where(shared, vec_got[0], 0.0)
    copy = vector_step(1, device(z, 1 - x, y, core))
    run(tail[3])
    copy.wait()
    sums[2] = sums[1] + vec_got[1]
    copy = vector_step(2, device(z, x, 1 - y, core))
    copy.wait()
    line_got[z] = sums[2] + vec_got[2]

    def line_copy(there, arrives):
        return pltpu.make_async_remote_copy(
            src_ref=line_got.at[z], dst_ref=line_got.at[arrives], send_sem=sems.at[0, 16 + there], recv_sem=sems.at[1, 16 + arrives],
            device_id=device(there, x, y, core), device_id_type=MESH)

    others = [(there, ok) for k in range(1, lines) for there, ok in ((z + k, z + k < lines), (z - k, z - k >= 0))]
    for there, ok in others:
        pl.when(ok)(lambda: line_copy(there, z).start())
    run(tail[4])
    for there, ok in others:
        pl.when(ok)(lambda: line_copy(there, there).wait())
    result = line_got[0]
    for line in range(1, lines):
        result = result + line_got[line]
    own_sums[...] = result
    store_out.wait()
    store_far.wait()
    for copy in (copy_o, copy_q, copy_u):
        copy.wait()
    for scatter in scatters:
        scatter.drain()


def close_kernel(
    unit, output_in, input_own, input_far, grad_one, grad_two, grad_up, grad_down, own_sums,
    output, input_grad, g_query, g_key, g_value, g_out, g_up, g_down, gb_query, gb_value, gb_up, *rest,
):
    vector_grads, (staged, sem) = rest[:-2], rest[-2:]
    z, x, y, core = place()
    own = lax.axis_index("dp")
    total = input_own.shape[1]
    half = total // 2
    loads = [pltpu.make_async_copy(output_in.at[i * half : (i + 1) * half], staged.at[i], sem.at[i]) for i in range(4)]
    stores = [pltpu.make_async_copy(staged.at[i], output.at[i * half : (i + 1) * half], sem.at[4 + i]) for i in range(4)]
    for copy in loads:
        copy.start()
    input_grad[:, rows_at(y * total, total)] = input_own[...]
    input_grad[:, rows_at((1 - y) * total, total)] = input_far[...].astype(jnp.float32)

    for load, store in zip(loads, stores):
        load.wait()
        store.start()

    def third(values, which):
        start = which * 2 * HEAD
        return jnp.where(y == 0, values[:, start : start + HEAD], values[:, start + HEAD : start + 2 * HEAD])

    def free(values, which):
        start = which * 2 * HEAD
        return jnp.where(y == 0, values[:, start + HEAD : start + 2 * HEAD], values[:, start : start + HEAD])

    one, two = grad_one[...], grad_two[...]
    for which, target in enumerate((g_query, g_key, g_value)):
        target[:, 0 : 2 * HEAD] = one[:, tile(which)]
        target[:, 2 * HEAD : 3 * HEAD] = third(two, which)
    for which in range(3):
        g_out[which * HEAD : (which + 1) * HEAD] = free(two, which).T
    g_up[...] = grad_up[...]
    g_down[...] = grad_down[...]
    sums = own_sums[...]
    rows = jnp.where(y == 0, sums[6:7], sums[7:8])
    for which, target in ((0, gb_query), (2, gb_value)):
        target[:, 0 : 2 * HEAD] = rows[:, tile(which)]
        target[:, 2 * HEAD : 3 * HEAD] = third(rows[:, 3 * lanes :], which)
    gb_up[...] = jnp.where(y == 0, sums[8], sums[9])
    kept = jnp.zeros((8, unit), jnp.float32)
    for part in range(sums.shape[1] // unit):
        kept = jnp.where(own == part, sums[0:8, part * unit : (part + 1) * unit], kept)
    for index, target in enumerate(vector_grads):
        target[...] = kept[index : index + 1]
    for copy in stores:
        copy.wait()


def fits(mesh, tokens, seq_lens, block_sizes, w_query, *others):
    unit, columns = w_query.shape
    w_up = others[8]
    return (
        mesh.shape["tensor"] == 4
        and mesh.shape["dp"] % 4 == 0
        and seq_lens.shape[0] == 2
        and tokens.shape[0] % (4 * block) == 0
        and columns == 3 * HEAD
        and unit % 16 == 0
        and unit <= lanes
        and unit * mesh.shape["dp"] == tokens.shape[1] == 12 * HEAD == w_up.shape[1]
    )


def on_device_fast(lines, tokens, seq_lens, block_sizes, w_query, b_query, w_key, w_value, b_value, w_out, b_out,
                   gain_one, shift_one, w_up, b_up, w_down, b_down, gain_two, shift_two, cotangent):
    bf16, f32 = jnp.bfloat16, jnp.float32
    total, width = tokens.shape[0] // 2, tokens.shape[1]
    half, pairs = total // 2, width // 2
    unit = w_query.shape[0]
    slots = lines * 4
    blocks = total // block
    dma = pltpu.SemaphoreType.DMA
    shape = jax.ShapeDtypeStruct
    anywhere, on_chip = pl.BlockSpec(memory_space=pl.ANY), pl.BlockSpec(memory_space=pltpu.VMEM)
    scalars = pl.BlockSpec(memory_space=pltpu.SMEM)
    pair, single = slice(0, 2 * HEAD), slice(2 * HEAD, 3 * HEAD)
    zero, zeros = jnp.zeros((HEAD,), bf16), jnp.zeros((2 * HEAD,), bf16)
    near = jnp.concatenate([b_query[pair], zeros, b_value[pair], b_query[single], zero, zeros, b_value[single], zero])
    far = jnp.concatenate([b_query[pair], zeros, b_value[pair], zero, b_query[single], zeros, zero, b_value[single]])
    vectors = jnp.stack([b_out, gain_one, shift_one, b_down, gain_two, shift_two])
    extra = jnp.concatenate([
        jnp.where(lax.axis_index("tensor") // 2 == 0, near, far)[None], b_up[None],
        jnp.pad(vectors, ((0, 0), (0, width - unit))), jnp.zeros((8, width), bf16)])
    raw = pl.pallas_call(
        functools.partial(layer_kernel, lines),
        out_shape=(
            shape((2 * total, width), bf16), shape((width // 4, total), f32), shape((width // 4, total), bf16),
            shape((unit, pairs), f32), shape((unit, pairs), f32), shape((unit, width), f32), shape((unit, width), f32),
            shape((16, width), f32)),
        in_specs=[anywhere] * 2 + [scalars] * 2 + [on_chip] * 7,
        out_specs=(anywhere,) + (on_chip,) * 7,
        scratch_shapes=[
            pltpu.VMEM((total, width), bf16), pltpu.VMEM((half, width), bf16),
            pltpu.VMEM((2, width, pairs), bf16), pltpu.VMEM((2, width, pairs), bf16),
            pltpu.VMEM((2, width, width), bf16), pltpu.VMEM((2, width, width), bf16),
            pltpu.VMEM((2, lines * 2 * 16, width), bf16), pltpu.VMEM((16, width), f32),
            *[pltpu.VMEM((total, pairs), bf16)] * 4, pltpu.VMEM((total, lanes), f32),
            pltpu.VMEM((total, 1), jnp.int32), pltpu.VMEM((blocks, 8, block), jnp.int32),
            *[pltpu.VMEM((blocks, 8, block), f32)] * 2,
            pltpu.VMEM((width, pairs), bf16), *[pltpu.VMEM((half, width), f32)] * 3, pltpu.VMEM((half, lanes), f32),
            pltpu.VMEM((total, width), bf16), *[pltpu.VMEM((total, 2 * width), bf16)] * 2,
            pltpu.VMEM((half, width), f32), *[pltpu.VMEM((total, width), bf16)] * 2,
            pltpu.VMEM((total, pairs), bf16), pltpu.VMEM((width, pairs), f32), *[pltpu.VMEM((half, width), bf16)] * 2,
            *[pltpu.VMEM((total, lanes), f32)] * 3, *[pltpu.VMEM((2, width, pairs), bf16)] * 2,
            pltpu.VMEM((2, 5, lines, unit, pairs), bf16), pltpu.VMEM((2, 7, lines, unit, width), bf16),
            *[pltpu.VMEM((3, 16, width), f32)] * 2, pltpu.VMEM((lines, 16, width), f32),
            *[pltpu.VMEM((2, total, width // 4), bf16)] * 2, pltpu.VMEM((width // 4, total), bf16),
            dma((3,)), dma((4, slots)), dma((4, 4, slots)), dma((slots,)), dma((4, slots)),
            dma((4, 7, lines)), dma((4, 7, lines)), dma((2, 16 + lines))],
        compiler_params=pltpu.CompilerParams(collective_id=0, has_side_effects=True, vmem_limit_bytes=62 * 2**20),
    )(tokens, cotangent, seq_lens, block_sizes, w_query, w_key, w_value, w_out, w_up, w_down.T, extra)

    small = [3 * HEAD, 3 * HEAD, width] + [unit] * 6
    done = pl.pallas_call(
        functools.partial(close_kernel, unit),
        out_shape=(
            shape((2 * total, width), bf16), shape((width // 4, 2 * total), f32),
            *[shape((unit, 3 * HEAD), f32)] * 3, shape((3 * HEAD, unit), f32), shape((unit, width), f32), shape((unit, width), f32),
            *[shape((1, size), f32) if size != width else shape((size,), f32) for size in small]),
        in_specs=[anywhere] + [on_chip] * 7,
        out_specs=(anywhere,) + (on_chip,) * 16,
        scratch_shapes=[pltpu.VMEM((4, half, width), bf16), dma((8,))],
        compiler_params=pltpu.CompilerParams(vmem_limit_bytes=62 * 2**20),
    )(*raw)
    output, input_grad, g_query, g_key, g_value, g_out, g_up, g_down = done[:8]
    gb_query, gb_value, gb_up, gb_out, g_gain_one, g_shift_one, gb_down, g_gain_two, g_shift_two = [array.reshape(-1) for array in done[8:]]
    return (output, input_grad.T, g_query, gb_query, g_key, g_value, gb_value, g_out, gb_out, g_gain_one, g_shift_one,
            g_up, gb_up, g_down.T, gb_down, g_gain_two, g_shift_two)


def solution(mesh):
    in_specs = (
        P("dp", None),
        P("dp"),
        P("dp"),
        P("dp", "tensor"),
        P("tensor"),
        P("dp", "tensor"),
        P("dp", "tensor"),
        P("tensor"),
        P("tensor", "dp"),
        P("dp"),
        P("dp"),
        P("dp"),
        P("dp", "tensor"),
        P("tensor"),
        P("tensor", "dp"),
        P("dp"),
        P("dp"),
        P("dp"),
        P("dp", None),
    )
    out_specs = (
        P("dp", None),
        P("dp", "tensor"),
        P("dp", "tensor"),
        P("tensor"),
        P("dp", "tensor"),
        P("dp", "tensor"),
        P("tensor"),
        P("tensor", "dp"),
        P("dp"),
        P("dp"),
        P("dp"),
        P("dp", "tensor"),
        P("tensor"),
        P("tensor", "dp"),
        P("dp"),
        P("dp"),
        P("dp"),
    )
    lines = mesh.shape["dp"] // 2

    def on_device(*arrays):
        if fits(mesh, *arrays):
            return on_device_fast(lines, *arrays)
        return on_device_plain(*arrays)

    return jax.shard_map(
        on_device, mesh=mesh, in_specs=in_specs, out_specs=out_specs, check_vma=False
    )
```
